128 devices in a mesh: tab: 32 (over x, y, core), rep: 4 (over z).
Axes of the slice: x: 4, y: 4, z: 4, core: 2. Of those that a mesh axis runs over, the one named last changes fastest.
Arguments:
- pooled: bfloat16 [64, 16384, 128], P('tab', 'rep'), may hold values from -6 to 6
- widths: int32 [64], replicated, may hold values from 16 to 128, as said below
- placement: int32 [64], replicated, may hold values from 0 to 63, each once
- route: int32 [4, 4096], P('rep'), may hold values from 0 to 4095, each once within a row
- labels: int32 [4, 4096], P('rep'), may hold values 0 or 1
- proj: bfloat16 [64, 128, 32], replicated, may hold values from -0.5 to 0.5
- senet_in: float32 [64, 32], replicated, may hold values from -6 to 6
- senet_out: float32 [32, 64], replicated, may hold values from -1 to 1
- bilinear: float32 [32, 32], replicated, may hold values from -1 to 1
- w_first: bfloat16 [4096, 256], replicated, may hold values from -0.09375 to 0.09375
- w_second: bfloat16 [256, 256], replicated, may hold values from -0.75 to 0.75
- w_last: bfloat16 [256], replicated, may hold values from -0.375 to 0.375
Outputs:
- scores: float32 [4, 4096], P('rep', 'tab')
- d_pooled: bfloat16 [64, 16384, 128], P('tab', 'rep')
- d_proj: float32 [64, 128, 32], P('tab')
- d_senet_in: float32 [64, 32], replicated
- d_senet_out: float32 [32, 64], replicated
- d_bilinear: float32 [32, 32], replicated
- d_first: float32 [4096, 256], P('tab')
- d_second: float32 [256, 256], replicated
- d_last: float32 [256], replicated
The draws below stay inside these ranges and needn't reach their ends.
Inputs may be any that keep to these rules, and one draw needn't show every extreme that they name: `widths`: each field's width is 128, 64, 32 or 16. `placement`: a permutation of the fields. `route`: each row is a permutation of 0 to 4095.
All inputs are finite; a program needn't handle non-finite values. No bound on the sum of `labels` on one device may be relied on, other than what follows from the above.
Results may differ from the reference program's by a relative error of at most 0.017.
Values may be sent and summed in bfloat16 or wider, within the bound.
A program may use at most 64 MiB of HBM per device.

```python
import jax
import jax.numpy as jnp
from jax import lax

F = 64
WMAX = 128
E = 32
R = 32
H = 256
B_DEV = 128
B_REP = 4096
BATCH = 16384
N_REP = 4


second_bound = 0.75


def draw_widths(key, part):
    levels = jax.random.randint(key, (F,), 0, 4)
    result = jnp.right_shift(jnp.full((F,), WMAX, jnp.int32), levels.astype(jnp.int32))
    chosen = jax.random.randint(jax.random.fold_in(key, 7), (), 0, F)
    return result.at[chosen].set(WMAX).astype(jnp.int32)


def draw_w_second(key, part):
    base = jax.random.uniform(jax.random.fold_in(key, 11), (H, H), jnp.float32, -second_bound, second_bound)
    result = base
    return result.astype(jnp.bfloat16)


def touch_ends(array, own_key, least, largest):
    extent = array.shape
    spot = [jax.random.randint(jax.random.fold_in(own_key, axis), (), 0, extent[axis]) for axis in range(len(extent))]
    array = array.at[tuple(spot)].set(least)
    longest = extent.index(max(extent))
    spot[longest] = (spot[longest] + 1) % extent[longest]
    return array.at[tuple(spot)].set(largest)


def shard_levels(rng, extent, shards, low, high):
    def one(position, blocks):
        draws = jax.random.uniform(jax.random.fold_in(jax.random.fold_in(rng, 6), position), (blocks,), jnp.float32, low / len(shards), high / len(shards))
        return jnp.repeat(jnp.exp(draws), extent[position] // blocks).reshape((-1,) + (1,) * (len(extent) - position - 1))

    gain = one(*shards[0])
    for cut in shards[1:]:
        gain = gain * one(*cut)
    return gain


def gaussian(key, extent, scale, bound, cuts=(), kind=jnp.bfloat16):
    factor_of = shard_levels(key, extent, cuts, -0.22, 0.18) if cuts else 1.0
    array = jax.random.normal(key, extent, jnp.float32) * scale * factor_of
    return jnp.minimum(jnp.maximum(array, -bound), bound).astype(kind)


def setup_inputs(seed: int = 0) -> dict:
    key_list = jax.random.split(jax.random.key(seed), 13)
    pooled = gaussian(key_list[0], (F, BATCH, WMAX), 1.0, 6.0, ((0, 32), (1, 4)))
    widths = draw_widths(jax.random.fold_in(key_list[12], 71), 0)
    placement = jax.random.permutation(key_list[2], F).astype(jnp.int32)
    route = jax.vmap(lambda own: jax.random.permutation(own, B_REP))(jax.random.split(key_list[3], N_REP)).reshape((N_REP, B_REP)).astype(jnp.int32)
    labels = touch_ends((jax.random.randint(key_list[4], (N_REP, B_REP), 0, 4) < 1).astype(jnp.int32), jax.random.fold_in(key_list[4], 1), 0, 1)
    proj = gaussian(key_list[5], (F, WMAX, E), WMAX ** -0.5, 0.5)
    senet_in = gaussian(key_list[6], (F, R), 1.0, 6.0, (), jnp.float32)
    senet_out = gaussian(key_list[7], (R, F), R ** -0.5, 1.0, (), jnp.float32)
    bilinear = gaussian(key_list[8], (E, E), E ** -0.5, 1.0, (), jnp.float32)
    w_first = gaussian(key_list[9], (2 * F * E, H), (2 * F * E) ** -0.5, 0.09375)
    w_second = draw_w_second(jax.random.fold_in(key_list[12], 71), 0)
    w_last = gaussian(key_list[11], (H,), H ** -0.5, 0.375)
    return {"pooled": pooled, "widths": widths, "placement": placement, "route": route, "labels": labels, "proj": proj, "senet_in": senet_in, "senet_out": senet_out, "bilinear": bilinear, "w_first": w_first, "w_second": w_second, "w_last": w_last}


PRECISE = lax.Precision.HIGHEST


def silu_slope(pre_act):
    logistic = jax.nn.sigmoid(pre_act)
    return logistic * (1.0 + pre_act * (1.0 - logistic))


def bilinear_forward(fields_in, bilinear, factor):
    product = jnp.einsum("fnc,cd->fnd", fields_in, bilinear, precision=PRECISE)
    others = jnp.sum(fields_in, axis=0, keepdims=True) - fields_in
    return product * others * factor, product, others


def bilinear_backward(fields_in, product, others, upstream, bilinear, factor):
    d_product = upstream * others * factor
    d_others = upstream * product * factor
    d_fields = jnp.einsum("fnd,cd->fnc", d_product, bilinear, precision=PRECISE)
    d_fields = d_fields + jnp.sum(d_others, axis=0, keepdims=True) - d_others
    d_weight = jnp.einsum("fnc,fnd->cd", fields_in, d_product, precision=PRECISE)
    return d_fields, d_weight


def owner_pass(embeds, targets, senet_in, senet_out, bilinear, w_first, w_second, w_last):
    count = embeds.shape[0]
    width = embeds.shape[2]
    hidden = w_second.shape[0]
    factor = count ** -0.5
    first = w_first.reshape(2, count, width, hidden).astype(jnp.float32)
    dense = embeds.astype(jnp.float32)
    squeeze = jnp.mean(dense, axis=2)
    pre_one = jnp.einsum("fn,fr->rn", squeeze, senet_in, precision=PRECISE)
    act_one = jax.nn.silu(pre_one)
    pre_two = jnp.einsum("rn,rf->fn", act_one, senet_out, precision=PRECISE)
    weights = jax.nn.sigmoid(pre_two)
    scaled = weights[:, :, None] * dense
    plain_out, plain_prod, plain_rest = bilinear_forward(dense, bilinear, factor)
    scaled_out, scaled_prod, scaled_rest = bilinear_forward(scaled, bilinear, factor)
    joined = jnp.stack([plain_out, scaled_out]).astype(jnp.bfloat16)
    joined_wide = joined.astype(jnp.float32)
    pre_hidden = jnp.einsum("kfnc,kfch->nh", joined_wide, first, precision=PRECISE)
    hidden_one = jax.nn.silu(pre_hidden).astype(jnp.bfloat16)
    pre_second = jnp.dot(hidden_one, w_second, preferred_element_type=jnp.float32)
    hidden_two = jax.nn.silu(pre_second).astype(jnp.bfloat16)
    logits = jnp.dot(hidden_two, w_last, preferred_element_type=jnp.float32)
    grad_logit = jax.nn.sigmoid(logits) - targets
    d_last = jnp.dot(grad_logit, hidden_two.astype(jnp.float32), precision=PRECISE)
    last_wide = w_last.astype(jnp.float32)
    d_pre_two = (grad_logit[:, None] * last_wide[None, :] * silu_slope(pre_second)).astype(jnp.bfloat16)
    d_second = jnp.dot(hidden_one.T, d_pre_two, preferred_element_type=jnp.float32)
    back_two = jnp.dot(d_pre_two, w_second.T, preferred_element_type=jnp.float32)
    d_pre_one = (back_two * silu_slope(pre_hidden)).astype(jnp.bfloat16)
    d_pre_wide = d_pre_one.astype(jnp.float32)
    d_first = jnp.einsum("kfnc,nh->kfch", joined_wide, d_pre_wide, precision=PRECISE).reshape(-1, hidden)
    d_joined = jnp.einsum("nh,kfch->kfnc", d_pre_wide, first, precision=PRECISE)
    d_plain, d_bil_plain = bilinear_backward(dense, plain_prod, plain_rest, d_joined[0], bilinear, factor)
    d_scaled, d_bil_scaled = bilinear_backward(scaled, scaled_prod, scaled_rest, d_joined[1], bilinear, factor)
    d_weights = jnp.sum(d_scaled * dense, axis=2)
    d_pre_w = d_weights * weights * (1.0 - weights)
    d_senet_out = jnp.einsum("rn,fn->rf", act_one, d_pre_w, precision=PRECISE)
    d_act = jnp.einsum("fn,rf->rn", d_pre_w, senet_out, precision=PRECISE) * silu_slope(pre_one)
    d_senet_in = jnp.einsum("fn,rn->fr", squeeze, d_act, precision=PRECISE)
    d_squeeze = jnp.einsum("rn,fr->fn", d_act, senet_in, precision=PRECISE)
    d_embeds = d_plain + weights[:, :, None] * d_scaled + d_squeeze[:, :, None] / width
    small = (d_senet_in, d_senet_out, d_bil_plain + d_bil_scaled, d_second, d_last)
    return logits, d_embeds.astype(jnp.bfloat16), small, d_first


def reference(pooled, widths, placement, route, labels, proj, senet_in, senet_out, bilinear, w_first, w_second, w_last):
    total = pooled.shape[1]
    padded = pooled.shape[2]
    field_count = placement.shape[0]
    ids = jnp.arange(field_count, dtype=jnp.int32)
    slot_width = widths[placement]
    slot_mask = (jnp.arange(padded, dtype=jnp.int32)[None, :] < slot_width[:, None]).astype(pooled.dtype)
    slot_proj = proj[placement].astype(jnp.float32)
    inverse = jnp.zeros_like(placement).at[placement].set(ids)
    flat_labels = labels.reshape(-1).astype(jnp.float32)
    block = B_DEV * N_REP
    turns = total // block
    hidden = w_second.shape[0]
    width = proj.shape[2]
    senet_rows = senet_in.shape[1]

    def one_block(index, carry):
        grads_pooled, logits_all, sums, first_sum = carry
        start = (index * block).astype(jnp.int32)
        rows = lax.dynamic_slice_in_dim(pooled, start, block, 1)
        masked = rows * slot_mask[:, None, :]
        embed_slot = jnp.einsum("fnc,fcd->fnd", masked.astype(jnp.float32), slot_proj, precision=PRECISE).astype(jnp.bfloat16)
        embed_field = embed_slot[inverse]
        targets = lax.dynamic_slice_in_dim(flat_labels, start, block)
        logits, d_embeds, small, d_first = owner_pass(embed_field, targets, senet_in, senet_out, bilinear, w_first, w_second, w_last)
        d_slot = d_embeds[placement].astype(jnp.float32)
        back = jnp.einsum("fnd,fcd->fnc", d_slot, slot_proj, precision=PRECISE)
        back = (back * slot_mask[:, None, :].astype(jnp.float32)).astype(pooled.dtype)
        d_proj_part = jnp.einsum("fnc,fnd->fcd", masked.astype(jnp.float32), d_slot, precision=PRECISE)
        grads_pooled = lax.dynamic_update_slice_in_dim(grads_pooled, back, start, 1)
        logits_all = lax.dynamic_update_slice_in_dim(logits_all, logits, start, 0)
        parts = (d_proj_part,) + small
        sums = tuple(old + new for old, new in zip(sums, parts))
        return grads_pooled, logits_all, sums, first_sum + d_first

    start_sums = (
        jnp.zeros((field_count, padded, width), jnp.float32),
        jnp.zeros((field_count, senet_rows), jnp.float32),
        jnp.zeros((senet_rows, field_count), jnp.float32),
        jnp.zeros((width, width), jnp.float32),
        jnp.zeros((hidden, hidden), jnp.float32),
        jnp.zeros((hidden,), jnp.float32),
    )
    start = (jnp.zeros_like(pooled), jnp.zeros((total,), jnp.float32), start_sums, jnp.zeros(w_first.shape, jnp.float32))
    grads_pooled, logits_all, sums, first_sum = lax.fori_loop(0, turns, one_block, start)
    scores = jnp.take_along_axis(logits_all.reshape(N_REP, B_REP), route, axis=1)
    d_proj, d_senet_in, d_senet_out, d_bilinear, d_second, d_last = sums
    return scores, grads_pooled, d_proj, d_senet_in, d_senet_out, d_bilinear, first_sum, d_second, d_last
```

```python
import functools

import jax
import jax.numpy as jnp
from jax import lax
from jax.experimental import pallas as pl
from jax.experimental.pallas import tpu as pltpu
from jax.sharding import PartitionSpec as P

F32 = jnp.float32
BF = jnp.bfloat16
HI = lax.Precision.HIGHEST
NN = (((1,), (0,)), ((), ()))
NT = (((1,), (1,)), ((), ()))
TN = (((0,), (0,)), ((), ()))

FIELDS = 64
E = 32
TAB = 32
REP = 4
SIDE = 4
LANES = 128
HID = 256
BLOCK = 272
SMALL = 144
FACTOR = 0.125


def mm(a, b, dims, precision=None):
    return lax.dot_general(a, b, dims, precision=precision, preferred_element_type=F32)


def slope(u):
    s = jax.nn.sigmoid(u)
    return s * (1.0 + u * (1.0 - s))


def iota(shape, dim):
    return lax.broadcasted_iota(jnp.int32, shape, dim)


def project_kernel(tab_ref, place_ref, width_ref, pooled_ref, proj_ref, e_ref, pt_ref, mask_ref, inv_ref):
    i = pl.program_id(0)
    j = pl.program_id(1)
    field = place_ref[2 * tab_ref[0] + i]
    width = width_ref[field]

    @pl.when((i == 0) & (j == 0))
    def _():
        def put(s, _):
            inv_ref[place_ref[s]] = s
            return 0

        lax.fori_loop(0, FIELDS, put, 0)

    eye = (iota((E, E), 0) == iota((E, E), 1)).astype(BF)
    keep = iota((E, LANES), 1) < width
    turned = jnp.where(keep, mm(eye, proj_ref[0], NT), 0.0).astype(BF)
    pt_ref[...] = turned
    mask_ref[...] = keep.astype(F32)
    out = mm(turned, pooled_ref[0], NT).astype(BF)
    for d in range(out.shape[1] // LANES):
        e_ref[d, 0] = out[:, d * LANES : (d + 1) * LANES]


def project(tab, placement, widths, pooled, proj):
    rows = pooled.shape[1]
    steps = 2
    chunk = rows // steps
    grid_spec = pltpu.PrefetchScalarGridSpec(
        num_scalar_prefetch=3,
        grid=(2, steps),
        in_specs=[
            pl.BlockSpec((1, chunk, LANES), lambda i, j, t, p, w: (i, j, 0)),
            pl.BlockSpec((1, LANES, E), lambda i, j, t, p, w: (p[2 * t[0] + i], 0, 0)),
        ],
        out_specs=[
            pl.BlockSpec((chunk // LANES, 1, E, LANES), lambda i, j, t, p, w: (j, i, 0, 0)),
            pl.BlockSpec((E, LANES), lambda i, j, t, p, w: (i, 0)),
            pl.BlockSpec((E, LANES), lambda i, j, t, p, w: (i, 0)),
            pl.BlockSpec(memory_space=pltpu.SMEM),
        ],
    )
    return pl.pallas_call(
        project_kernel,
        grid_spec=grid_spec,
        out_shape=[
            jax.ShapeDtypeStruct((TAB, 2, E, LANES), BF),
            jax.ShapeDtypeStruct((2 * E, LANES), BF),
            jax.ShapeDtypeStruct((2 * E, LANES), F32),
            jax.ShapeDtypeStruct((FIELDS,), jnp.int32),
        ],
        compiler_params=pltpu.CompilerParams(vmem_limit_bytes=16 << 20),
        name="project",
    )(tab, placement, widths, pooled, proj)


def send(src, dst, ssem, rsem, dev):
    pltpu.make_async_remote_copy(
        src_ref=src, dst_ref=dst, send_sem=ssem, recv_sem=rsem, device_id=dev,
        device_id_type=pl.DeviceIdType.MESH,
    ).start()


def got(dst, ssem, rsem, dev):
    pltpu.make_async_remote_copy(
        src_ref=dst, dst_ref=dst, send_sem=ssem, recv_sem=rsem, device_id=dev,
        device_id_type=pl.DeviceIdType.MESH,
    ).wait_recv()


def sent(src, ssem, rsem, dev):
    pltpu.make_async_remote_copy(
        src_ref=src, dst_ref=src, send_sem=ssem, recv_sem=rsem, device_id=dev,
        device_id_type=pl.DeviceIdType.MESH,
    ).wait_send()


def main_kernel(
    inv_ref, place_ref, e_ref, labels_ref, sin_ref, sout_ref, bil_ref, w2_ref, wl_ref, w1_hbm, pooled_hbm,
    rd_ref, lg_ref, df_ref, ag_ref, smf_ref, dpt_ref,
    w1, xs, recv, emb, prod, du, sq, wts, dpw, dsq, js, jp, dpb, d2, d2p, dbil, demb, dslot, dfb, r1, r2, rz, sr, dz,
    load_sem, es, er, ds, dr, ls, lr, gs, gr, ps, pr, s1, q1, s2, q2, sz, qz, ss, sq_r, sd, qd,
):
    t = lax.axis_index("tab")
    r = lax.axis_index("rep")
    c = lax.rem(t, 2)
    n = t // 2
    x = n // SIDE
    y = lax.rem(n, SIDE)
    a = x + c * (y - x)
    b = y + c * (x - y)

    def at(a_, b_):
        return ((a_ + c * (b_ - a_)) * SIDE + (b_ + c * (a_ - b_))) * 2 + c

    def block_of(tab):
        c_ = lax.rem(tab, 2)
        n_ = tab // 2
        x_ = n_ // SIDE
        y_ = lax.rem(n_, SIDE)
        return 16 * c_ + SIDE * (x_ + c_ * (y_ - x_)) + y_ + c_ * (x_ - y_)

    mate = {"tab": t + 1 - 2 * c}
    barrier = pltpu.get_barrier_semaphore()

    def hello(i, _):
        pl.semaphore_signal(barrier, inc=1, device_id={"tab": lax.rem(t + i, TAB)}, device_id_type=pl.DeviceIdType.MESH)
        return 0

    lax.fori_loop(1, TAB, hello, 0)
    for d in range(1, REP):
        pl.semaphore_signal(barrier, inc=1, device_id={"rep": lax.rem(r + d, REP)}, device_id_type=pl.DeviceIdType.MESH)

    load_w1 = pltpu.make_async_copy(w1_hbm, w1, load_sem.at[0])
    load_x = pltpu.make_async_copy(pooled_hbm, xs, load_sem.at[1])
    load_w1.start()
    load_x.start()

    small_rows = (lax.rem(iota((HID, E), 0), E) == iota((HID, E), 1)).astype(BF)
    small_cols = (lax.rem(iota((E, HID), 1), E) == iota((E, HID), 0)).astype(BF)
    diag = (iota((HID, HID), 0) // E) == (iota((HID, HID), 1) // E)
    bil = bil_ref[...].astype(BF)
    tall = mm(small_rows, bil, NN).astype(BF)
    tall_t = mm(small_rows, bil, NT).astype(BF)
    kron = jnp.where(diag, mm(tall, small_cols, NN), 0.0).astype(BF)
    kron_t = jnp.where(diag, mm(tall_t, small_cols, NN), 0.0).astype(BF)
    square = iota((LANES, LANES), 0) == iota((LANES, LANES), 1)
    label_row = labels_ref[:, pl.ds(pl.multiple_of(t * LANES, LANES), LANES)].astype(F32)
    target = jnp.sum(jnp.where(square, label_row, 0.0), axis=1, keepdims=True)

    pl.semaphore_wait(barrier, TAB - 1 + REP - 1)

    def pair(p):
        return pl.ds(p * 2, 2)

    def e_send(i, _):
        p = lax.rem(t + i, TAB)
        send(e_ref.at[p], recv.at[pair(t)], es.at[p], er.at[t], {"tab": p})
        return 0

    lax.fori_loop(1, TAB, e_send, 0)
    recv[pair(t)] = e_ref[t]

    def e_wait(i, _):
        p = lax.rem(t + i, TAB)
        got(recv.at[pair(p)], es.at[p], er.at[p], {"tab": p})
        return 0

    lax.fori_loop(1, TAB, e_wait, 0)

    def rows32(f):
        return pl.ds(pl.multiple_of(f * E, E), E)

    def by_field(f, _):
        emb[rows32(f), :] = recv[inv_ref[f]]
        return 0

    lax.fori_loop(0, FIELDS, by_field, 0)

    groups = FIELDS // 8

    def rows256(g):
        return pl.ds(pl.multiple_of(g * HID, HID), HID)

    def rows8(g):
        return pl.ds(pl.multiple_of(g * 8, 8), 8)

    def cube(v):
        return v.reshape(8, E, LANES)

    def flat(v):
        return v.reshape(HID, LANES)

    def first_pass(g, total):
        u = cube(emb[rows256(g), :].astype(F32))
        sq[rows8(g), :] = jnp.sum(u, axis=1) * (1.0 / E)
        return total + jnp.sum(u, axis=0)

    zero = jnp.zeros((E, LANES), F32)
    total = lax.fori_loop(0, groups, first_pass, zero)
    squeeze = sq[...]
    pre_one = mm(sin_ref[...], squeeze, TN, HI)
    act_one = pre_one * jax.nn.sigmoid(pre_one)
    weights = jax.nn.sigmoid(mm(sout_ref[...], act_one, TN, HI))
    wts[...] = weights

    def scaled_of(g):
        u = cube(emb[rows256(g), :].astype(F32))
        return u, u * wts[rows8(g), :][:, None, :]

    def second_pass(g, tot):
        return tot + jnp.sum(scaled_of(g)[1], axis=0)

    total_s = lax.fori_loop(0, groups, second_pass, zero)

    load_w1.wait()

    def third_pass(g, acc):
        u, sc = scaled_of(g)
        for k, (v, vb, tot) in enumerate(((u, emb[rows256(g), :], total), (sc, flat(sc).astype(BF), total_s))):
            p = mm(kron_t, vb, NN)
            prod[k, rows256(g), :] = p
            j = flat(cube(p) * (tot[None] - v) * FACTOR).astype(BF)
            chip = k * groups + g
            js[chip] = j[:LANES]
            js[16 + lax.rem(chip, SIDE) * SIDE + chip // SIDE] = j[LANES:]
            acc = acc + mm(j, w1[rows256(k * groups + g), :], TN)
        return acc

    pre_hidden = lax.fori_loop(0, groups, third_pass, jnp.zeros((LANES, HID), F32))
    half = pl.ds((1 - c) * 16, 16)
    send(js.at[half], jp, ps.at[0], pr.at[0], mate)

    h1 = (pre_hidden * jax.nn.sigmoid(pre_hidden)).astype(BF)
    pre_second = mm(h1, w2_ref[...], NN)
    h2 = (pre_second * jax.nn.sigmoid(pre_second)).astype(BF).astype(F32)
    wl = wl_ref[...].astype(F32)
    logit = jnp.sum(h2 * wl, axis=1, keepdims=True)
    lg_ref[t] = jnp.sum(jnp.where(square, logit, 0.0), axis=0, keepdims=True)

    def l_send(i, _):
        p = lax.rem(t + i, TAB)
        send(lg_ref.at[t], lg_ref.at[t], ls.at[p], lr.at[t], {"tab": p})
        return 0

    lax.fori_loop(1, TAB, l_send, 0)
    grad = jax.nn.sigmoid(logit) - target
    d_last = jnp.sum(grad * h2, axis=0, keepdims=True)
    dp2 = (grad * wl * slope(pre_second)).astype(BF)
    d_second = mm(h1, dp2, TN).astype(BF)
    for i in range(16):
        for h in range(2):
            d2[2 * i + h] = d_second[16 * i : 16 * i + 16, LANES * h : LANES * h + LANES]
    dp1 = (mm(dp2, w2_ref[...], NT) * slope(pre_hidden)).astype(BF)
    dpb[0] = dp1
    send(dpb.at[0], dpb.at[1], ps.at[1], pr.at[1], mate)
    send(d2.at[half], d2p, ps.at[2], pr.at[2], mate)

    dbil[...] = jnp.zeros_like(dbil)

    def fourth_pass(g, sums):
        u, sc = scaled_of(g)
        out = []
        for k, (v, vb, tot) in enumerate(((u, emb[rows256(g), :], total), (sc, flat(sc).astype(BF), total_s))):
            up = cube(mm(w1[rows256(k * groups + g), :], dp1, NT)) * FACTOR
            dq = up * cube(prod[k, rows256(g), :])
            dp = flat(up * (tot[None] - v)).astype(BF)
            du[k, rows256(g), :] = mm(kron, dp, NN) - flat(dq)
            dbil[...] += mm(vb, dp, NT)
            out.append(sums[k] + jnp.sum(dq, axis=0))
        return tuple(out)

    sum_q, sum_qs = lax.fori_loop(0, groups, fourth_pass, (zero, zero))

    got(jp, ps.at[0], pr.at[0], mate)
    got(dpb.at[1], ps.at[1], pr.at[1], mate)
    got(d2p, ps.at[2], pr.at[2], mate)
    both = dpb[...].reshape(2 * LANES, HID)

    def d_first_row(i):
        def one(k, _):
            q = i * SIDE + k
            left = jnp.concatenate([js[16 * c + q], jp[q]], axis=1)
            out = mm(left, both, NN).astype(BF)
            dfb[i, k, 0:LANES] = out[:, :LANES]
            dfb[i, k, LANES : 2 * LANES] = out[:, LANES:]
            dfb[i, k, 2 * LANES : BLOCK] = (d2[16 * c + q].astype(F32) + d2p[q].astype(F32)).astype(BF)
            return 0

        lax.fori_loop(0, SIDE, one, 0)

    for d in range(1, SIDE):
        i = lax.rem(a + d, SIDE)
        d_first_row(i)
        send(dfb.at[i], r1.at[a], s1.at[d], q1.at[a], {"tab": at(i, b)})
    d_first_row(a)

    def fifth_pass(g, _):
        u = cube(emb[rows256(g), :].astype(F32))
        w = wts[rows8(g), :]
        d_w = jnp.sum((cube(du[1, rows256(g), :]) + sum_qs[None]) * u, axis=1)
        dpw[rows8(g), :] = d_w * w * (1.0 - w)
        return 0

    lax.fori_loop(0, groups, fifth_pass, 0)
    d_pre_w = dpw[...]
    d_act = mm(sout_ref[...], d_pre_w, NN, HI) * slope(pre_one)
    dsq[...] = mm(sin_ref[...], d_act, NN, HI) * (1.0 / E)

    def sixth_pass(g, _):
        w = wts[rows8(g), :][:, None, :]
        out = cube(du[0, rows256(g), :]) + sum_q[None] + w * (cube(du[1, rows256(g), :]) + sum_qs[None])
        out = out + dsq[rows8(g), :][:, None, :]
        demb[rows8(g)] = out.astype(BF)
        return 0

    lax.fori_loop(0, groups, sixth_pass, 0)

    def by_slot(s, _):
        dslot[s] = demb[place_ref[s]]
        return 0

    lax.fori_loop(0, FIELDS, by_slot, 0)

    def d_send(i, _):
        p = lax.rem(t + i, TAB)
        send(dslot.at[pair(p)], rd_ref.at[pair(t)], ds.at[p], dr.at[t], {"tab": p})
        return 0

    lax.fori_loop(1, TAB, d_send, 0)
    rd_ref[pair(t)] = dslot[pair(t)]

    d_in = mm(squeeze, d_act, NT, HI)
    d_out = mm(act_one, d_pre_w, NT, HI)
    both_d = jnp.where(diag, dbil[...], 0.0)
    d_bil = mm(mm(small_cols.astype(F32), both_d, NN, HI), small_rows.astype(F32), NN, HI)
    sr[0, c] = jnp.zeros((SMALL, LANES), BF)
    sr[0, c, 0:FIELDS, 0:E] = d_in.astype(BF)
    sr[0, c, FIELDS : FIELDS + E, 0:FIELDS] = d_out.astype(BF)
    sr[0, c, FIELDS + E : FIELDS + 2 * E, 0:E] = d_bil.astype(BF)
    low = iota((16, LANES), 0)
    last = jnp.where(low == 0, d_last[:, :LANES], jnp.where(low == 1, d_last[:, LANES:], 0.0))
    sr[0, c, FIELDS + 2 * E : SMALL] = last.astype(BF)

    def peers(phase):
        if phase == 0:
            return c, [(1 - c, mate)]
        if phase == 1:
            return a, [(lax.rem(a + d, SIDE), {"tab": at(lax.rem(a + d, SIDE), b)}) for d in range(1, SIDE)]
        if phase == 2:
            return b, [(lax.rem(b + d, SIDE), {"tab": at(a, lax.rem(b + d, SIDE))}) for d in range(1, SIDE)]
        return r, [(lax.rem(r + d, REP), {"rep": lax.rem(r + d, REP)}) for d in range(1, REP)]

    def small_start(phase):
        me, others = peers(phase)
        for d, (_, dev) in enumerate(others):
            send(sr.at[phase, me], sr.at[phase, me], ss.at[phase, d], sq_r.at[phase, me], dev)

    def small_end(phase):
        me, others = peers(phase)
        for d, (who, dev) in enumerate(others):
            got(sr.at[phase, who], ss.at[phase, d], sq_r.at[phase, who], dev)
        size = 2 if phase == 0 else 4
        out = sr[phase, 0].astype(F32)
        for k in range(1, size):
            out = out + sr[phase, k].astype(F32)
        return out

    small_start(0)

    for d in range(1, SIDE):
        i = lax.rem(a + d, SIDE)
        got(r1.at[i], s1.at[d], q1.at[i], {"tab": at(i, b)})

    def first_sum(k, _):
        out = dfb[a, k].astype(F32)
        for d in range(1, SIDE):
            out = out + r1[lax.rem(a + d, SIDE), k].astype(F32)
        dfb[a, k] = out.astype(BF)
        return 0

    for d in range(1, SIDE):
        k = lax.rem(b + d, SIDE)
        first_sum(k, 0)
        send(dfb.at[a, k], r2.at[b], s2.at[d], q2.at[b], {"tab": at(a, k)})
    first_sum(b, 0)

    sr[1, a] = small_end(0).astype(BF)
    small_start(1)

    load_x.wait()

    def d_wait(i, _):
        p = lax.rem(t + i, TAB)
        got(rd_ref.at[pair(p)], ds.at[p], dr.at[p], {"tab": p})
        return 0

    lax.fori_loop(1, TAB, d_wait, 0)

    def proj_pass(j, acc):
        left = jnp.concatenate([rd_ref[pair(2 * j)].reshape(2 * E, LANES), rd_ref[pair(2 * j + 1)].reshape(2 * E, LANES)], axis=1)
        right = jnp.concatenate([xs[0, rows256(j), :], xs[1, rows256(j), :]], axis=1)
        return acc + mm(left, right, NN)

    acc = lax.fori_loop(0, TAB // 2, proj_pass, jnp.zeros((2 * E, 2 * LANES), F32))
    dz[r] = jnp.concatenate([acc[:E, :LANES], acc[E:, LANES:]], axis=0).astype(BF)
    for d in range(1, REP):
        o = lax.rem(r + d, REP)
        send(dz.at[r], dz.at[r], sd.at[d], qd.at[r], {"rep": o})

    sr[2, b] = small_end(1).astype(BF)
    small_start(2)

    for d in range(1, SIDE):
        k = lax.rem(b + d, SIDE)
        got(r2.at[k], s2.at[d], q2.at[k], {"tab": at(a, k)})
    out = dfb[a, b].astype(F32)
    for d in range(1, SIDE):
        out = out + r2[lax.rem(b + d, SIDE)].astype(F32)
    rz[r] = out.astype(BF)
    for d in range(1, REP):
        o = lax.rem(r + d, REP)
        send(rz.at[r], rz.at[r], sz.at[d], qz.at[r], {"rep": o})

    sr[3, r] = small_end(2).astype(BF)
    small_start(3)

    for d in range(1, REP):
        o = lax.rem(r + d, REP)
        got(rz.at[o], sz.at[d], qz.at[o], {"rep": o})
    out = rz[0].astype(F32)
    for k in range(1, REP):
        out = out + rz[k].astype(F32)
    df_ref[...] = out[: 2 * LANES]
    mine = block_of(t)
    ag_ref[mine] = out[2 * LANES :].astype(BF)

    def g_send(i, _):
        p = lax.rem(t + i, TAB)
        send(ag_ref.at[mine], ag_ref.at[mine], gs.at[p], gr.at[t], {"tab": p})
        return 0

    lax.fori_loop(1, TAB, g_send, 0)

    for d in range(1, REP):
        o = lax.rem(r + d, REP)
        got(dz.at[o], sd.at[d], qd.at[o], {"rep": o})
    out = dz[0].astype(F32)
    for k in range(1, REP):
        out = out + dz[k].astype(F32)
    dpt_ref[...] = out
    smf_ref[...] = small_end(3)

    def last_wait(i, _):
        p = lax.rem(t + i, TAB)
        dev = {"tab": p}
        got(lg_ref.at[p], ls.at[p], lr.at[p], dev)
        got(ag_ref.at[block_of(p)], gs.at[p], gr.at[p], dev)
        sent(e_ref.at[p], es.at[p], er.at[p], dev)
        sent(dslot.at[pair(p)], ds.at[p], dr.at[p], dev)
        sent(lg_ref.at[t], ls.at[p], lr.at[p], dev)
        sent(ag_ref.at[mine], gs.at[p], gr.at[p], dev)
        return 0

    lax.fori_loop(1, TAB, last_wait, 0)
    sent(js.at[half], ps.at[0], pr.at[0], mate)
    sent(dpb.at[0], ps.at[1], pr.at[1], mate)
    sent(d2.at[half], ps.at[2], pr.at[2], mate)
    for d in range(1, SIDE):
        i = lax.rem(a + d, SIDE)
        k = lax.rem(b + d, SIDE)
        o = lax.rem(r + d, REP)
        sent(dfb.at[i], s1.at[d], q1.at[i], {"tab": at(i, b)})
        sent(dfb.at[a, k], s2.at[d], q2.at[k], {"tab": at(a, k)})
        sent(rz.at[r], sz.at[d], qz.at[r], {"rep": o})
        sent(dz.at[r], sd.at[d], qd.at[r], {"rep": o})
    for phase in range(4):
        me, others = peers(phase)
        for d, (_, dev) in enumerate(others):
            sent(sr.at[phase, me], ss.at[phase, d], sq_r.at[phase, me], dev)


def exchange(inv, placement, e, labels, sin, sout, bil, w2, wl, w1, pooled):
    vmem = pl.BlockSpec(memory_space=pltpu.VMEM)
    smem = pl.BlockSpec(memory_space=pltpu.SMEM)
    hbm = pl.BlockSpec(memory_space=pl.ANY)
    rows = FIELDS * E
    dma = pltpu.SemaphoreType.DMA
    return pl.pallas_call(
        main_kernel,
        in_specs=[smem, smem] + [vmem] * 7 + [hbm, hbm],
        out_specs=[vmem] * 6,
        out_shape=[
            jax.ShapeDtypeStruct((FIELDS, E, LANES), BF),
            jax.ShapeDtypeStruct((TAB, 1, LANES), F32),
            jax.ShapeDtypeStruct((2 * LANES, LANES), F32),
            jax.ShapeDtypeStruct((TAB, 16, LANES), BF),
            jax.ShapeDtypeStruct((SMALL, LANES), F32),
            jax.ShapeDtypeStruct((2 * E, LANES), F32),
        ],
        scratch_shapes=[
            pltpu.VMEM(w1.shape, BF),
            pltpu.VMEM(pooled.shape, BF),
            pltpu.VMEM((FIELDS, E, LANES), BF),
            pltpu.VMEM((rows, LANES), BF),
            pltpu.VMEM((2, rows, LANES), F32),
            pltpu.VMEM((2, rows, LANES), F32),
            pltpu.VMEM((FIELDS, LANES), F32),
            pltpu.VMEM((FIELDS, LANES), F32),
            pltpu.VMEM((FIELDS, LANES), F32),
            pltpu.VMEM((FIELDS, LANES), F32),
            pltpu.VMEM((TAB, LANES, LANES), BF),
            pltpu.VMEM((16, LANES, LANES), BF),
            pltpu.VMEM((2, LANES, HID), BF),
            pltpu.VMEM((TAB, 16, LANES), BF),
            pltpu.VMEM((16, 16, LANES), BF),
            pltpu.VMEM((HID, HID), F32),
            pltpu.VMEM((FIELDS, E, LANES), BF),
            pltpu.VMEM((FIELDS, E, LANES), BF),
            pltpu.VMEM((SIDE, SIDE, BLOCK, LANES), BF),
            pltpu.VMEM((SIDE, SIDE, BLOCK, LANES), BF),
            pltpu.VMEM((SIDE, BLOCK, LANES), BF),
            pltpu.VMEM((REP, BLOCK, LANES), BF),
            pltpu.VMEM((4, 4, SMALL, LANES), BF),
            pltpu.VMEM((REP, 2 * E, LANES), BF),
            dma((2,)),
            dma((TAB,)), dma((TAB,)), dma((TAB,)), dma((TAB,)),
            dma((TAB,)), dma((TAB,)), dma((TAB,)), dma((TAB,)),
            dma((3,)), dma((3,)),
            dma((4,)), dma((4,)), dma((4,)), dma((4,)), dma((4,)), dma((4,)),
            dma((4, 4)), dma((4, 4)), dma((4,)), dma((4,)),
        ],
        compiler_params=pltpu.CompilerParams(
            collective_id=0, has_side_effects=True, vmem_limit_bytes=40 << 20
        ),
        name="exchange",
    )(inv, placement, e, labels, sin, sout, bil, w2, wl, w1, pooled)


def finish_kernel(
    tab_ref, rd_ref, pt_ref, mask_ref, lg_ref, df_ref, ag_ref, smf_ref, dpt_ref, route_ref,
    scores_ref, dx_ref, dproj_ref, din_ref, dout_ref, dbil_ref, dfirst_ref, dsecond_ref, dlast_ref,
):
    j = pl.program_id(0)
    pt = pt_ref[...]
    nil = jnp.zeros((E, LANES), BF)
    wide = jnp.concatenate(
        [jnp.concatenate([pt[:E], nil], axis=1), jnp.concatenate([nil, pt[E:]], axis=1)], axis=0
    )
    blocks = rd_ref.shape[0] // 2
    for k in range(blocks):
        out = mm(rd_ref[2 * k : 2 * k + 2].reshape(2 * E, LANES), wide, TN).astype(BF)
        dx_ref[0, k * LANES : (k + 1) * LANES] = out[:, :LANES]
        dx_ref[1, k * LANES : (k + 1) * LANES] = out[:, LANES:]

    @pl.when(j == 0)
    def _():
        idx = route_ref[:, pl.ds(pl.multiple_of(tab_ref[0] * LANES, LANES), LANES)]
        table = lg_ref[...].reshape(TAB, LANES)
        low = jnp.broadcast_to(lax.rem(idx, LANES), (TAB, LANES))
        found = jnp.take_along_axis(table, low, axis=1)
        scores_ref[...] = jnp.sum(
            jnp.where(idx // LANES == iota((TAB, LANES), 0), found, 0.0), axis=0, keepdims=True
        )
        eye = (iota((LANES, LANES), 0) == iota((LANES, LANES), 1)).astype(F32)
        kept = jnp.where(mask_ref[...] > 0, dpt_ref[...], 0.0)
        for s in range(2):
            dproj_ref[s] = mm(eye, kept[s * E : (s + 1) * E], NT, HI)
        din_ref[...] = smf_ref[0:FIELDS, 0:E]
        dout_ref[...] = smf_ref[FIELDS : FIELDS + E, 0:FIELDS]
        dbil_ref[...] = smf_ref[FIELDS + E : FIELDS + 2 * E, 0:E]
        dlast_ref[:, 0:LANES] = smf_ref[FIELDS + 2 * E : FIELDS + 2 * E + 1, :]
        dlast_ref[:, LANES:] = smf_ref[FIELDS + 2 * E + 1 : FIELDS + 2 * E + 2, :]
        dfirst_ref[:, 0:LANES] = df_ref[0:LANES, :]
        dfirst_ref[:, LANES:] = df_ref[LANES : 2 * LANES, :]
        for i in range(16):
            dsecond_ref[16 * i : 16 * i + 16, 0:LANES] = ag_ref[2 * i].astype(F32)
            dsecond_ref[16 * i : 16 * i + 16, LANES:] = ag_ref[2 * i + 1].astype(F32)


def finish(tab, rd, pt, mask, lg, df, ag, smf, dpt, route, pooled_shape):
    steps = 4
    rows = pooled_shape[1]
    chunk = rows // steps

    def whole(shape):
        return pl.BlockSpec(shape, lambda j, t: (0,) * len(shape))

    outs = [
        ((1, LANES), F32), (pooled_shape, BF), ((2, LANES, E), F32), ((FIELDS, E), F32), ((E, FIELDS), F32),
        ((E, E), F32), ((LANES, HID), F32), ((HID, HID), F32), ((1, HID), F32),
    ]
    out_specs = [whole(s) for s, _ in outs]
    out_specs[1] = pl.BlockSpec((2, chunk, LANES), lambda j, t: (0, j, 0))
    grid_spec = pltpu.PrefetchScalarGridSpec(
        num_scalar_prefetch=1,
        grid=(steps,),
        in_specs=[pl.BlockSpec((rd.shape[0] // steps, E, LANES), lambda j, t: (j, 0, 0))]
        + [whole(v.shape) for v in (pt, mask, lg, df, ag, smf, dpt, route)],
        out_specs=out_specs,
    )
    return pl.pallas_call(
        finish_kernel,
        grid_spec=grid_spec,
        out_shape=[jax.ShapeDtypeStruct(s, d) for s, d in outs],
        compiler_params=pltpu.CompilerParams(vmem_limit_bytes=16 << 20),
        name="finish",
    )(tab, rd, pt, mask, lg, df, ag, smf, dpt, route)


def shards(pooled, widths, placement, route, labels, proj, senet_in, senet_out, bilinear, w_first, w_second, w_last):
    tab = lax.axis_index("tab").astype(jnp.int32).reshape(1)
    e, pt, mask, inv = project(tab, placement, widths, pooled, proj)
    rd, lg, df, ag, smf, dpt = exchange(
        inv, placement, e, labels, senet_in, senet_out, bilinear, w_second, w_last[None, :], w_first, pooled
    )
    scores, dx, dproj, din, dout, dbil, dfirst, dsecond, dlast = finish(
        tab, rd, pt, mask, lg, df, ag, smf, dpt, route, pooled.shape
    )
    return scores, dx, dproj, din, dout, dbil, dfirst, dsecond, dlast[0]


def solution(mesh):
    whole = P()
    placed = (
        P("tab", "rep", None), whole, whole, P("rep", None), P("rep", None), whole, whole, whole, whole, whole,
        whole, whole,
    )
    return jax.shard_map(
        shards,
        mesh=mesh,
        in_specs=placed,
        out_specs=(
            P("rep", "tab"), P("tab", "rep", None), P("tab", None, None), whole, whole, whole, P("tab", None),
            whole, whole,
        ),
        check_vma=False,
    )
```

```python
import functools

import jax
import jax.numpy as jnp
from jax import lax
from jax.experimental import pallas as pl
from jax.experimental.pallas import tpu as pltpu
from jax.sharding import PartitionSpec as P

F32 = jnp.float32
BF = jnp.bfloat16
HI = lax.Precision.HIGHEST
NN = (((1,), (0,)), ((), ()))
NT = (((1,), (1,)), ((), ()))
TN = (((0,), (0,)), ((), ()))

FIELDS = 64
E = 32
TAB = 32
REP = 4
EARLY = 4
SIDE = 4
PARTS = 4
LANES = 128
HID = 256
BLOCK = 256
SMALL = 80
FACTOR = 0.125


def mm(a, b, dims, precision=None):
    return lax.dot_general(a, b, dims, precision=precision, preferred_element_type=F32)


def slope(u):
    s = jax.nn.sigmoid(u)
    return s * (1.0 + u * (1.0 - s))


def iota(shape, dim):
    return lax.broadcasted_iota(jnp.int32, shape, dim)


def send(src, dst, ssem, rsem, dev):
    pltpu.make_async_remote_copy(
        src_ref=src, dst_ref=dst, send_sem=ssem, recv_sem=rsem, device_id=dev,
        device_id_type=pl.DeviceIdType.MESH,
    ).start()


def got(dst, ssem, rsem, dev):
    pltpu.make_async_remote_copy(
        src_ref=dst, dst_ref=dst, send_sem=ssem, recv_sem=rsem, device_id=dev,
        device_id_type=pl.DeviceIdType.MESH,
    ).wait_recv()


def sent(src, ssem, rsem, dev):
    pltpu.make_async_remote_copy(
        src_ref=src, dst_ref=src, send_sem=ssem, recv_sem=rsem, device_id=dev,
        device_id_type=pl.DeviceIdType.MESH,
    ).wait_send()


def main_kernel(
    inv_ref, place_ref, width_ref, labels_hbm, proj_hbm, sin_hbm, sout_hbm, bil_hbm, w1_hbm, w2_hbm, wl_hbm, pooled_hbm,
    rd_ref, lg_ref, df_ref, ag_ref, smf_ref, dpt_ref, pt_ref,
    labels_ref, projs, sin_ref, sout_ref, bil_ref, w1, w2_ref, wl_ref, xs, e_ref, recv, emb, prod, du, sq, wts, dpw, dsq, js, jp, dpb, d2, d2p, demb, dslot, dfb, r1, r2, rz, sr, dz, d2b, rd1, rd2, rdz,
    load_sem, es, er, ds, dr, ls, lr, gs, gr, ps, pr, s1, q1, s2, q2, sz, qz, ss, sq_r, sd, qd, s1d, q1d, s2d, q2d, szd, qzd,
):
    t = lax.axis_index("tab")
    r = lax.axis_index("rep")
    c = lax.rem(t, 2)
    n = t // 2
    x = n // SIDE
    y = lax.rem(n, SIDE)
    a = x + c * (y - x)
    b = y + c * (x - y)

    def at(a_, b_):
        return ((a_ + c * (b_ - a_)) * SIDE + (b_ + c * (a_ - b_))) * 2 + c

    def block_of(tab):
        c_ = lax.rem(tab, 2)
        n_ = tab // 2
        x_ = n_ // SIDE
        y_ = lax.rem(n_, SIDE)
        return 16 * c_ + SIDE * (x_ + c_ * (y_ - x_)) + y_ + c_ * (x_ - y_)

    mate = {"tab": t + 1 - 2 * c}
    barrier = pltpu.get_barrier_semaphore()

    def hello(i, _):
        pl.semaphore_signal(barrier, inc=1, device_id={"tab": lax.rem(t + i, TAB)}, device_id_type=pl.DeviceIdType.MESH)
        return 0

    lax.fori_loop(1, TAB, hello, 0)
    for d in range(1, REP):
        pl.semaphore_signal(barrier, inc=1, device_id={"rep": lax.rem(r + d, REP)}, device_id_type=pl.DeviceIdType.MESH)

    pairs = (
        (proj_hbm, projs), (labels_hbm, labels_ref), (bil_hbm, bil_ref), (sin_hbm, sin_ref), (sout_hbm, sout_ref),
        (w2_hbm, w2_ref), (wl_hbm, wl_ref), (w1_hbm, w1),
    )
    loads = [pltpu.make_async_copy(src, dst, load_sem.at[i]) for i, (src, dst) in enumerate(pairs)]
    part = xs.shape[1] // PARTS
    for k in range(PARTS):
        piece = pl.ds(k * part, part)
        loads.append(pltpu.make_async_copy(pooled_hbm.at[:, piece], xs.at[:, piece], load_sem.at[len(pairs) + k]))
    for k in [0] + list(range(len(pairs), len(pairs) + PARTS)) + list(range(1, len(pairs))):
        loads[k].start()

    loads[0].wait()
    keep = []
    for i in range(2):
        field = place_ref[2 * t + i]
        keep.append(iota((E, LANES), 1) < width_ref[field])
        pt_ref[i * E : (i + 1) * E, :] = jnp.where(keep[i], projs[field].astype(F32), 0.0).astype(BF)
    for k in range(PARTS):
        loads[len(pairs) + k].wait()
        for i in range(2):
            out = mm(pt_ref[i * E : (i + 1) * E, :], xs[i, k * part : (k + 1) * part, :], NT).astype(BF)
            for d in range(part // LANES):
                e_ref[k * (part // LANES) + d, i] = out[:, d * LANES : (d + 1) * LANES]

    small_rows = (lax.rem(iota((HID, E), 0), E) == iota((HID, E), 1)).astype(BF)
    loads[1].wait()
    loads[2].wait()
    small_cols = (lax.rem(iota((E, HID), 1), E) == iota((E, HID), 0)).astype(BF)
    diag = (iota((HID, HID), 0) // E) == (iota((HID, HID), 1) // E)
    bil = bil_ref[...].astype(BF)
    tall = mm(small_rows, bil, NN).astype(BF)
    tall_t = mm(small_rows, bil, NT).astype(BF)
    kron = jnp.where(diag, mm(tall, small_cols, NN), 0.0).astype(BF)
    kron_t = jnp.where(diag, mm(tall_t, small_cols, NN), 0.0).astype(BF)
    square = iota((LANES, LANES), 0) == iota((LANES, LANES), 1)
    label_row = labels_ref[:, pl.ds(pl.multiple_of(t * LANES, LANES), LANES)].astype(F32)
    target = jnp.sum(jnp.where(square, label_row, 0.0), axis=1, keepdims=True)

    pl.semaphore_wait(barrier, TAB - 1 + REP - 1)

    def pair(p):
        return pl.ds(p * 2, 2)

    def e_send(i, _):
        p = lax.rem(t + i, TAB)
        send(e_ref.at[p], recv.at[pair(t)], es.at[p], er.at[t], {"tab": p})
        return 0

    lax.fori_loop(1, TAB, e_send, 0)
    recv[pair(t)] = e_ref[t]

    def e_wait(i, _):
        p = lax.rem(t + i, TAB)
        got(recv.at[pair(p)], es.at[p], er.at[p], {"tab": p})
        return 0

    lax.fori_loop(1, TAB, e_wait, 0)

    def rows32(f):
        return pl.ds(pl.multiple_of(f * E, E), E)

    def by_field(f, _):
        emb[rows32(f), :] = recv[inv_ref[f]]
        return 0

    lax.fori_loop(0, FIELDS, by_field, 0)

    groups = FIELDS // 8

    def rows256(g):
        return pl.ds(pl.multiple_of(g * HID, HID), HID)

    def rows8(g):
        return pl.ds(pl.multiple_of(g * 8, 8), 8)

    def cube(v):
        return v.reshape(8, E, LANES)

    def flat(v):
        return v.reshape(HID, LANES)

    def first_pass(g, total):
        u = cube(emb[rows256(g), :].astype(F32))
        sq[rows8(g), :] = jnp.sum(u, axis=1) * (1.0 / E)
        return total + jnp.sum(u, axis=0)

    zero = jnp.zeros((E, LANES), F32)
    total = lax.fori_loop(0, groups, first_pass, zero)
    squeeze = sq[...]
    loads[3].wait()
    loads[4].wait()
    pre_one = mm(sin_ref[...], squeeze, NN, HI)
    act_one = pre_one * jax.nn.sigmoid(pre_one)
    weights = jax.nn.sigmoid(mm(sout_ref[...], act_one, TN, HI))
    wts[...] = weights

    def scaled_of(g):
        u = cube(emb[rows256(g), :].astype(F32))
        return u, u * wts[rows8(g), :][:, None, :]

    def second_pass(g, tot):
        return tot + jnp.sum(scaled_of(g)[1], axis=0)

    total_s = lax.fori_loop(0, groups, second_pass, zero)

    for k in range(5, len(pairs)):
        loads[k].wait()

    def third_pass(g, acc):
        u, sc = scaled_of(g)
        for k, (v, vb, tot) in enumerate(((u, emb[rows256(g), :], total), (sc, flat(sc).astype(BF), total_s))):
            p = mm(kron_t, vb, NN)
            prod[k, rows256(g), :] = p
            j = flat(cube(p) * (tot[None] - v) * FACTOR).astype(BF)
            chip = k * groups + g
            js[chip] = j[:LANES]
            js[16 + lax.rem(chip, SIDE) * SIDE + chip // SIDE] = j[LANES:]
            acc = acc + mm(j, w1[rows256(k * groups + g), :], TN)
        return acc

    pre_hidden = lax.fori_loop(0, groups, third_pass, jnp.zeros((LANES, HID), F32))
    half = pl.ds((1 - c) * 16, 16)
    send(js.at[half], jp, ps.at[0], pr.at[0], mate)

    h1 = (pre_hidden * jax.nn.sigmoid(pre_hidden)).astype(BF)
    pre_second = mm(h1, w2_ref[...], NN)
    h2 = (pre_second * jax.nn.sigmoid(pre_second)).astype(BF).astype(F32)
    wl = wl_ref[...].reshape(1, HID).astype(F32)
    logit = jnp.sum(h2 * wl, axis=1, keepdims=True)
    lg_ref[t] = jnp.sum(jnp.where(square, logit, 0.0), axis=0, keepdims=True)

    def l_send(i, _):
        p = lax.rem(t + i, TAB)
        send(lg_ref.at[t], lg_ref.at[t], ls.at[p], lr.at[t], {"tab": p})
        return 0

    lax.fori_loop(1, TAB, l_send, 0)
    grad = jax.nn.sigmoid(logit) - target
    d_last = jnp.sum(grad * h2, axis=0, keepdims=True)
    dp2 = (grad * wl * slope(pre_second)).astype(BF)
    d_second = mm(h1, dp2, TN).astype(BF)
    for i in range(16):
        for h in range(2):
            d2[2 * i + h] = d_second[16 * i : 16 * i + 16, LANES * h : LANES * h + LANES]
    dp1 = (mm(dp2, w2_ref[...], NT) * slope(pre_hidden)).astype(BF)
    dpb[0] = dp1
    send(dpb.at[0], dpb.at[1], ps.at[1], pr.at[1], mate)
    send(d2.at[half], d2p, ps.at[2], pr.at[2], mate)

    def side(v):
        return jnp.concatenate([v[i * E : (i + 1) * E] for i in range(8)], axis=1)

    def fourth_pass(g, sums):
        u, sc = scaled_of(g)
        out = []
        bil_sum = sums[2]
        for k, (v, vb, tot) in enumerate(((u, emb[rows256(g), :], total), (sc, flat(sc).astype(BF), total_s))):
            up = cube(mm(w1[rows256(k * groups + g), :], dp1, NT)) * FACTOR
            dq = up * cube(prod[k, rows256(g), :])
            dp = flat(up * (tot[None] - v)).astype(BF)
            du[k, rows256(g), :] = mm(kron, dp, NN) - flat(dq)
            bil_sum = bil_sum + mm(side(vb), side(dp), NT)
            out.append(sums[k] + jnp.sum(dq, axis=0))
        return (*out, bil_sum)

    sums = lax.fori_loop(0, EARLY, fourth_pass, (zero, zero, jnp.zeros((E, E), F32)))

    def peer(me, d):
        return lax.rem(me + d, SIDE)

    got(jp, ps.at[0], pr.at[0], mate)
    got(dpb.at[1], ps.at[1], pr.at[1], mate)
    got(d2p, ps.at[2], pr.at[2], mate)
    d2b[...] = (d2[pl.ds(c * 16, 16)].astype(F32) + d2p[...].astype(F32)).astype(BF).reshape(d2b.shape)
    for d in range(1, SIDE):
        i = peer(a, d)
        send(d2b.at[i], rd1.at[a], s1d.at[d], q1d.at[a], {"tab": at(i, b)})

    both = dpb[...].reshape(2 * LANES, HID)

    def d_first_row(i):
        left = jnp.concatenate(
            [js[pl.ds(16 * c + i * SIDE, SIDE)].reshape(SIDE * LANES, LANES), jp[pl.ds(i * SIDE, SIDE)].reshape(SIDE * LANES, LANES)],
            axis=1,
        )
        out = mm(left, both, NN).astype(BF)
        for k in range(SIDE):
            dfb[i, k, 0:LANES] = out[k * LANES : (k + 1) * LANES, :LANES]
            dfb[i, k, LANES:] = out[k * LANES : (k + 1) * LANES, LANES:]

    for d in range(1, SIDE):
        i = peer(a, d)
        d_first_row(i)
        send(dfb.at[i], r1.at[a], s1.at[d], q1.at[a], {"tab": at(i, b)})
    d_first_row(a)

    for d in range(1, SIDE):
        i = peer(a, d)
        got(rd1.at[i], s1d.at[d], q1d.at[i], {"tab": at(i, b)})
    out = d2b[a].astype(F32)
    for d in range(1, SIDE):
        out = out + rd1[peer(a, d)].astype(F32)
    d2b[a] = out.astype(BF)
    for d in range(1, SIDE):
        k = peer(b, d)
        send(d2b.at[a, k], rd2.at[b], s2d.at[d], q2d.at[b], {"tab": at(a, k)})

    sum_q, sum_qs, d_bil = lax.fori_loop(EARLY, groups, fourth_pass, sums)

    for d in range(1, SIDE):
        k = peer(b, d)
        got(rd2.at[k], s2d.at[d], q2d.at[k], {"tab": at(a, k)})
    out = d2b[a, b].astype(F32)
    for d in range(1, SIDE):
        out = out + rd2[peer(b, d)].astype(F32)
    rdz[r] = out.astype(BF)
    for d in range(1, REP):
        send(rdz.at[r], rdz.at[r], szd.at[d], qzd.at[r], {"rep": peer(r, d)})

    def fifth_pass(g, _):
        u = cube(emb[rows256(g), :].astype(F32))
        w = wts[rows8(g), :]
        d_w = jnp.sum((cube(du[1, rows256(g), :]) + sum_qs[None]) * u, axis=1)
        dpw[rows8(g), :] = d_w * w * (1.0 - w)
        return 0

    lax.fori_loop(0, groups, fifth_pass, 0)
    d_pre_w = dpw[...]
    d_act = mm(sout_ref[...], d_pre_w, NN, HI) * slope(pre_one)
    dsq[...] = mm(sin_ref[...], d_act, TN, HI) * (1.0 / E)

    def sixth_pass(g, _):
        w = wts[rows8(g), :][:, None, :]
        out = cube(du[0, rows256(g), :]) + sum_q[None] + w * (cube(du[1, rows256(g), :]) + sum_qs[None])
        out = out + dsq[rows8(g), :][:, None, :]
        demb[rows8(g)] = out.astype(BF)
        return 0

    lax.fori_loop(0, groups, sixth_pass, 0)

    def by_slot(s, _):
        dslot[s] = demb[place_ref[s]]
        return 0

    lax.fori_loop(0, FIELDS, by_slot, 0)

    def d_send(i, _):
        p = lax.rem(t + i, TAB)
        send(dslot.at[pair(p)], rd_ref.at[pair(t)], ds.at[p], dr.at[t], {"tab": p})
        return 0

    lax.fori_loop(1, TAB, d_send, 0)
    rd_ref[pair(t)] = dslot[pair(t)]

    d_in = mm(d_act, squeeze, NT, HI)
    d_out = mm(act_one, d_pre_w, NT, HI)
    sr[0, c, 0:E] = jnp.concatenate([d_in, d_out], axis=1).astype(BF)
    sr[0, c, E : 2 * E] = jnp.zeros((E, LANES), BF)
    sr[0, c, E : 2 * E, 0:E] = d_bil.astype(BF)
    low = iota((16, LANES), 0)
    last = jnp.where(low == 0, d_last[:, :LANES], jnp.where(low == 1, d_last[:, LANES:], 0.0))
    sr[0, c, 2 * E : SMALL] = last.astype(BF)

    def peers(phase):
        if phase == 0:
            return c, [(1 - c, mate)]
        if phase == 1:
            return a, [(lax.rem(a + d, SIDE), {"tab": at(lax.rem(a + d, SIDE), b)}) for d in range(1, SIDE)]
        if phase == 2:
            return b, [(lax.rem(b + d, SIDE), {"tab": at(a, lax.rem(b + d, SIDE))}) for d in range(1, SIDE)]
        return r, [(lax.rem(r + d, REP), {"rep": lax.rem(r + d, REP)}) for d in range(1, REP)]

    def small_start(phase):
        me, others = peers(phase)
        for d, (_, dev) in enumerate(others):
            send(sr.at[phase, me], sr.at[phase, me], ss.at[phase, d], sq_r.at[phase, me], dev)

    def small_end(phase):
        me, others = peers(phase)
        for d, (who, dev) in enumerate(others):
            got(sr.at[phase, who], ss.at[phase, d], sq_r.at[phase, who], dev)
        size = 2 if phase == 0 else 4
        out = sr[phase, 0].astype(F32)
        for k in range(1, size):
            out = out + sr[phase, k].astype(F32)
        return out

    small_start(0)

    for d in range(1, REP):
        got(rdz.at[peer(r, d)], szd.at[d], qzd.at[peer(r, d)], {"rep": peer(r, d)})
    out = rdz[0].astype(F32)
    for k in range(1, REP):
        out = out + rdz[k].astype(F32)
    mine = block_of(t)
    ag_ref[mine] = out.astype(BF)

    def g_send(i, _):
        p = lax.rem(t + i, TAB)
        send(ag_ref.at[mine], ag_ref.at[mine], gs.at[p], gr.at[t], {"tab": p})
        return 0

    lax.fori_loop(1, TAB, g_send, 0)

    for d in range(1, SIDE):
        i = lax.rem(a + d, SIDE)
        got(r1.at[i], s1.at[d], q1.at[i], {"tab": at(i, b)})

    def first_sum(k, _):
        out = dfb[a, k].astype(F32)
        for d in range(1, SIDE):
            out = out + r1[lax.rem(a + d, SIDE), k].astype(F32)
        dfb[a, k] = out.astype(BF)
        return 0

    for d in range(1, SIDE):
        k = lax.rem(b + d, SIDE)
        first_sum(k, 0)
        send(dfb.at[a, k], r2.at[b], s2.at[d], q2.at[b], {"tab": at(a, k)})
    first_sum(b, 0)

    sr[1, a] = small_end(0).astype(BF)
    small_start(1)


    def d_wait(i, _):
        p = lax.rem(t + i, TAB)
        got(rd_ref.at[pair(p)], ds.at[p], dr.at[p], {"tab": p})
        return 0

    lax.fori_loop(1, TAB, d_wait, 0)

    def proj_pass(j, acc):
        left = jnp.concatenate([rd_ref[pair(2 * j)].reshape(2 * E, LANES), rd_ref[pair(2 * j + 1)].reshape(2 * E, LANES)], axis=1)
        right = jnp.concatenate([xs[0, rows256(j), :], xs[1, rows256(j), :]], axis=1)
        return acc + mm(left, right, NN)

    acc = lax.fori_loop(0, TAB // 2, proj_pass, jnp.zeros((2 * E, 2 * LANES), F32))
    dz[r] = jnp.concatenate([acc[:E, :LANES], acc[E:, LANES:]], axis=0).astype(BF)
    for d in range(1, REP):
        o = lax.rem(r + d, REP)
        send(dz.at[r], dz.at[r], sd.at[d], qd.at[r], {"rep": o})

    sr[2, b] = small_end(1).astype(BF)
    small_start(2)

    for d in range(1, SIDE):
        k = lax.rem(b + d, SIDE)
        got(r2.at[k], s2.at[d], q2.at[k], {"tab": at(a, k)})
    out = dfb[a, b].astype(F32)
    for d in range(1, SIDE):
        out = out + r2[lax.rem(b + d, SIDE)].astype(F32)
    rz[r] = out.astype(BF)
    for d in range(1, REP):
        o = lax.rem(r + d, REP)
        send(rz.at[r], rz.at[r], sz.at[d], qz.at[r], {"rep": o})

    sr[3, r] = small_end(2).astype(BF)
    small_start(3)

    for d in range(1, REP):
        o = lax.rem(r + d, REP)
        got(rz.at[o], sz.at[d], qz.at[o], {"rep": o})
    out = rz[0].astype(F32)
    for k in range(1, REP):
        out = out + rz[k].astype(F32)
    df_ref[...] = out

    for d in range(1, REP):
        o = lax.rem(r + d, REP)
        got(dz.at[o], sd.at[d], qd.at[o], {"rep": o})
    out = dz[0].astype(F32)
    for k in range(1, REP):
        out = out + dz[k].astype(F32)
    for i in range(2):
        dpt_ref[i] = jnp.where(keep[i], out[i * E : (i + 1) * E], 0.0)
    smf_ref[...] = small_end(3)

    def last_wait(i, _):
        p = lax.rem(t + i, TAB)
        dev = {"tab": p}
        got(lg_ref.at[p], ls.at[p], lr.at[p], dev)
        got(ag_ref.at[block_of(p)], gs.at[p], gr.at[p], dev)
        sent(e_ref.at[p], es.at[p], er.at[p], dev)
        sent(dslot.at[pair(p)], ds.at[p], dr.at[p], dev)
        sent(lg_ref.at[t], ls.at[p], lr.at[p], dev)
        sent(ag_ref.at[mine], gs.at[p], gr.at[p], dev)
        return 0

    lax.fori_loop(1, TAB, last_wait, 0)
    sent(js.at[half], ps.at[0], pr.at[0], mate)
    sent(dpb.at[0], ps.at[1], pr.at[1], mate)
    sent(d2.at[half], ps.at[2], pr.at[2], mate)
    for d in range(1, SIDE):
        i = lax.rem(a + d, SIDE)
        k = lax.rem(b + d, SIDE)
        o = lax.rem(r + d, REP)
        sent(dfb.at[i], s1.at[d], q1.at[i], {"tab": at(i, b)})
        sent(dfb.at[a, k], s2.at[d], q2.at[k], {"tab": at(a, k)})
        sent(rz.at[r], sz.at[d], qz.at[r], {"rep": o})
        sent(d2b.at[i], s1d.at[d], q1d.at[i], {"tab": at(i, b)})
        sent(d2b.at[a, k], s2d.at[d], q2d.at[k], {"tab": at(a, k)})
        sent(rdz.at[r], szd.at[d], qzd.at[r], {"rep": o})
        sent(dz.at[r], sd.at[d], qd.at[r], {"rep": o})
    for phase in range(4):
        me, others = peers(phase)
        for d, (_, dev) in enumerate(others):
            sent(sr.at[phase, me], ss.at[phase, d], sq_r.at[phase, me], dev)


def exchange(inv, placement, widths, labels, proj, sin, sout, bil, w1, w2, wl, pooled):
    vmem = pl.BlockSpec(memory_space=pltpu.VMEM)
    smem = pl.BlockSpec(memory_space=pltpu.SMEM)
    hbm = pl.BlockSpec(memory_space=pltpu.HBM)
    rows = FIELDS * E
    dma = pltpu.SemaphoreType.DMA
    arrays = (labels, proj, sin, sout, bil, w1, w2, wl, pooled)
    return pl.pallas_call(
        main_kernel,
        in_specs=[smem] * 3 + [hbm] * len(arrays),
        out_specs=[vmem] * 7,
        out_shape=[
            jax.ShapeDtypeStruct((FIELDS, E, LANES), BF),
            jax.ShapeDtypeStruct((TAB, 1, LANES), F32),
            jax.ShapeDtypeStruct((BLOCK, LANES), F32),
            jax.ShapeDtypeStruct((TAB, 16, LANES), BF),
            jax.ShapeDtypeStruct((SMALL, LANES), F32),
            jax.ShapeDtypeStruct((2, E, LANES), F32),
            jax.ShapeDtypeStruct((2 * E, LANES), BF),
        ],
        scratch_shapes=[pltpu.VMEM(v.shape, v.dtype) for v in arrays]
        + [
            pltpu.VMEM((TAB, 2, E, LANES), BF),
            pltpu.VMEM((FIELDS, E, LANES), BF),
            pltpu.VMEM((rows, LANES), BF),
            pltpu.VMEM((2, rows, LANES), F32),
            pltpu.VMEM((2, rows, LANES), F32),
            pltpu.VMEM((FIELDS, LANES), F32),
            pltpu.VMEM((FIELDS, LANES), F32),
            pltpu.VMEM((FIELDS, LANES), F32),
            pltpu.VMEM((FIELDS, LANES), F32),
            pltpu.VMEM((TAB, LANES, LANES), BF),
            pltpu.VMEM((16, LANES, LANES), BF),
            pltpu.VMEM((2, LANES, HID), BF),
            pltpu.VMEM((TAB, 16, LANES), BF),
            pltpu.VMEM((16, 16, LANES), BF),
            pltpu.VMEM((FIELDS, E, LANES), BF),
            pltpu.VMEM((FIELDS, E, LANES), BF),
            pltpu.VMEM((SIDE, SIDE, BLOCK, LANES), BF),
            pltpu.VMEM((SIDE, SIDE, BLOCK, LANES), BF),
            pltpu.VMEM((SIDE, BLOCK, LANES), BF),
            pltpu.VMEM((REP, BLOCK, LANES), BF),
            pltpu.VMEM((4, 4, SMALL, LANES), BF),
            pltpu.VMEM((REP, 2 * E, LANES), BF),
            pltpu.VMEM((SIDE, SIDE, 16, LANES), BF),
            pltpu.VMEM((SIDE, SIDE, 16, LANES), BF),
            pltpu.VMEM((SIDE, 16, LANES), BF),
            pltpu.VMEM((REP, 16, LANES), BF),
            dma((8 + PARTS,)),
        ]
        + [dma((TAB,))] * 8
        + [dma((3,))] * 2
        + [dma((4,))] * 6
        + [dma((4, 4))] * 2
        + [dma((4,))] * 8,
        compiler_params=pltpu.CompilerParams(
            collective_id=0, has_side_effects=True, vmem_limit_bytes=60 * 1024 * 1024
        ),
        name="exchange",
    )(inv, placement, widths, *arrays)


def finish_kernel(
    tab_ref, rd_ref, pt_ref, lg_ref, df_ref, ag_ref, smf_ref, dpt_ref, route_ref,
    scores_ref, dx_ref, dproj_ref, din_ref, dout_ref, dbil_ref, dfirst_ref, dsecond_ref, dlast_ref,
):
    j = pl.program_id(0)
    pt = pt_ref[...]
    nil = jnp.zeros((E, LANES), BF)
    wide = jnp.concatenate(
        [jnp.concatenate([pt[:E], nil], axis=1), jnp.concatenate([nil, pt[E:]], axis=1)], axis=0
    )
    blocks = rd_ref.shape[0] // 2
    for k in range(blocks):
        out = mm(rd_ref[2 * k : 2 * k + 2].reshape(2 * E, LANES), wide, TN).astype(BF)
        dx_ref[0, k * LANES : (k + 1) * LANES] = out[:, :LANES]
        dx_ref[1, k * LANES : (k + 1) * LANES] = out[:, LANES:]

    @pl.when(j == 0)
    def _():
        idx = route_ref[:, pl.ds(pl.multiple_of(tab_ref[0] * LANES, LANES), LANES)]
        table = lg_ref[...].reshape(TAB, LANES)
        low = jnp.broadcast_to(lax.rem(idx, LANES), (TAB, LANES))
        found = jnp.take_along_axis(table, low, axis=1)
        scores_ref[...] = jnp.sum(
            jnp.where(idx // LANES == iota((TAB, LANES), 0), found, 0.0), axis=0, keepdims=True
        )
        dproj_ref[...] = dpt_ref[...]
        din_ref[...] = smf_ref[0:E, 0:FIELDS]
        dout_ref[...] = smf_ref[0:E, FIELDS:]
        dbil_ref[...] = smf_ref[E : 2 * E, 0:E]
        dlast_ref[:, 0:LANES] = smf_ref[2 * E : 2 * E + 1, :]
        dlast_ref[:, LANES:] = smf_ref[2 * E + 1 : 2 * E + 2, :]
        dfirst_ref[:, 0:LANES] = df_ref[0:LANES, :]
        dfirst_ref[:, LANES:] = df_ref[LANES : 2 * LANES, :]
        for i in range(16):
            dsecond_ref[16 * i : 16 * i + 16, 0:LANES] = ag_ref[2 * i].astype(F32)
            dsecond_ref[16 * i : 16 * i + 16, LANES:] = ag_ref[2 * i + 1].astype(F32)


def finish(tab, rd, pt, lg, df, ag, smf, dpt, route, pooled_shape):
    steps = 4
    rows = pooled_shape[1]
    chunk = rows // steps

    def whole(shape):
        return pl.BlockSpec(shape, lambda j, t: (0,) * len(shape))

    outs = [
        ((1, LANES), F32), (pooled_shape, BF), ((2, E, LANES), F32), ((E, FIELDS), F32), ((E, FIELDS), F32),
        ((E, E), F32), ((LANES, HID), F32), ((HID, HID), F32), ((1, HID), F32),
    ]
    out_specs = [whole(s) for s, _ in outs]
    out_specs[1] = pl.BlockSpec((2, chunk, LANES), lambda j, t: (0, j, 0))
    grid_spec = pltpu.PrefetchScalarGridSpec(
        num_scalar_prefetch=1,
        grid=(steps,),
        in_specs=[pl.BlockSpec((rd.shape[0] // steps, E, LANES), lambda j, t: (j, 0, 0))]
        + [whole(v.shape) for v in (pt, lg, df, ag, smf, dpt, route)],
        out_specs=out_specs,
    )
    return pl.pallas_call(
        finish_kernel,
        grid_spec=grid_spec,
        out_shape=[jax.ShapeDtypeStruct(s, d) for s, d in outs],
        compiler_params=pltpu.CompilerParams(vmem_limit_bytes=60 * 1024 * 1024),
        name="finish",
    )(tab, rd, pt, lg, df, ag, smf, dpt, route)


def shards(pooled, widths, placement, route, labels, proj, senet_in, senet_out, bilinear, w_first, w_second, w_last):
    tab = lax.axis_index("tab").astype(jnp.int32).reshape(1)
    fields = jnp.arange(FIELDS, dtype=jnp.int32)
    inv = jnp.sum(jnp.where(placement[:, None] == fields[None, :], fields[:, None], 0), axis=0)
    rd, lg, df, ag, smf, dpt, pt = exchange(
        inv, placement, widths, labels, jnp.swapaxes(proj, 1, 2), senet_in.T, senet_out, bilinear, w_first, w_second,
        w_last, pooled,
    )
    scores, dx, dproj, din, dout, dbil, dfirst, dsecond, dlast = finish(
        tab, rd, pt, lg, df, ag, smf, dpt, route, pooled.shape
    )
    return scores, dx, jnp.swapaxes(dproj, 1, 2), din.T, dout, dbil, dfirst, dsecond, dlast[0]


def solution(mesh):
    whole = P()
    placed = (
        P("tab", "rep", None), whole, whole, P("rep", None), P("rep", None), whole, whole, whole, whole, whole,
        whole, whole,
    )
    return jax.shard_map(
        shards,
        mesh=mesh,
        in_specs=placed,
        out_specs=(
            P("rep", "tab"), P("tab", "rep", None), P("tab", None, None), whole, whole, whole, P("tab", None),
            whole, whole,
        ),
        check_vma=False,
    )
```

```python
import functools

import jax
import jax.numpy as jnp
from jax import lax
from jax.experimental import pallas as pl
from jax.experimental.pallas import tpu as pltpu
from jax.sharding import PartitionSpec as P

F32 = jnp.float32
BF = jnp.bfloat16
HI = lax.Precision.HIGHEST
NN = (((1,), (0,)), ((), ()))
NT = (((1,), (1,)), ((), ()))
TN = (((0,), (0,)), ((), ()))

FIELDS = 64
E = 32
TAB = 32
REP = 4
EARLY = 4
SIDE = 4
PARTS = 4
LANES = 128
HID = 256
BLOCK = 256
SMALL = 80
FACTOR = 0.125


def mm(a, b, dims, precision=None):
    return lax.dot_general(a, b, dims, precision=precision, preferred_element_type=F32)


def slope(u):
    s = jax.nn.sigmoid(u)
    return s * (1.0 + u * (1.0 - s))


def iota(shape, dim):
    return lax.broadcasted_iota(jnp.int32, shape, dim)


def send(src, dst, ssem, rsem, dev):
    pltpu.make_async_remote_copy(
        src_ref=src, dst_ref=dst, send_sem=ssem, recv_sem=rsem, device_id=dev,
        device_id_type=pl.DeviceIdType.MESH,
    ).start()


def got(dst, ssem, rsem, dev):
    pltpu.make_async_remote_copy(
        src_ref=dst, dst_ref=dst, send_sem=ssem, recv_sem=rsem, device_id=dev,
        device_id_type=pl.DeviceIdType.MESH,
    ).wait_recv()


def sent(src, ssem, rsem, dev):
    pltpu.make_async_remote_copy(
        src_ref=src, dst_ref=src, send_sem=ssem, recv_sem=rsem, device_id=dev,
        device_id_type=pl.DeviceIdType.MESH,
    ).wait_send()


def main_kernel(
    place_ref, width_ref, place_hbm, labels_hbm, proj_hbm, sin_hbm, sout_hbm, bil_hbm, w1_hbm, w2_hbm, wl_hbm, pooled_hbm,
    rd_ref, lg_ref, df_ref, ag_ref, smf_ref, dpt_ref, pt_ref,
    place_vec, labels_ref, projs, sin_ref, sout_ref, bil_ref, w1, w2_ref, wl_ref, xs, e_ref, recv, emb, prod, du, sq, wts, dpw, dsq, js, jp, dpb, d2, d2p, demb, dslot, dfb, r1, r2, rz, sr, dz, d2b, rd1, rd2, rdz, inv_vec, inv_ref,
    load_sem, es, er, ds, dr, ls, lr, gs, gr, ps, pr, s1, q1, s2, q2, sz, qz, ss, sq_r, sd, qd, s1d, q1d, s2d, q2d, szd, qzd,
):
    t = lax.axis_index("tab")
    r = lax.axis_index("rep")
    c = lax.rem(t, 2)
    n = t // 2
    x = n // SIDE
    y = lax.rem(n, SIDE)
    a = x + c * (y - x)
    b = y + c * (x - y)

    def at(a_, b_):
        return ((a_ + c * (b_ - a_)) * SIDE + (b_ + c * (a_ - b_))) * 2 + c

    def block_of(tab):
        c_ = lax.rem(tab, 2)
        n_ = tab // 2
        x_ = n_ // SIDE
        y_ = lax.rem(n_, SIDE)
        return 16 * c_ + SIDE * (x_ + c_ * (y_ - x_)) + y_ + c_ * (x_ - y_)

    mate = {"tab": t + 1 - 2 * c}
    barrier = pltpu.get_barrier_semaphore()

    def hello(i, _):
        pl.semaphore_signal(barrier, inc=1, device_id={"tab": lax.rem(t + i, TAB)}, device_id_type=pl.DeviceIdType.MESH)
        return 0

    lax.fori_loop(1, TAB, hello, 0)
    for d in range(1, REP):
        pl.semaphore_signal(barrier, inc=1, device_id={"rep": lax.rem(r + d, REP)}, device_id_type=pl.DeviceIdType.MESH)

    pairs = (
        (proj_hbm, projs), (labels_hbm, labels_ref), (bil_hbm, bil_ref), (sin_hbm, sin_ref), (sout_hbm, sout_ref),
        (w2_hbm, w2_ref), (wl_hbm, wl_ref), (w1_hbm, w1), (place_hbm, place_vec),
    )
    loads = [pltpu.make_async_copy(src, dst, load_sem.at[i]) for i, (src, dst) in enumerate(pairs)]
    part = xs.shape[1] // PARTS
    for k in range(PARTS):
        piece = pl.ds(k * part, part)
        loads.append(pltpu.make_async_copy(pooled_hbm.at[:, piece], xs.at[:, piece], load_sem.at[len(pairs) + k]))
    for k in [8, 0] + list(range(len(pairs), len(pairs) + PARTS)) + list(range(1, 8)):
        loads[k].start()

    loads[8].wait()
    line = place_vec[...].reshape(1, FIELDS)
    eye = iota((FIELDS, FIELDS), 0) == iota((FIELDS, FIELDS), 1)
    column = jnp.sum(jnp.where(eye, line, 0), axis=1, keepdims=True)
    spots = iota((FIELDS, FIELDS), 0)
    slot_of = jnp.sum(jnp.where(column == iota((FIELDS, FIELDS), 1), spots, 0), axis=0, keepdims=True)
    inv_vec[...] = jnp.minimum(slot_of, FIELDS - 1)
    invert = pltpu.make_async_copy(inv_vec, inv_ref, load_sem.at[9 + PARTS])
    invert.start()

    loads[0].wait()
    keep = []
    for i in range(2):
        field = place_ref[2 * t + i]
        keep.append(iota((E, LANES), 1) < width_ref[field])
        pt_ref[i * E : (i + 1) * E, :] = jnp.where(keep[i], projs[field].astype(F32), 0.0).astype(BF)
    for k in range(PARTS):
        loads[len(pairs) + k].wait()
        for i in range(2):
            out = mm(pt_ref[i * E : (i + 1) * E, :], xs[i, k * part : (k + 1) * part, :], NT).astype(BF)
            for d in range(part // LANES):
                e_ref[k * (part // LANES) + d, i] = out[:, d * LANES : (d + 1) * LANES]

    small_rows = (lax.rem(iota((HID, E), 0), E) == iota((HID, E), 1)).astype(BF)
    loads[1].wait()
    loads[2].wait()
    small_cols = (lax.rem(iota((E, HID), 1), E) == iota((E, HID), 0)).astype(BF)
    diag = (iota((HID, HID), 0) // E) == (iota((HID, HID), 1) // E)
    bil = bil_ref[...].astype(BF)
    tall = mm(small_rows, bil, NN).astype(BF)
    tall_t = mm(small_rows, bil, NT).astype(BF)
    kron = jnp.where(diag, mm(tall, small_cols, NN), 0.0).astype(BF)
    kron_t = jnp.where(diag, mm(tall_t, small_cols, NN), 0.0).astype(BF)
    square = iota((LANES, LANES), 0) == iota((LANES, LANES), 1)
    label_row = labels_ref[:, pl.ds(pl.multiple_of(t * LANES, LANES), LANES)].astype(F32)
    target = jnp.sum(jnp.where(square, label_row, 0.0), axis=1, keepdims=True)

    pl.semaphore_wait(barrier, TAB - 1 + REP - 1)

    def pair(p):
        return pl.ds(p * 2, 2)

    def e_send(i, _):
        p = lax.rem(t + i, TAB)
        send(e_ref.at[p], recv.at[pair(t)], es.at[p], er.at[t], {"tab": p})
        return 0

    lax.fori_loop(1, TAB, e_send, 0)
    recv[pair(t)] = e_ref[t]

    def e_wait(i, _):
        p = lax.rem(t + i, TAB)
        got(recv.at[pair(p)], es.at[p], er.at[p], {"tab": p})
        return 0

    lax.fori_loop(1, TAB, e_wait, 0)

    def rows32(f):
        return pl.ds(pl.multiple_of(f * E, E), E)

    invert.wait()

    def by_field(f, _):
        emb[rows32(f), :] = recv[inv_ref[0, f]]
        return 0

    lax.fori_loop(0, FIELDS, by_field, 0, unroll=16)

    groups = FIELDS // 8

    def rows256(g):
        return pl.ds(pl.multiple_of(g * HID, HID), HID)

    def rows8(g):
        return pl.ds(pl.multiple_of(g * 8, 8), 8)

    def cube(v):
        return v.reshape(8, E, LANES)

    def flat(v):
        return v.reshape(HID, LANES)

    def first_pass(g, total):
        u = cube(emb[rows256(g), :].astype(F32))
        sq[rows8(g), :] = jnp.sum(u, axis=1) * (1.0 / E)
        return total + jnp.sum(u, axis=0)

    zero = jnp.zeros((E, LANES), F32)
    total = lax.fori_loop(0, groups, first_pass, zero, unroll=8)
    squeeze = sq[...]
    loads[3].wait()
    loads[4].wait()
    pre_one = mm(sin_ref[...], squeeze, NN, HI)
    act_one = pre_one * jax.nn.sigmoid(pre_one)
    weights = jax.nn.sigmoid(mm(sout_ref[...], act_one, TN, HI))
    wts[...] = weights

    def scaled_of(g):
        u = cube(emb[rows256(g), :].astype(F32))
        return u, u * wts[rows8(g), :][:, None, :]

    def second_pass(g, tot):
        return tot + jnp.sum(scaled_of(g)[1], axis=0)

    total_s = lax.fori_loop(0, groups, second_pass, zero, unroll=8)

    for k in range(5, 8):
        loads[k].wait()

    def third_pass(g, acc):
        u, sc = scaled_of(g)
        for k, (v, vb, tot) in enumerate(((u, emb[rows256(g), :], total), (sc, flat(sc).astype(BF), total_s))):
            p = mm(kron_t, vb, NN)
            prod[k, rows256(g), :] = p
            j = flat(cube(p) * (tot[None] - v) * FACTOR).astype(BF)
            chip = k * groups + g
            js[chip] = j[:LANES]
            js[16 + lax.rem(chip, SIDE) * SIDE + chip // SIDE] = j[LANES:]
            acc = acc + mm(j, w1[rows256(k * groups + g), :], TN)
        return acc

    pre_hidden = lax.fori_loop(0, groups, third_pass, jnp.zeros((LANES, HID), F32), unroll=8)
    half = pl.ds((1 - c) * 16, 16)
    send(js.at[half], jp, ps.at[0], pr.at[0], mate)

    h1 = (pre_hidden * jax.nn.sigmoid(pre_hidden)).astype(BF)
    pre_second = mm(h1, w2_ref[...], NN)
    h2 = (pre_second * jax.nn.sigmoid(pre_second)).astype(BF).astype(F32)
    wl = wl_ref[...].reshape(1, HID).astype(F32)
    logit = jnp.sum(h2 * wl, axis=1, keepdims=True)
    lg_ref[t] = jnp.sum(jnp.where(square, logit, 0.0), axis=0, keepdims=True)

    def l_send(i, _):
        p = lax.rem(t + i, TAB)
        send(lg_ref.at[t], lg_ref.at[t], ls.at[p], lr.at[t], {"tab": p})
        return 0

    lax.fori_loop(1, TAB, l_send, 0)
    grad = jax.nn.sigmoid(logit) - target
    d_last = jnp.sum(grad * h2, axis=0, keepdims=True)
    dp2 = (grad * wl * slope(pre_second)).astype(BF)
    d_second = mm(h1, dp2, TN).astype(BF)
    for i in range(16):
        for h in range(2):
            d2[2 * i + h] = d_second[16 * i : 16 * i + 16, LANES * h : LANES * h + LANES]
    dp1 = (mm(dp2, w2_ref[...], NT) * slope(pre_hidden)).astype(BF)
    dpb[0] = dp1
    send(dpb.at[0], dpb.at[1], ps.at[1], pr.at[1], mate)
    send(d2.at[half], d2p, ps.at[2], pr.at[2], mate)

    def side(v):
        return jnp.concatenate([v[i * E : (i + 1) * E] for i in range(8)], axis=1)

    def fourth_pass(g, sums):
        u, sc = scaled_of(g)
        out = []
        bil_sum = sums[2]
        for k, (v, vb, tot) in enumerate(((u, emb[rows256(g), :], total), (sc, flat(sc).astype(BF), total_s))):
            up = cube(mm(w1[rows256(k * groups + g), :], dp1, NT)) * FACTOR
            dq = up * cube(prod[k, rows256(g), :])
            dp = flat(up * (tot[None] - v)).astype(BF)
            du[k, rows256(g), :] = mm(kron, dp, NN) - flat(dq)
            bil_sum = bil_sum + mm(side(vb), side(dp), NT)
            out.append(sums[k] + jnp.sum(dq, axis=0))
        return (*out, bil_sum)

    sums = lax.fori_loop(0, EARLY, fourth_pass, (zero, zero, jnp.zeros((E, E), F32)), unroll=4)

    def peer(me, d):
        return lax.rem(me + d, SIDE)

    got(jp, ps.at[0], pr.at[0], mate)
    got(dpb.at[1], ps.at[1], pr.at[1], mate)
    got(d2p, ps.at[2], pr.at[2], mate)
    d2b[...] = (d2[pl.ds(c * 16, 16)].astype(F32) + d2p[...].astype(F32)).astype(BF).reshape(d2b.shape)
    for d in range(1, SIDE):
        i = peer(a, d)
        send(d2b.at[i], rd1.at[a], s1d.at[d], q1d.at[a], {"tab": at(i, b)})

    both = dpb[...].reshape(2 * LANES, HID)

    def d_first_row(i):
        left = jnp.concatenate(
            [js[pl.ds(16 * c + i * SIDE, SIDE)].reshape(SIDE * LANES, LANES), jp[pl.ds(i * SIDE, SIDE)].reshape(SIDE * LANES, LANES)],
            axis=1,
        )
        out = mm(left, both, NN).astype(BF)
        for k in range(SIDE):
            dfb[i, k, 0:LANES] = out[k * LANES : (k + 1) * LANES, :LANES]
            dfb[i, k, LANES:] = out[k * LANES : (k + 1) * LANES, LANES:]

    for d in range(1, SIDE):
        i = peer(a, d)
        d_first_row(i)
        send(dfb.at[i], r1.at[a], s1.at[d], q1.at[a], {"tab": at(i, b)})
    d_first_row(a)

    for d in range(1, SIDE):
        i = peer(a, d)
        got(rd1.at[i], s1d.at[d], q1d.at[i], {"tab": at(i, b)})
    out = d2b[a].astype(F32)
    for d in range(1, SIDE):
        out = out + rd1[peer(a, d)].astype(F32)
    d2b[a] = out.astype(BF)
    for d in range(1, SIDE):
        k = peer(b, d)
        send(d2b.at[a, k], rd2.at[b], s2d.at[d], q2d.at[b], {"tab": at(a, k)})

    sum_q, sum_qs, d_bil = lax.fori_loop(EARLY, groups, fourth_pass, sums, unroll=4)

    for d in range(1, SIDE):
        k = peer(b, d)
        got(rd2.at[k], s2d.at[d], q2d.at[k], {"tab": at(a, k)})
    out = d2b[a, b].astype(F32)
    for d in range(1, SIDE):
        out = out + rd2[peer(b, d)].astype(F32)
    rdz[r] = out.astype(BF)
    for d in range(1, REP):
        send(rdz.at[r], rdz.at[r], szd.at[d], qzd.at[r], {"rep": peer(r, d)})

    def fifth_pass(g, _):
        u = cube(emb[rows256(g), :].astype(F32))
        w = wts[rows8(g), :]
        d_w = jnp.sum((cube(du[1, rows256(g), :]) + sum_qs[None]) * u, axis=1)
        dpw[rows8(g), :] = d_w * w * (1.0 - w)
        return 0

    lax.fori_loop(0, groups, fifth_pass, 0, unroll=8)
    d_pre_w = dpw[...]
    d_act = mm(sout_ref[...], d_pre_w, NN, HI) * slope(pre_one)
    dsq[...] = mm(sin_ref[...], d_act, TN, HI) * (1.0 / E)

    def sixth_pass(g, _):
        w = wts[rows8(g), :][:, None, :]
        out = cube(du[0, rows256(g), :]) + sum_q[None] + w * (cube(du[1, rows256(g), :]) + sum_qs[None])
        out = out + dsq[rows8(g), :][:, None, :]
        demb[rows8(g)] = out.astype(BF)
        return 0

    lax.fori_loop(0, groups, sixth_pass, 0, unroll=8)

    def by_slot(s, _):
        dslot[s] = demb[place_ref[s]]
        return 0

    lax.fori_loop(0, FIELDS, by_slot, 0, unroll=16)

    def d_send(i, _):
        p = lax.rem(t + i, TAB)
        send(dslot.at[pair(p)], rd_ref.at[pair(t)], ds.at[p], dr.at[t], {"tab": p})
        return 0

    lax.fori_loop(1, TAB, d_send, 0)
    rd_ref[pair(t)] = dslot[pair(t)]

    d_in = mm(d_act, squeeze, NT, HI)
    d_out = mm(act_one, d_pre_w, NT, HI)
    sr[0, c, 0:E] = jnp.concatenate([d_in, d_out], axis=1).astype(BF)
    sr[0, c, E : 2 * E] = jnp.zeros((E, LANES), BF)
    sr[0, c, E : 2 * E, 0:E] = d_bil.astype(BF)
    low = iota((16, LANES), 0)
    last = jnp.where(low == 0, d_last[:, :LANES], jnp.where(low == 1, d_last[:, LANES:], 0.0))
    sr[0, c, 2 * E : SMALL] = last.astype(BF)

    def peers(phase):
        if phase == 0:
            return c, [(1 - c, mate)]
        if phase == 1:
            return a, [(lax.rem(a + d, SIDE), {"tab": at(lax.rem(a + d, SIDE), b)}) for d in range(1, SIDE)]
        if phase == 2:
            return b, [(lax.rem(b + d, SIDE), {"tab": at(a, lax.rem(b + d, SIDE))}) for d in range(1, SIDE)]
        return r, [(lax.rem(r + d, REP), {"rep": lax.rem(r + d, REP)}) for d in range(1, REP)]

    def small_start(phase):
        me, others = peers(phase)
        for d, (_, dev) in enumerate(others):
            send(sr.at[phase, me], sr.at[phase, me], ss.at[phase, d], sq_r.at[phase, me], dev)

    def small_end(phase):
        me, others = peers(phase)
        for d, (who, dev) in enumerate(others):
            got(sr.at[phase, who], ss.at[phase, d], sq_r.at[phase, who], dev)
        size = 2 if phase == 0 else 4
        out = sr[phase, 0].astype(F32)
        for k in range(1, size):
            out = out + sr[phase, k].astype(F32)
        return out

    small_start(0)

    for d in range(1, REP):
        got(rdz.at[peer(r, d)], szd.at[d], qzd.at[peer(r, d)], {"rep": peer(r, d)})
    out = rdz[0].astype(F32)
    for k in range(1, REP):
        out = out + rdz[k].astype(F32)
    mine = block_of(t)
    ag_ref[mine] = out.astype(BF)

    def g_send(i, _):
        p = lax.rem(t + i, TAB)
        send(ag_ref.at[mine], ag_ref.at[mine], gs.at[p], gr.at[t], {"tab": p})
        return 0

    lax.fori_loop(1, TAB, g_send, 0)

    for d in range(1, SIDE):
        i = lax.rem(a + d, SIDE)
        got(r1.at[i], s1.at[d], q1.at[i], {"tab": at(i, b)})

    def first_sum(k, _):
        out = dfb[a, k].astype(F32)
        for d in range(1, SIDE):
            out = out + r1[lax.rem(a + d, SIDE), k].astype(F32)
        dfb[a, k] = out.astype(BF)
        return 0

    for d in range(1, SIDE):
        k = lax.rem(b + d, SIDE)
        first_sum(k, 0)
        send(dfb.at[a, k], r2.at[b], s2.at[d], q2.at[b], {"tab": at(a, k)})
    first_sum(b, 0)

    sr[1, a] = small_end(0).astype(BF)
    small_start(1)


    def d_wait(i, _):
        p = lax.rem(t + i, TAB)
        got(rd_ref.at[pair(p)], ds.at[p], dr.at[p], {"tab": p})
        return 0

    lax.fori_loop(1, TAB, d_wait, 0)

    def proj_pass(j, acc):
        left = jnp.concatenate([rd_ref[pair(2 * j)].reshape(2 * E, LANES), rd_ref[pair(2 * j + 1)].reshape(2 * E, LANES)], axis=1)
        right = jnp.concatenate([xs[0, rows256(j), :], xs[1, rows256(j), :]], axis=1)
        return acc + mm(left, right, NN)

    acc = lax.fori_loop(0, TAB // 2, proj_pass, jnp.zeros((2 * E, 2 * LANES), F32), unroll=8)
    dz[r] = jnp.concatenate([acc[:E, :LANES], acc[E:, LANES:]], axis=0).astype(BF)
    for d in range(1, REP):
        o = lax.rem(r + d, REP)
        send(dz.at[r], dz.at[r], sd.at[d], qd.at[r], {"rep": o})

    sr[2, b] = small_end(1).astype(BF)
    small_start(2)

    for d in range(1, SIDE):
        k = lax.rem(b + d, SIDE)
        got(r2.at[k], s2.at[d], q2.at[k], {"tab": at(a, k)})
    out = dfb[a, b].astype(F32)
    for d in range(1, SIDE):
        out = out + r2[lax.rem(b + d, SIDE)].astype(F32)
    rz[r] = out.astype(BF)
    for d in range(1, REP):
        o = lax.rem(r + d, REP)
        send(rz.at[r], rz.at[r], sz.at[d], qz.at[r], {"rep": o})

    sr[3, r] = small_end(2).astype(BF)
    small_start(3)

    for d in range(1, REP):
        o = lax.rem(r + d, REP)
        got(rz.at[o], sz.at[d], qz.at[o], {"rep": o})
    out = rz[0].astype(F32)
    for k in range(1, REP):
        out = out + rz[k].astype(F32)
    df_ref[...] = out

    for d in range(1, REP):
        o = lax.rem(r + d, REP)
        got(dz.at[o], sd.at[d], qd.at[o], {"rep": o})
    out = dz[0].astype(F32)
    for k in range(1, REP):
        out = out + dz[k].astype(F32)
    for i in range(2):
        dpt_ref[i] = jnp.where(keep[i], out[i * E : (i + 1) * E], 0.0)
    smf_ref[...] = small_end(3)

    def last_wait(i, _):
        p = lax.rem(t + i, TAB)
        dev = {"tab": p}
        got(lg_ref.at[p], ls.at[p], lr.at[p], dev)
        got(ag_ref.at[block_of(p)], gs.at[p], gr.at[p], dev)
        sent(e_ref.at[p], es.at[p], er.at[p], dev)
        sent(dslot.at[pair(p)], ds.at[p], dr.at[p], dev)
        sent(lg_ref.at[t], ls.at[p], lr.at[p], dev)
        sent(ag_ref.at[mine], gs.at[p], gr.at[p], dev)
        return 0

    lax.fori_loop(1, TAB, last_wait, 0)
    sent(js.at[half], ps.at[0], pr.at[0], mate)
    sent(dpb.at[0], ps.at[1], pr.at[1], mate)
    sent(d2.at[half], ps.at[2], pr.at[2], mate)
    for d in range(1, SIDE):
        i = lax.rem(a + d, SIDE)
        k = lax.rem(b + d, SIDE)
        o = lax.rem(r + d, REP)
        sent(dfb.at[i], s1.at[d], q1.at[i], {"tab": at(i, b)})
        sent(dfb.at[a, k], s2.at[d], q2.at[k], {"tab": at(a, k)})
        sent(rz.at[r], sz.at[d], qz.at[r], {"rep": o})
        sent(d2b.at[i], s1d.at[d], q1d.at[i], {"tab": at(i, b)})
        sent(d2b.at[a, k], s2d.at[d], q2d.at[k], {"tab": at(a, k)})
        sent(rdz.at[r], szd.at[d], qzd.at[r], {"rep": o})
        sent(dz.at[r], sd.at[d], qd.at[r], {"rep": o})
    for phase in range(4):
        me, others = peers(phase)
        for d, (_, dev) in enumerate(others):
            sent(sr.at[phase, me], ss.at[phase, d], sq_r.at[phase, me], dev)


def exchange(placement, widths, labels, proj, sin, sout, bil, w1, w2, wl, pooled):
    vmem = pl.BlockSpec(memory_space=pltpu.VMEM)
    smem = pl.BlockSpec(memory_space=pltpu.SMEM)
    hbm = pl.BlockSpec(memory_space=pltpu.HBM)
    rows = FIELDS * E
    dma = pltpu.SemaphoreType.DMA
    arrays = (placement, labels, proj, sin, sout, bil, w1, w2, wl, pooled)
    return pl.pallas_call(
        main_kernel,
        in_specs=[smem] * 2 + [hbm] * len(arrays),
        out_specs=[vmem] * 7,
        out_shape=[
            jax.ShapeDtypeStruct((FIELDS, E, LANES), BF),
            jax.ShapeDtypeStruct((TAB, 1, LANES), F32),
            jax.ShapeDtypeStruct((BLOCK, LANES), F32),
            jax.ShapeDtypeStruct((TAB, 16, LANES), BF),
            jax.ShapeDtypeStruct((SMALL, LANES), F32),
            jax.ShapeDtypeStruct((2, E, LANES), F32),
            jax.ShapeDtypeStruct((2 * E, LANES), BF),
        ],
        scratch_shapes=[pltpu.VMEM(v.shape, v.dtype) for v in arrays]
        + [
            pltpu.VMEM((TAB, 2, E, LANES), BF),
            pltpu.VMEM((FIELDS, E, LANES), BF),
            pltpu.VMEM((rows, LANES), BF),
            pltpu.VMEM((2, rows, LANES), F32),
            pltpu.VMEM((2, rows, LANES), F32),
            pltpu.VMEM((FIELDS, LANES), F32),
            pltpu.VMEM((FIELDS, LANES), F32),
            pltpu.VMEM((FIELDS, LANES), F32),
            pltpu.VMEM((FIELDS, LANES), F32),
            pltpu.VMEM((TAB, LANES, LANES), BF),
            pltpu.VMEM((16, LANES, LANES), BF),
            pltpu.VMEM((2, LANES, HID), BF),
            pltpu.VMEM((TAB, 16, LANES), BF),
            pltpu.VMEM((16, 16, LANES), BF),
            pltpu.VMEM((FIELDS, E, LANES), BF),
            pltpu.VMEM((FIELDS, E, LANES), BF),
            pltpu.VMEM((SIDE, SIDE, BLOCK, LANES), BF),
            pltpu.VMEM((SIDE, SIDE, BLOCK, LANES), BF),
            pltpu.VMEM((SIDE, BLOCK, LANES), BF),
            pltpu.VMEM((REP, BLOCK, LANES), BF),
            pltpu.VMEM((4, 4, SMALL, LANES), BF),
            pltpu.VMEM((REP, 2 * E, LANES), BF),
            pltpu.VMEM((SIDE, SIDE, 16, LANES), BF),
            pltpu.VMEM((SIDE, SIDE, 16, LANES), BF),
            pltpu.VMEM((SIDE, 16, LANES), BF),
            pltpu.VMEM((REP, 16, LANES), BF),
            pltpu.VMEM((1, FIELDS), jnp.int32),
            pltpu.SMEM((1, FIELDS), jnp.int32),
            dma((10 + PARTS,)),
        ]
        + [dma((TAB,))] * 8
        + [dma((3,))] * 2
        + [dma((4,))] * 6
        + [dma((4, 4))] * 2
        + [dma((4,))] * 8,
        compiler_params=pltpu.CompilerParams(
            collective_id=0, has_side_effects=True, vmem_limit_bytes=60 * 1024 * 1024
        ),
        name="exchange",
    )(placement, widths, *arrays)


def finish_kernel(
    tab_ref, rd_hbm, pt_hbm, lg_hbm, df_hbm, ag_hbm, smf_hbm, dpt_hbm, route_hbm,
    scores_ref, dx_hbm, dproj_ref, din_ref, dout_ref, dbil_ref, dfirst_ref, dsecond_ref, dlast_ref,
    rd_ref, pt_ref, lg_ref, df_ref, ag_ref, smf_ref, route_ref, dx, load_sem, out_sem,
):
    pairs = (
        (rd_hbm, rd_ref), (pt_hbm, pt_ref), (lg_hbm, lg_ref), (route_hbm, route_ref), (smf_hbm, smf_ref),
        (df_hbm, df_ref), (ag_hbm, ag_ref), (dpt_hbm, dproj_ref),
    )
    loads = [pltpu.make_async_copy(src, dst, load_sem.at[i]) for i, (src, dst) in enumerate(pairs)]
    for k in (1, 0, 2, 3, 4, 5, 6, 7):
        loads[k].start()
    loads[1].wait()
    pt = pt_ref[...]
    nil = jnp.zeros((E, LANES), BF)
    wide = jnp.concatenate(
        [jnp.concatenate([pt[:E], nil], axis=1), jnp.concatenate([nil, pt[E:]], axis=1)], axis=0
    )
    loads[0].wait()
    part = dx.shape[1] // PARTS
    writes = []
    for p in range(PARTS):
        for k in range(p * (TAB // PARTS), (p + 1) * (TAB // PARTS)):
            out = mm(rd_ref[2 * k : 2 * k + 2].reshape(2 * E, LANES), wide, TN).astype(BF)
            dx[0, k * LANES : (k + 1) * LANES] = out[:, :LANES]
            dx[1, k * LANES : (k + 1) * LANES] = out[:, LANES:]
        piece = pl.ds(p * part, part)
        writes.append(pltpu.make_async_copy(dx.at[:, piece], dx_hbm.at[:, piece], out_sem.at[p]))
        writes[p].start()

    for k in range(2, len(pairs)):
        loads[k].wait()
    idx = route_ref[:, pl.ds(pl.multiple_of(tab_ref[0] * LANES, LANES), LANES)]
    table = lg_ref[...].reshape(TAB, LANES)
    low = jnp.broadcast_to(lax.rem(idx, LANES), (TAB, LANES))
    found = jnp.take_along_axis(table, low, axis=1)
    scores_ref[...] = jnp.sum(
        jnp.where(idx // LANES == iota((TAB, LANES), 0), found, 0.0), axis=0, keepdims=True
    )
    din_ref[...] = smf_ref[0:E, 0:FIELDS]
    dout_ref[...] = smf_ref[0:E, FIELDS:]
    dbil_ref[...] = smf_ref[E : 2 * E, 0:E]
    dlast_ref[:, 0:LANES] = smf_ref[2 * E : 2 * E + 1, :]
    dlast_ref[:, LANES:] = smf_ref[2 * E + 1 : 2 * E + 2, :]
    dfirst_ref[:, 0:LANES] = df_ref[0:LANES, :]
    dfirst_ref[:, LANES:] = df_ref[LANES : 2 * LANES, :]
    for i in range(16):
        dsecond_ref[16 * i : 16 * i + 16, 0:LANES] = ag_ref[2 * i].astype(F32)
        dsecond_ref[16 * i : 16 * i + 16, LANES:] = ag_ref[2 * i + 1].astype(F32)
    for w in writes:
        w.wait()


def finish(tab, rd, pt, lg, df, ag, smf, dpt, route, pooled_shape):
    vmem = pl.BlockSpec(memory_space=pltpu.VMEM)
    smem = pl.BlockSpec(memory_space=pltpu.SMEM)
    hbm = pl.BlockSpec(memory_space=pltpu.HBM)
    arrays = (rd, pt, lg, df, ag, smf, dpt, route)
    outs = [
        ((1, LANES), F32), (pooled_shape, BF), ((2, E, LANES), F32), ((E, FIELDS), F32), ((E, FIELDS), F32),
        ((E, E), F32), ((LANES, HID), F32), ((HID, HID), F32), ((1, HID), F32),
    ]
    return pl.pallas_call(
        finish_kernel,
        in_specs=[smem] + [hbm] * len(arrays),
        out_specs=[vmem, hbm] + [vmem] * 7,
        out_shape=[jax.ShapeDtypeStruct(s, d) for s, d in outs],
        scratch_shapes=[pltpu.VMEM(v.shape, v.dtype) for v in (rd, pt, lg, df, ag, smf, route)]
        + [
            pltpu.VMEM(pooled_shape, BF),
            pltpu.SemaphoreType.DMA((len(arrays),)),
            pltpu.SemaphoreType.DMA((PARTS,)),
        ],
        compiler_params=pltpu.CompilerParams(vmem_limit_bytes=60 * 1024 * 1024),
        name="finish",
    )(tab, *arrays)


def shards(pooled, widths, placement, route, labels, proj, senet_in, senet_out, bilinear, w_first, w_second, w_last):
    tab = lax.axis_index("tab").astype(jnp.int32).reshape(1)
    rd, lg, df, ag, smf, dpt, pt = exchange(
        placement, widths, labels, jnp.swapaxes(proj, 1, 2), senet_in.T, senet_out, bilinear, w_first, w_second,
        w_last, pooled,
    )
    scores, dx, dproj, din, dout, dbil, dfirst, dsecond, dlast = finish(
        tab, rd, pt, lg, df, ag, smf, dpt, route, pooled.shape
    )
    return scores, dx, jnp.swapaxes(dproj, 1, 2), din.T, dout, dbil, dfirst, dsecond, dlast[0]


def solution(mesh):
    whole = P()
    placed = (
        P("tab", "rep", None), whole, whole, P("rep", None), P("rep", None), whole, whole, whole, whole, whole,
        whole, whole,
    )
    return jax.shard_map(
        shards,
        mesh=mesh,
        in_specs=placed,
        out_specs=(
            P("rep", "tab"), P("tab", "rep", None), P("tab", None, None), whole, whole, whole, P("tab", None),
            whole, whole,
        ),
        check_vma=False,
    )
```

```python
import functools

import jax
import jax.numpy as jnp
from jax import lax
from jax.experimental import pallas as pl
from jax.experimental.pallas import tpu as pltpu
from jax.sharding import PartitionSpec as P

F32 = jnp.float32
BF = jnp.bfloat16
HI = lax.Precision.HIGHEST
NN = (((1,), (0,)), ((), ()))
NT = (((1,), (1,)), ((), ()))
TN = (((0,), (0,)), ((), ()))

FIELDS = 64
E = 32
TAB = 32
REP = 4
EARLY = 4
SIDE = 4
PARTS = 4
LANES = 128
HID = 256
BLOCK = 256
SMALL = 80
FACTOR = 0.125


def mm(a, b, dims, precision=None):
    return lax.dot_general(a, b, dims, precision=precision, preferred_element_type=F32)


def slope(u):
    s = jax.nn.sigmoid(u)
    return s * (1.0 + u * (1.0 - s))


def iota(shape, dim):
    return lax.broadcasted_iota(jnp.int32, shape, dim)


def send(src, dst, ssem, rsem, dev):
    pltpu.make_async_remote_copy(
        src_ref=src, dst_ref=dst, send_sem=ssem, recv_sem=rsem, device_id=dev,
        device_id_type=pl.DeviceIdType.MESH,
    ).start()


def got(dst, ssem, rsem, dev):
    pltpu.make_async_remote_copy(
        src_ref=dst, dst_ref=dst, send_sem=ssem, recv_sem=rsem, device_id=dev,
        device_id_type=pl.DeviceIdType.MESH,
    ).wait_recv()


def sent(src, ssem, rsem, dev):
    pltpu.make_async_remote_copy(
        src_ref=src, dst_ref=src, send_sem=ssem, recv_sem=rsem, device_id=dev,
        device_id_type=pl.DeviceIdType.MESH,
    ).wait_send()


def main_kernel(
    place_ref, width_ref, place_hbm, labels_hbm, proj_hbm, sin_hbm, sout_hbm, bil_hbm, w1_hbm, w2_hbm, wl_hbm, pooled_hbm,
    dx_hbm, lg_ref, df_ref, ag_ref, smf_ref, dpt_ref,
    rd_ref, pt_ref,
    place_vec, labels_ref, projs, sin_ref, sout_ref, bil_ref, w1, w2_ref, wl_ref, xs, e_ref, recv, emb, prod, du, sq, wts, dpw, dsq, js, jp, dpb, d2, d2p, demb, dslot, dfb, r1, r2, rz, sr, dz, d2b, rd1, rd2, rdz, inv_vec, inv_ref,
    load_sem, es, er, ds, dr, ls, lr, gs, gr, ps, pr, s1, q1, s2, q2, sz, qz, ss, sq_r, sd, qd, s1d, q1d, s2d, q2d, szd, qzd, out_sem,
):
    t = lax.axis_index("tab")
    r = lax.axis_index("rep")
    c = lax.rem(t, 2)
    n = t // 2
    x = n // SIDE
    y = lax.rem(n, SIDE)
    a = x + c * (y - x)
    b = y + c * (x - y)

    def at(a_, b_):
        return ((a_ + c * (b_ - a_)) * SIDE + (b_ + c * (a_ - b_))) * 2 + c

    def block_of(tab):
        c_ = lax.rem(tab, 2)
        n_ = tab // 2
        x_ = n_ // SIDE
        y_ = lax.rem(n_, SIDE)
        return 16 * c_ + SIDE * (x_ + c_ * (y_ - x_)) + y_ + c_ * (x_ - y_)

    mate = {"tab": t + 1 - 2 * c}
    barrier = pltpu.get_barrier_semaphore()

    def away(v):
        return min(v, SIDE - v)

    hops = sorted(
        ((dx, dy, dc) for dx in range(SIDE) for dy in range(SIDE) for dc in range(2) if dx or dy or dc),
        key=lambda h: -(away(h[0]) + away(h[1])),
    )
    others = [
        (lax.rem(x + dx, SIDE) * SIDE + lax.rem(y + dy, SIDE)) * 2 + lax.rem(c + dc, 2) for dx, dy, dc in hops
    ]

    for d in (2, 1, 3):
        pl.semaphore_signal(barrier, inc=1, device_id={"rep": lax.rem(r + d, REP)}, device_id_type=pl.DeviceIdType.MESH)
    for p in others:
        pl.semaphore_signal(barrier, inc=1, device_id={"tab": p}, device_id_type=pl.DeviceIdType.MESH)

    pairs = (
        (proj_hbm, projs), (labels_hbm, labels_ref), (bil_hbm, bil_ref), (sin_hbm, sin_ref), (sout_hbm, sout_ref),
        (w2_hbm, w2_ref), (wl_hbm, wl_ref), (w1_hbm, w1), (place_hbm, place_vec),
    )
    loads = [pltpu.make_async_copy(src, dst, load_sem.at[i]) for i, (src, dst) in enumerate(pairs)]
    part = xs.shape[1] // PARTS
    for k in range(PARTS):
        piece = pl.ds(k * part, part)
        loads.append(pltpu.make_async_copy(pooled_hbm.at[:, piece], xs.at[:, piece], load_sem.at[len(pairs) + k]))
    for k in [8, 0] + list(range(len(pairs), len(pairs) + PARTS)) + list(range(1, 8)):
        loads[k].start()

    loads[8].wait()
    line = place_vec[...].reshape(1, FIELDS)
    eye = iota((FIELDS, FIELDS), 0) == iota((FIELDS, FIELDS), 1)
    column = jnp.sum(jnp.where(eye, line, 0), axis=1, keepdims=True)
    spots = iota((FIELDS, FIELDS), 0)
    slot_of = jnp.sum(jnp.where(column == iota((FIELDS, FIELDS), 1), spots, 0), axis=0, keepdims=True)
    inv_vec[...] = jnp.minimum(slot_of, FIELDS - 1)
    invert = pltpu.make_async_copy(inv_vec, inv_ref, load_sem.at[9 + PARTS])
    invert.start()

    loads[0].wait()
    keep = []
    for i in range(2):
        field = place_ref[2 * t + i]
        keep.append(iota((E, LANES), 1) < width_ref[field])
        pt_ref[i * E : (i + 1) * E, :] = jnp.where(keep[i], projs[field].astype(F32), 0.0).astype(BF)
    for k in range(PARTS):
        loads[len(pairs) + k].wait()
        for i in range(2):
            out = mm(pt_ref[i * E : (i + 1) * E, :], xs[i, k * part : (k + 1) * part, :], NT).astype(BF)
            for d in range(part // LANES):
                e_ref[k * (part // LANES) + d, i] = out[:, d * LANES : (d + 1) * LANES]

    small_rows = (lax.rem(iota((HID, E), 0), E) == iota((HID, E), 1)).astype(BF)
    loads[1].wait()
    loads[2].wait()
    small_cols = (lax.rem(iota((E, HID), 1), E) == iota((E, HID), 0)).astype(BF)
    diag = (iota((HID, HID), 0) // E) == (iota((HID, HID), 1) // E)
    bil = bil_ref[...].astype(BF)
    tall = mm(small_rows, bil, NN).astype(BF)
    tall_t = mm(small_rows, bil, NT).astype(BF)
    kron = jnp.where(diag, mm(tall, small_cols, NN), 0.0).astype(BF)
    kron_t = jnp.where(diag, mm(tall_t, small_cols, NN), 0.0).astype(BF)
    square = iota((LANES, LANES), 0) == iota((LANES, LANES), 1)
    label_row = labels_ref[:, pl.ds(pl.multiple_of(t * LANES, LANES), LANES)].astype(F32)
    target = jnp.sum(jnp.where(square, label_row, 0.0), axis=1, keepdims=True)

    pl.semaphore_wait(barrier, TAB - 1 + REP - 1)

    def pair(p):
        return pl.ds(p * 2, 2)

    for p in others:
        send(e_ref.at[p], recv.at[pair(t)], es.at[p], er.at[t], {"tab": p})
    recv[pair(t)] = e_ref[t]

    def e_wait(i, _):
        p = lax.rem(t + i, TAB)
        got(recv.at[pair(p)], es.at[p], er.at[p], {"tab": p})
        return 0

    lax.fori_loop(1, TAB, e_wait, 0)

    def rows32(f):
        return pl.ds(pl.multiple_of(f * E, E), E)

    invert.wait()

    def by_field(f, _):
        emb[rows32(f), :] = recv[inv_ref[0, f]]
        return 0

    lax.fori_loop(0, FIELDS, by_field, 0, unroll=16)

    groups = FIELDS // 8

    def rows256(g):
        return pl.ds(pl.multiple_of(g * HID, HID), HID)

    def rows8(g):
        return pl.ds(pl.multiple_of(g * 8, 8), 8)

    def cube(v):
        return v.reshape(8, E, LANES)

    def flat(v):
        return v.reshape(HID, LANES)

    def first_pass(g, total):
        u = cube(emb[rows256(g), :].astype(F32))
        sq[rows8(g), :] = jnp.sum(u, axis=1) * (1.0 / E)
        return total + jnp.sum(u, axis=0)

    zero = jnp.zeros((E, LANES), F32)
    total = lax.fori_loop(0, groups, first_pass, zero, unroll=8)
    squeeze = sq[...]
    loads[3].wait()
    loads[4].wait()
    pre_one = mm(sin_ref[...], squeeze, NN, HI)
    act_one = pre_one * jax.nn.sigmoid(pre_one)
    weights = jax.nn.sigmoid(mm(sout_ref[...], act_one, TN, HI))
    wts[...] = weights

    def scaled_of(g):
        u = cube(emb[rows256(g), :].astype(F32))
        return u, u * wts[rows8(g), :][:, None, :]

    def second_pass(g, tot):
        return tot + jnp.sum(scaled_of(g)[1], axis=0)

    total_s = lax.fori_loop(0, groups, second_pass, zero, unroll=8)

    for k in range(5, 8):
        loads[k].wait()

    def third_pass(g, acc):
        u, sc = scaled_of(g)
        for k, (v, vb, tot) in enumerate(((u, emb[rows256(g), :], total), (sc, flat(sc).astype(BF), total_s))):
            p = mm(kron_t, vb, NN)
            prod[k, rows256(g), :] = p
            j = flat(cube(p) * (tot[None] - v) * FACTOR).astype(BF)
            chip = k * groups + g
            js[chip] = j[:LANES]
            js[16 + lax.rem(chip, SIDE) * SIDE + chip // SIDE] = j[LANES:]
            acc = acc + mm(j, w1[rows256(k * groups + g), :], TN)
        return acc

    pre_hidden = lax.fori_loop(0, groups, third_pass, jnp.zeros((LANES, HID), F32), unroll=8)
    half = pl.ds((1 - c) * 16, 16)
    send(js.at[half], jp, ps.at[0], pr.at[0], mate)

    h1 = (pre_hidden * jax.nn.sigmoid(pre_hidden)).astype(BF)
    pre_second = mm(h1, w2_ref[...], NN)
    h2 = (pre_second * jax.nn.sigmoid(pre_second)).astype(BF).astype(F32)
    wl = wl_ref[...].reshape(1, HID).astype(F32)
    logit = jnp.sum(h2 * wl, axis=1, keepdims=True)
    lg_ref[t] = jnp.sum(jnp.where(square, logit, 0.0), axis=0, keepdims=True)

    grad = jax.nn.sigmoid(logit) - target
    d_last = jnp.sum(grad * h2, axis=0, keepdims=True)
    dp2 = (grad * wl * slope(pre_second)).astype(BF)
    d_second = mm(h1, dp2, TN).astype(BF)
    for i in range(16):
        for h in range(2):
            d2[2 * i + h] = d_second[16 * i : 16 * i + 16, LANES * h : LANES * h + LANES]
    dp1 = (mm(dp2, w2_ref[...], NT) * slope(pre_hidden)).astype(BF)
    dpb[0] = dp1
    send(dpb.at[0], dpb.at[1], ps.at[1], pr.at[1], mate)
    send(d2.at[half], d2p, ps.at[2], pr.at[2], mate)

    def side(v):
        return jnp.concatenate([v[i * E : (i + 1) * E] for i in range(8)], axis=1)

    def fourth_pass(g, sums):
        u, sc = scaled_of(g)
        out = []
        bil_sum = sums[2]
        for k, (v, vb, tot) in enumerate(((u, emb[rows256(g), :], total), (sc, flat(sc).astype(BF), total_s))):
            up = cube(mm(w1[rows256(k * groups + g), :], dp1, NT)) * FACTOR
            dq = up * cube(prod[k, rows256(g), :])
            dp = flat(up * (tot[None] - v)).astype(BF)
            du[k, rows256(g), :] = mm(kron, dp, NN) - flat(dq)
            bil_sum = bil_sum + mm(side(vb), side(dp), NT)
            out.append(sums[k] + jnp.sum(dq, axis=0))
        return (*out, bil_sum)

    sums = lax.fori_loop(0, EARLY, fourth_pass, (zero, zero, jnp.zeros((E, E), F32)), unroll=4)

    def peer(me, d):
        return lax.rem(me + d, SIDE)

    got(jp, ps.at[0], pr.at[0], mate)
    got(dpb.at[1], ps.at[1], pr.at[1], mate)
    got(d2p, ps.at[2], pr.at[2], mate)
    d2b[...] = (d2[pl.ds(c * 16, 16)].astype(F32) + d2p[...].astype(F32)).astype(BF).reshape(d2b.shape)
    for d in range(1, SIDE):
        i = peer(a, d)
        send(d2b.at[i], rd1.at[a], s1d.at[d], q1d.at[a], {"tab": at(i, b)})

    both = dpb[...].reshape(2 * LANES, HID)

    def d_first_row(i):
        left = jnp.concatenate(
            [js[pl.ds(16 * c + i * SIDE, SIDE)].reshape(SIDE * LANES, LANES), jp[pl.ds(i * SIDE, SIDE)].reshape(SIDE * LANES, LANES)],
            axis=1,
        )
        out = mm(left, both, NN).astype(BF)
        for k in range(SIDE):
            dfb[i, k, 0:LANES] = out[k * LANES : (k + 1) * LANES, :LANES]
            dfb[i, k, LANES:] = out[k * LANES : (k + 1) * LANES, LANES:]

    for d in range(1, SIDE):
        i = peer(a, d)
        d_first_row(i)
        send(dfb.at[i], r1.at[a], s1.at[d], q1.at[a], {"tab": at(i, b)})
    d_first_row(a)

    for p in others:
        send(lg_ref.at[t], lg_ref.at[t], ls.at[p], lr.at[t], {"tab": p})
    for d in range(1, SIDE):
        i = peer(a, d)
        got(rd1.at[i], s1d.at[d], q1d.at[i], {"tab": at(i, b)})
    out = d2b[a].astype(F32)
    for d in range(1, SIDE):
        out = out + rd1[peer(a, d)].astype(F32)
    d2b[a] = out.astype(BF)
    for d in range(1, SIDE):
        k = peer(b, d)
        send(d2b.at[a, k], rd2.at[b], s2d.at[d], q2d.at[b], {"tab": at(a, k)})

    sum_q, sum_qs, d_bil = lax.fori_loop(EARLY, groups, fourth_pass, sums, unroll=4)

    for d in range(1, SIDE):
        k = peer(b, d)
        got(rd2.at[k], s2d.at[d], q2d.at[k], {"tab": at(a, k)})
    out = d2b[a, b].astype(F32)
    for d in range(1, SIDE):
        out = out + rd2[peer(b, d)].astype(F32)
    rdz[r] = out.astype(BF)
    for d in range(1, REP):
        send(rdz.at[r], rdz.at[r], szd.at[d], qzd.at[r], {"rep": peer(r, d)})

    def fifth_pass(g, _):
        u = cube(emb[rows256(g), :].astype(F32))
        w = wts[rows8(g), :]
        d_w = jnp.sum((cube(du[1, rows256(g), :]) + sum_qs[None]) * u, axis=1)
        dpw[rows8(g), :] = d_w * w * (1.0 - w)
        return 0

    lax.fori_loop(0, groups, fifth_pass, 0, unroll=8)
    d_pre_w = dpw[...]
    d_act = mm(sout_ref[...], d_pre_w, NN, HI) * slope(pre_one)
    dsq[...] = mm(sin_ref[...], d_act, TN, HI) * (1.0 / E)

    def sixth_pass(g, _):
        w = wts[rows8(g), :][:, None, :]
        out = cube(du[0, rows256(g), :]) + sum_q[None] + w * (cube(du[1, rows256(g), :]) + sum_qs[None])
        out = out + dsq[rows8(g), :][:, None, :]
        demb[rows8(g)] = out.astype(BF)
        return 0

    lax.fori_loop(0, groups, sixth_pass, 0, unroll=8)

    def by_slot(s, _):
        dslot[s] = demb[place_ref[s]]
        return 0

    lax.fori_loop(0, FIELDS, by_slot, 0, unroll=16)

    for p in others:
        send(dslot.at[pair(p)], rd_ref.at[pair(t)], ds.at[p], dr.at[t], {"tab": p})
    rd_ref[pair(t)] = dslot[pair(t)]

    d_in = mm(d_act, squeeze, NT, HI)
    d_out = mm(act_one, d_pre_w, NT, HI)
    sr[0, c, 0:E] = jnp.concatenate([d_in, d_out], axis=1).astype(BF)
    sr[0, c, E : 2 * E] = jnp.zeros((E, LANES), BF)
    sr[0, c, E : 2 * E, 0:E] = d_bil.astype(BF)
    low = iota((16, LANES), 0)
    last = jnp.where(low == 0, d_last[:, :LANES], jnp.where(low == 1, d_last[:, LANES:], 0.0))
    sr[0, c, 2 * E : SMALL] = last.astype(BF)

    def peers(phase):
        if phase == 0:
            return c, [(1 - c, mate)]
        if phase == 1:
            return a, [(lax.rem(a + d, SIDE), {"tab": at(lax.rem(a + d, SIDE), b)}) for d in range(1, SIDE)]
        if phase == 2:
            return b, [(lax.rem(b + d, SIDE), {"tab": at(a, lax.rem(b + d, SIDE))}) for d in range(1, SIDE)]
        return r, [(lax.rem(r + d, REP), {"rep": lax.rem(r + d, REP)}) for d in range(1, REP)]

    def small_start(phase):
        me, rest = peers(phase)
        for d, (_, dev) in enumerate(rest):
            send(sr.at[phase, me], sr.at[phase, me], ss.at[phase, d], sq_r.at[phase, me], dev)

    def small_end(phase):
        me, rest = peers(phase)
        for d, (who, dev) in enumerate(rest):
            got(sr.at[phase, who], ss.at[phase, d], sq_r.at[phase, who], dev)
        size = 2 if phase == 0 else 4
        out = sr[phase, 0].astype(F32)
        for k in range(1, size):
            out = out + sr[phase, k].astype(F32)
        return out

    small_start(0)

    for d in range(1, SIDE):
        i = lax.rem(a + d, SIDE)
        got(r1.at[i], s1.at[d], q1.at[i], {"tab": at(i, b)})

    def first_sum(k, _):
        out = dfb[a, k].astype(F32)
        for d in range(1, SIDE):
            out = out + r1[lax.rem(a + d, SIDE), k].astype(F32)
        dfb[a, k] = out.astype(BF)
        return 0

    for d in range(1, SIDE):
        k = lax.rem(b + d, SIDE)
        first_sum(k, 0)
        send(dfb.at[a, k], r2.at[b], s2.at[d], q2.at[b], {"tab": at(a, k)})
    first_sum(b, 0)

    sr[1, a] = small_end(0).astype(BF)
    small_start(1)

    for d in range(1, SIDE):
        k = lax.rem(b + d, SIDE)
        got(r2.at[k], s2.at[d], q2.at[k], {"tab": at(a, k)})
    out = dfb[a, b].astype(F32)
    for d in range(1, SIDE):
        out = out + r2[lax.rem(b + d, SIDE)].astype(F32)
    rz[r] = out.astype(BF)
    for d in range(1, REP):
        o = lax.rem(r + d, REP)
        send(rz.at[r], rz.at[r], sz.at[d], qz.at[r], {"rep": o})

    for d in range(1, REP):
        got(rdz.at[peer(r, d)], szd.at[d], qzd.at[peer(r, d)], {"rep": peer(r, d)})
    out = rdz[0].astype(F32)
    for k in range(1, REP):
        out = out + rdz[k].astype(F32)
    mine = block_of(t)
    ag_ref[mine] = out.astype(BF)

    for p in others:
        send(ag_ref.at[mine], ag_ref.at[mine], gs.at[p], gr.at[t], {"tab": p})

    sr[2, b] = small_end(1).astype(BF)
    small_start(2)


    def d_wait(i, _):
        p = lax.rem(t + i, TAB)
        got(rd_ref.at[pair(p)], ds.at[p], dr.at[p], {"tab": p})
        return 0

    lax.fori_loop(1, TAB, d_wait, 0)

    def proj_pass(j, acc):
        left = jnp.concatenate([rd_ref[pair(2 * j)].reshape(2 * E, LANES), rd_ref[pair(2 * j + 1)].reshape(2 * E, LANES)], axis=1)
        right = jnp.concatenate([xs[0, rows256(j), :], xs[1, rows256(j), :]], axis=1)
        return acc + mm(left, right, NN)

    acc = lax.fori_loop(0, TAB // 2, proj_pass, jnp.zeros((2 * E, 2 * LANES), F32), unroll=8)
    dz[r] = jnp.concatenate([acc[:E, :LANES], acc[E:, LANES:]], axis=0).astype(BF)
    for d in range(1, REP):
        o = lax.rem(r + d, REP)
        send(dz.at[r], dz.at[r], sd.at[d], qd.at[r], {"rep": o})

    pt = pt_ref[...]
    nil = jnp.zeros((E, LANES), BF)
    wide = jnp.concatenate(
        [jnp.concatenate([pt[:E], nil], axis=1), jnp.concatenate([nil, pt[E:]], axis=1)], axis=0
    )
    writes = []
    for p in range(PARTS):
        for k in range(p * (TAB // PARTS), (p + 1) * (TAB // PARTS)):
            out = mm(rd_ref[2 * k : 2 * k + 2].reshape(2 * E, LANES), wide, TN).astype(BF)
            xs[0, k * LANES : (k + 1) * LANES] = out[:, :LANES]
            xs[1, k * LANES : (k + 1) * LANES] = out[:, LANES:]
        piece = pl.ds(p * part, part)
        writes.append(pltpu.make_async_copy(xs.at[:, piece], dx_hbm.at[:, piece], out_sem.at[p]))
        writes[p].start()

    sr[3, r] = small_end(2).astype(BF)
    small_start(3)

    for d in range(1, REP):
        o = lax.rem(r + d, REP)
        got(rz.at[o], sz.at[d], qz.at[o], {"rep": o})
    out = rz[0].astype(F32)
    for k in range(1, REP):
        out = out + rz[k].astype(F32)
    df_ref[...] = out

    for d in range(1, REP):
        o = lax.rem(r + d, REP)
        got(dz.at[o], sd.at[d], qd.at[o], {"rep": o})
    out = dz[0].astype(F32)
    for k in range(1, REP):
        out = out + dz[k].astype(F32)
    for i in range(2):
        dpt_ref[i] = jnp.where(keep[i], out[i * E : (i + 1) * E], 0.0)
    smf_ref[...] = small_end(3)

    def last_wait(i, _):
        p = lax.rem(t + i, TAB)
        dev = {"tab": p}
        got(lg_ref.at[p], ls.at[p], lr.at[p], dev)
        got(ag_ref.at[block_of(p)], gs.at[p], gr.at[p], dev)
        sent(e_ref.at[p], es.at[p], er.at[p], dev)
        sent(dslot.at[pair(p)], ds.at[p], dr.at[p], dev)
        sent(lg_ref.at[t], ls.at[p], lr.at[p], dev)
        sent(ag_ref.at[mine], gs.at[p], gr.at[p], dev)
        return 0

    lax.fori_loop(1, TAB, last_wait, 0)
    sent(js.at[half], ps.at[0], pr.at[0], mate)
    sent(dpb.at[0], ps.at[1], pr.at[1], mate)
    sent(d2.at[half], ps.at[2], pr.at[2], mate)
    for d in range(1, SIDE):
        i = lax.rem(a + d, SIDE)
        k = lax.rem(b + d, SIDE)
        o = lax.rem(r + d, REP)
        sent(dfb.at[i], s1.at[d], q1.at[i], {"tab": at(i, b)})
        sent(dfb.at[a, k], s2.at[d], q2.at[k], {"tab": at(a, k)})
        sent(rz.at[r], sz.at[d], qz.at[r], {"rep": o})
        sent(d2b.at[i], s1d.at[d], q1d.at[i], {"tab": at(i, b)})
        sent(d2b.at[a, k], s2d.at[d], q2d.at[k], {"tab": at(a, k)})
        sent(rdz.at[r], szd.at[d], qzd.at[r], {"rep": o})
        sent(dz.at[r], sd.at[d], qd.at[r], {"rep": o})
    for copy in writes:
        copy.wait()
    for phase in range(4):
        me, rest = peers(phase)
        for d, (_, dev) in enumerate(rest):
            sent(sr.at[phase, me], ss.at[phase, d], sq_r.at[phase, me], dev)


def exchange(placement, widths, labels, proj, sin, sout, bil, w1, w2, wl, pooled):
    vmem = pl.BlockSpec(memory_space=pltpu.VMEM)
    smem = pl.BlockSpec(memory_space=pltpu.SMEM)
    hbm = pl.BlockSpec(memory_space=pltpu.HBM)
    rows = FIELDS * E
    dma = pltpu.SemaphoreType.DMA
    arrays = (placement, labels, proj, sin, sout, bil, w1, w2, wl, pooled)
    return pl.pallas_call(
        main_kernel,
        in_specs=[smem] * 2 + [hbm] * len(arrays),
        out_specs=[hbm] + [vmem] * 5,
        out_shape=[
            jax.ShapeDtypeStruct(pooled.shape, BF),
            jax.ShapeDtypeStruct((TAB, 1, LANES), F32),
            jax.ShapeDtypeStruct((BLOCK, LANES), F32),
            jax.ShapeDtypeStruct((TAB, 16, LANES), BF),
            jax.ShapeDtypeStruct((SMALL, LANES), F32),
            jax.ShapeDtypeStruct((2, E, LANES), F32),
        ],
        scratch_shapes=[pltpu.VMEM((FIELDS, E, LANES), BF), pltpu.VMEM((2 * E, LANES), BF)]
        + [pltpu.VMEM(v.shape, v.dtype) for v in arrays]
        + [
            pltpu.VMEM((TAB, 2, E, LANES), BF),
            pltpu.VMEM((FIELDS, E, LANES), BF),
            pltpu.VMEM((rows, LANES), BF),
            pltpu.VMEM((2, rows, LANES), F32),
            pltpu.VMEM((2, rows, LANES), F32),
            pltpu.VMEM((FIELDS, LANES), F32),
            pltpu.VMEM((FIELDS, LANES), F32),
            pltpu.VMEM((FIELDS, LANES), F32),
            pltpu.VMEM((FIELDS, LANES), F32),
            pltpu.VMEM((TAB, LANES, LANES), BF),
            pltpu.VMEM((16, LANES, LANES), BF),
            pltpu.VMEM((2, LANES, HID), BF),
            pltpu.VMEM((TAB, 16, LANES), BF),
            pltpu.VMEM((16, 16, LANES), BF),
            pltpu.VMEM((FIELDS, E, LANES), BF),
            pltpu.VMEM((FIELDS, E, LANES), BF),
            pltpu.VMEM((SIDE, SIDE, BLOCK, LANES), BF),
            pltpu.VMEM((SIDE, SIDE, BLOCK, LANES), BF),
            pltpu.VMEM((SIDE, BLOCK, LANES), BF),
            pltpu.VMEM((REP, BLOCK, LANES), BF),
            pltpu.VMEM((4, 4, SMALL, LANES), BF),
            pltpu.VMEM((REP, 2 * E, LANES), BF),
            pltpu.VMEM((SIDE, SIDE, 16, LANES), BF),
            pltpu.VMEM((SIDE, SIDE, 16, LANES), BF),
            pltpu.VMEM((SIDE, 16, LANES), BF),
            pltpu.VMEM((REP, 16, LANES), BF),
            pltpu.VMEM((1, FIELDS), jnp.int32),
            pltpu.SMEM((1, FIELDS), jnp.int32),
            dma((10 + PARTS,)),
        ]
        + [dma((TAB,))] * 8
        + [dma((3,))] * 2
        + [dma((4,))] * 6
        + [dma((4, 4))] * 2
        + [dma((4,))] * 8
        + [dma((PARTS,))],
        compiler_params=pltpu.CompilerParams(
            collective_id=0, has_side_effects=True, vmem_limit_bytes=60 * 1024 * 1024
        ),
        name="exchange",
    )(placement, widths, *arrays)


def finish_kernel(
    tab_ref, ready_hbm, lg_hbm, df_hbm, ag_hbm, smf_hbm, dpt_hbm, route_hbm,
    scores_ref, dx_hbm, dproj_ref, din_ref, dout_ref, dbil_ref, dfirst_ref, dsecond_ref, dlast_ref,
    lg_ref, df_ref, ag_ref, smf_ref, route_ref, dx, load_sem, out_sem,
):
    pairs = (
        (lg_hbm, lg_ref), (route_hbm, route_ref), (smf_hbm, smf_ref), (df_hbm, df_ref), (ag_hbm, ag_ref),
        (dpt_hbm, dproj_ref),
    )
    part = dx.shape[1] // PARTS
    pieces = [pl.ds(p * part, part) for p in range(PARTS)]
    reads = [pltpu.make_async_copy(ready_hbm.at[:, v], dx.at[:, v], load_sem.at[6 + p]) for p, v in enumerate(pieces)]
    writes = [pltpu.make_async_copy(dx.at[:, v], dx_hbm.at[:, v], out_sem.at[p]) for p, v in enumerate(pieces)]
    loads = [pltpu.make_async_copy(src, dst, load_sem.at[i]) for i, (src, dst) in enumerate(pairs)]
    reads[0].start()
    for copy in loads + reads[1:]:
        copy.start()
    for p in range(PARTS):
        reads[p].wait()
        writes[p].start()
    for copy in loads:
        copy.wait()
    idx = route_ref[:, pl.ds(pl.multiple_of(tab_ref[0] * LANES, LANES), LANES)]
    table = lg_ref[...].reshape(TAB, LANES)
    low = jnp.broadcast_to(lax.rem(idx, LANES), (TAB, LANES))
    found = jnp.take_along_axis(table, low, axis=1)
    scores_ref[...] = jnp.sum(
        jnp.where(idx // LANES == iota((TAB, LANES), 0), found, 0.0), axis=0, keepdims=True
    )
    din_ref[...] = smf_ref[0:E, 0:FIELDS]
    dout_ref[...] = smf_ref[0:E, FIELDS:]
    dbil_ref[...] = smf_ref[E : 2 * E, 0:E]
    dlast_ref[:, 0:LANES] = smf_ref[2 * E : 2 * E + 1, :]
    dlast_ref[:, LANES:] = smf_ref[2 * E + 1 : 2 * E + 2, :]
    dfirst_ref[:, 0:LANES] = df_ref[0:LANES, :]
    dfirst_ref[:, LANES:] = df_ref[LANES : 2 * LANES, :]
    for i in range(16):
        dsecond_ref[16 * i : 16 * i + 16, 0:LANES] = ag_ref[2 * i].astype(F32)
        dsecond_ref[16 * i : 16 * i + 16, LANES:] = ag_ref[2 * i + 1].astype(F32)
    for w in writes:
        w.wait()


def finish(tab, ready, lg, df, ag, smf, dpt, route, pooled_shape):
    vmem = pl.BlockSpec(memory_space=pltpu.VMEM)
    smem = pl.BlockSpec(memory_space=pltpu.SMEM)
    hbm = pl.BlockSpec(memory_space=pltpu.HBM)
    arrays = (ready, lg, df, ag, smf, dpt, route)
    outs = [
        ((1, LANES), F32), (pooled_shape, BF), ((2, E, LANES), F32), ((E, FIELDS), F32), ((E, FIELDS), F32),
        ((E, E), F32), ((LANES, HID), F32), ((HID, HID), F32), ((1, HID), F32),
    ]
    return pl.pallas_call(
        finish_kernel,
        in_specs=[smem] + [hbm] * len(arrays),
        out_specs=[vmem, hbm] + [vmem] * 7,
        out_shape=[jax.ShapeDtypeStruct(s, d) for s, d in outs],
        scratch_shapes=[pltpu.VMEM(v.shape, v.dtype) for v in (lg, df, ag, smf, route)]
        + [
            pltpu.VMEM(pooled_shape, BF),
            pltpu.SemaphoreType.DMA((6 + PARTS,)),
            pltpu.SemaphoreType.DMA((PARTS,)),
        ],
        compiler_params=pltpu.CompilerParams(vmem_limit_bytes=60 * 1024 * 1024),
        name="finish",
    )(tab, *arrays)


def shards(pooled, widths, placement, route, labels, proj, senet_in, senet_out, bilinear, w_first, w_second, w_last):
    tab = lax.axis_index("tab").astype(jnp.int32).reshape(1)
    ready, lg, df, ag, smf, dpt = exchange(
        placement, widths, labels, jnp.swapaxes(proj, 1, 2), senet_in.T, senet_out, bilinear, w_first, w_second,
        w_last, pooled,
    )
    scores, dx, dproj, din, dout, dbil, dfirst, dsecond, dlast = finish(
        tab, ready, lg, df, ag, smf, dpt, route, pooled.shape
    )
    return scores, dx, jnp.swapaxes(dproj, 1, 2), din.T, dout, dbil, dfirst, dsecond, dlast[0]


def solution(mesh):
    whole = P()
    placed = (
        P("tab", "rep", None), whole, whole, P("rep", None), P("rep", None), whole, whole, whole, whole, whole,
        whole, whole,
    )
    return jax.shard_map(
        shards,
        mesh=mesh,
        in_specs=placed,
        out_specs=(
            P("rep", "tab"), P("tab", "rep", None), P("tab", None, None), whole, whole, whole, P("tab", None),
            whole, whole,
        ),
        check_vma=False,
    )
```

```python
import functools

import jax
import jax.numpy as jnp
from jax import lax
from jax.experimental import pallas as pl
from jax.experimental.pallas import tpu as pltpu
from jax.sharding import PartitionSpec as P

F32 = jnp.float32
BF = jnp.bfloat16
HI = lax.Precision.HIGHEST
NN = (((1,), (0,)), ((), ()))
NT = (((1,), (1,)), ((), ()))
TN = (((0,), (0,)), ((), ()))

FIELDS = 64
E = 32
TAB = 32
REP = 4
EARLY = 4
SIDE = 4
PARTS = 4
LANES = 128
HID = 256
BLOCK = 256
SMALL = 80
FACTOR = 0.125


def mm(a, b, dims, precision=None):
    return lax.dot_general(a, b, dims, precision=precision, preferred_element_type=F32)


def slope(u):
    s = jax.nn.sigmoid(u)
    return s * (1.0 + u * (1.0 - s))


def iota(shape, dim):
    return lax.broadcasted_iota(jnp.int32, shape, dim)


def send(src, dst, ssem, rsem, dev):
    pltpu.make_async_remote_copy(
        src_ref=src, dst_ref=dst, send_sem=ssem, recv_sem=rsem, device_id=dev,
        device_id_type=pl.DeviceIdType.MESH,
    ).start()


def got(dst, ssem, rsem, dev):
    pltpu.make_async_remote_copy(
        src_ref=dst, dst_ref=dst, send_sem=ssem, recv_sem=rsem, device_id=dev,
        device_id_type=pl.DeviceIdType.MESH,
    ).wait_recv()


def sent(src, ssem, rsem, dev):
    pltpu.make_async_remote_copy(
        src_ref=src, dst_ref=src, send_sem=ssem, recv_sem=rsem, device_id=dev,
        device_id_type=pl.DeviceIdType.MESH,
    ).wait_send()


def main_kernel(
    place_ref, width_ref, place_hbm, labels_hbm, proj_hbm, sin_hbm, sout_hbm, bil_hbm, w1_hbm, w2_hbm, wl_hbm, pooled_hbm,
    dx_hbm, lg_ref, df_ref, ag_ref, smf_ref, dpt_ref,
    rd_ref, pt_ref,
    place_vec, labels_ref, projs, sin_ref, sout_ref, bil_ref, w1, w2_ref, wl_ref, xs, e_ref, recv, emb, prod, du, sq, wts, dpw, dsq, js, jp, dpb, d2, d2p, demb, dslot, dfb, r1, r2, rz, sr, dz, d2b, rd1, rd2, rdz, inv_vec, inv_ref,
    load_sem, es, er, ds, dr, ls, lr, gs, gr, ps, pr, s1, q1, s2, q2, sz, qz, ss, sq_r, sd, qd, s1d, q1d, s2d, q2d, szd, qzd, out_sem,
):
    t = lax.axis_index("tab")
    r = lax.axis_index("rep")
    c = lax.rem(t, 2)
    n = t // 2
    x = n // SIDE
    y = lax.rem(n, SIDE)
    a = x + c * (y - x)
    b = y + c * (x - y)

    def at(a_, b_):
        return ((a_ + c * (b_ - a_)) * SIDE + (b_ + c * (a_ - b_))) * 2 + c

    def block_of(tab):
        c_ = lax.rem(tab, 2)
        n_ = tab // 2
        x_ = n_ // SIDE
        y_ = lax.rem(n_, SIDE)
        return 16 * c_ + SIDE * (x_ + c_ * (y_ - x_)) + y_ + c_ * (x_ - y_)

    mate = {"tab": t + 1 - 2 * c}
    barrier = pltpu.get_barrier_semaphore()

    def away(v):
        return min(v, SIDE - v)

    hops = sorted(
        ((dx, dy, dc) for dx in range(SIDE) for dy in range(SIDE) for dc in range(2) if dx or dy or dc),
        key=lambda h: -(away(h[0]) + away(h[1])),
    )
    others = [
        (lax.rem(x + dx, SIDE) * SIDE + lax.rem(y + dy, SIDE)) * 2 + lax.rem(c + dc, 2) for dx, dy, dc in hops
    ]

    for d in (2, 1, 3):
        pl.semaphore_signal(barrier, inc=1, device_id={"rep": lax.rem(r + d, REP)}, device_id_type=pl.DeviceIdType.MESH)
    for p in others:
        pl.semaphore_signal(barrier, inc=1, device_id={"tab": p}, device_id_type=pl.DeviceIdType.MESH)

    pairs = (
        (proj_hbm, projs), (labels_hbm, labels_ref), (bil_hbm, bil_ref), (sin_hbm, sin_ref), (sout_hbm, sout_ref),
        (w2_hbm, w2_ref), (wl_hbm, wl_ref), (w1_hbm, w1), (place_hbm, place_vec),
    )
    loads = [pltpu.make_async_copy(src, dst, load_sem.at[i]) for i, (src, dst) in enumerate(pairs)]
    part = xs.shape[1] // PARTS
    for k in range(PARTS):
        piece = pl.ds(k * part, part)
        loads.append(pltpu.make_async_copy(pooled_hbm.at[:, piece], xs.at[:, piece], load_sem.at[len(pairs) + k]))
    for k in [8, 0] + list(range(len(pairs), len(pairs) + PARTS)) + list(range(1, 8)):
        loads[k].start()

    loads[8].wait()
    line = place_vec[...].reshape(1, FIELDS)
    eye = iota((FIELDS, FIELDS), 0) == iota((FIELDS, FIELDS), 1)
    column = jnp.sum(jnp.where(eye, line, 0), axis=1, keepdims=True)
    spots = iota((FIELDS, FIELDS), 0)
    slot_of = jnp.sum(jnp.where(column == iota((FIELDS, FIELDS), 1), spots, 0), axis=0, keepdims=True)
    inv_vec[...] = jnp.minimum(slot_of, FIELDS - 1)
    invert = pltpu.make_async_copy(inv_vec, inv_ref, load_sem.at[9 + PARTS])
    invert.start()

    loads[0].wait()
    keep = []
    for i in range(2):
        field = place_ref[2 * t + i]
        keep.append(iota((E, LANES), 1) < width_ref[field])
        pt_ref[i * E : (i + 1) * E, :] = jnp.where(keep[i], projs[field].astype(F32), 0.0).astype(BF)
    for k in range(PARTS):
        loads[len(pairs) + k].wait()
        for i in range(2):
            out = mm(pt_ref[i * E : (i + 1) * E, :], xs[i, k * part : (k + 1) * part, :], NT).astype(BF)
            for d in range(part // LANES):
                e_ref[k * (part // LANES) + d, i] = out[:, d * LANES : (d + 1) * LANES]

    small_rows = (lax.rem(iota((HID, E), 0), E) == iota((HID, E), 1)).astype(BF)
    loads[1].wait()
    loads[2].wait()
    small_cols = (lax.rem(iota((E, HID), 1), E) == iota((E, HID), 0)).astype(BF)
    diag = (iota((HID, HID), 0) // E) == (iota((HID, HID), 1) // E)
    bil = bil_ref[...].astype(BF)
    tall = mm(small_rows, bil, NN).astype(BF)
    tall_t = mm(small_rows, bil, NT).astype(BF)
    kron = jnp.where(diag, mm(tall, small_cols, NN), 0.0).astype(BF)
    kron_t = jnp.where(diag, mm(tall_t, small_cols, NN), 0.0).astype(BF)
    square = iota((LANES, LANES), 0) == iota((LANES, LANES), 1)
    label_row = labels_ref[:, pl.ds(pl.multiple_of(t * LANES, LANES), LANES)].astype(F32)
    target = jnp.sum(jnp.where(square, label_row, 0.0), axis=1, keepdims=True)

    pl.semaphore_wait(barrier, TAB - 1 + REP - 1)

    def pair(p):
        return pl.ds(p * 2, 2)

    for p in others:
        send(e_ref.at[p], recv.at[pair(t)], es.at[p], er.at[t], {"tab": p})
    recv[pair(t)] = e_ref[t]

    def e_wait(i, _):
        p = lax.rem(t + i, TAB)
        got(recv.at[pair(p)], es.at[p], er.at[p], {"tab": p})
        return 0

    lax.fori_loop(1, TAB, e_wait, 0)

    def rows32(f):
        return pl.ds(pl.multiple_of(f * E, E), E)

    invert.wait()

    def by_field(f, _):
        emb[rows32(f), :] = recv[inv_ref[0, f]]
        return 0

    lax.fori_loop(0, FIELDS, by_field, 0, unroll=16)

    groups = FIELDS // 8

    def rows256(g):
        return pl.ds(pl.multiple_of(g * HID, HID), HID)

    def rows8(g):
        return pl.ds(pl.multiple_of(g * 8, 8), 8)

    def cube(v):
        return v.reshape(8, E, LANES)

    def flat(v):
        return v.reshape(HID, LANES)

    def first_pass(g, total):
        u = cube(emb[rows256(g), :].astype(F32))
        sq[rows8(g), :] = jnp.sum(u, axis=1) * (1.0 / E)
        return total + jnp.sum(u, axis=0)

    zero = jnp.zeros((E, LANES), F32)
    total = lax.fori_loop(0, groups, first_pass, zero, unroll=8)
    squeeze = sq[...]
    loads[3].wait()
    loads[4].wait()
    pre_one = mm(sin_ref[...], squeeze, NN, HI)
    act_one = pre_one * jax.nn.sigmoid(pre_one)
    weights = jax.nn.sigmoid(mm(sout_ref[...], act_one, TN, HI))
    wts[...] = weights

    def scaled_of(g):
        u = cube(emb[rows256(g), :].astype(F32))
        return u, u * wts[rows8(g), :][:, None, :]

    def second_pass(g, tot):
        return tot + jnp.sum(scaled_of(g)[1], axis=0)

    total_s = lax.fori_loop(0, groups, second_pass, zero, unroll=8)

    for k in range(5, 8):
        loads[k].wait()

    def third_pass(g, acc):
        u, sc = scaled_of(g)
        for k, (v, vb, tot) in enumerate(((u, emb[rows256(g), :], total), (sc, flat(sc).astype(BF), total_s))):
            p = mm(kron_t, vb, NN)
            prod[k, rows256(g), :] = p
            j = flat(cube(p) * (tot[None] - v) * FACTOR).astype(BF)
            chip = k * groups + g
            js[chip] = j[:LANES]
            js[16 + lax.rem(chip, SIDE) * SIDE + chip // SIDE] = j[LANES:]
            acc = acc + mm(j, w1[rows256(k * groups + g), :], TN)
        return acc

    pre_hidden = lax.fori_loop(0, groups, third_pass, jnp.zeros((LANES, HID), F32), unroll=8)
    half = pl.ds((1 - c) * 16, 16)
    send(js.at[half], jp, ps.at[0], pr.at[0], mate)

    h1 = (pre_hidden * jax.nn.sigmoid(pre_hidden)).astype(BF)
    pre_second = mm(h1, w2_ref[...], NN)
    h2 = (pre_second * jax.nn.sigmoid(pre_second)).astype(BF).astype(F32)
    wl = wl_ref[...].reshape(1, HID).astype(F32)
    logit = jnp.sum(h2 * wl, axis=1, keepdims=True)
    lg_ref[t] = jnp.sum(jnp.where(square, logit, 0.0), axis=0, keepdims=True)

    grad = jax.nn.sigmoid(logit) - target
    d_last = jnp.sum(grad * h2, axis=0, keepdims=True)
    dp2 = (grad * wl * slope(pre_second)).astype(BF)
    d_second = mm(h1, dp2, TN).astype(BF)
    for i in range(16):
        for h in range(2):
            d2[2 * i + h] = d_second[16 * i : 16 * i + 16, LANES * h : LANES * h + LANES]
    dp1 = (mm(dp2, w2_ref[...], NT) * slope(pre_hidden)).astype(BF)
    dpb[0] = dp1
    send(dpb.at[0], dpb.at[1], ps.at[1], pr.at[1], mate)
    send(d2.at[half], d2p, ps.at[2], pr.at[2], mate)

    def side(v):
        return jnp.concatenate([v[i * E : (i + 1) * E] for i in range(8)], axis=1)

    def fourth_pass(g, sums):
        u, sc = scaled_of(g)
        out = []
        bil_sum = sums[2]
        for k, (v, vb, tot) in enumerate(((u, emb[rows256(g), :], total), (sc, flat(sc).astype(BF), total_s))):
            up = cube(mm(w1[rows256(k * groups + g), :], dp1, NT)) * FACTOR
            dq = up * cube(prod[k, rows256(g), :])
            dp = flat(up * (tot[None] - v)).astype(BF)
            du[k, rows256(g), :] = mm(kron, dp, NN) - flat(dq)
            bil_sum = bil_sum + mm(side(vb), side(dp), NT)
            out.append(sums[k] + jnp.sum(dq, axis=0))
        return (*out, bil_sum)

    sums = lax.fori_loop(0, EARLY, fourth_pass, (zero, zero, jnp.zeros((E, E), F32)), unroll=4)

    def peer(me, d):
        return lax.rem(me + d, SIDE)

    got(jp, ps.at[0], pr.at[0], mate)
    got(dpb.at[1], ps.at[1], pr.at[1], mate)
    got(d2p, ps.at[2], pr.at[2], mate)
    d2b[...] = (d2[pl.ds(c * 16, 16)].astype(F32) + d2p[...].astype(F32)).astype(BF).reshape(d2b.shape)
    for d in range(1, SIDE):
        i = peer(a, d)
        send(d2b.at[i], rd1.at[a], s1d.at[d], q1d.at[a], {"tab": at(i, b)})

    both = dpb[...].reshape(2 * LANES, HID)

    def d_first_row(i):
        left = jnp.concatenate(
            [js[pl.ds(16 * c + i * SIDE, SIDE)].reshape(SIDE * LANES, LANES), jp[pl.ds(i * SIDE, SIDE)].reshape(SIDE * LANES, LANES)],
            axis=1,
        )
        out = mm(left, both, NN).astype(BF)
        for k in range(SIDE):
            dfb[i, k, 0:LANES] = out[k * LANES : (k + 1) * LANES, :LANES]
            dfb[i, k, LANES:] = out[k * LANES : (k + 1) * LANES, LANES:]

    for d in range(1, SIDE):
        i = peer(a, d)
        d_first_row(i)
        send(dfb.at[i], r1.at[a], s1.at[d], q1.at[a], {"tab": at(i, b)})
    d_first_row(a)

    for p in others:
        send(lg_ref.at[t], lg_ref.at[t], ls.at[p], lr.at[t], {"tab": p})
    for d in range(1, SIDE):
        i = peer(a, d)
        got(rd1.at[i], s1d.at[d], q1d.at[i], {"tab": at(i, b)})
    out = d2b[a].astype(F32)
    for d in range(1, SIDE):
        out = out + rd1[peer(a, d)].astype(F32)
    d2b[a] = out.astype(BF)
    for d in range(1, SIDE):
        k = peer(b, d)
        send(d2b.at[a, k], rd2.at[b], s2d.at[d], q2d.at[b], {"tab": at(a, k)})

    sum_q, sum_qs, d_bil = lax.fori_loop(EARLY, groups, fourth_pass, sums, unroll=4)

    for d in range(1, SIDE):
        k = peer(b, d)
        got(rd2.at[k], s2d.at[d], q2d.at[k], {"tab": at(a, k)})
    out = d2b[a, b].astype(F32)
    for d in range(1, SIDE):
        out = out + rd2[peer(b, d)].astype(F32)
    rdz[r] = out.astype(BF)
    for d in range(1, REP):
        send(rdz.at[r], rdz.at[r], szd.at[d], qzd.at[r], {"rep": peer(r, d)})

    def fifth_pass(g, _):
        u = cube(emb[rows256(g), :].astype(F32))
        w = wts[rows8(g), :]
        d_w = jnp.sum((cube(du[1, rows256(g), :]) + sum_qs[None]) * u, axis=1)
        dpw[rows8(g), :] = d_w * w * (1.0 - w)
        return 0

    lax.fori_loop(0, groups, fifth_pass, 0, unroll=8)
    d_pre_w = dpw[...]
    d_act = mm(sout_ref[...], d_pre_w, NN, HI) * slope(pre_one)
    dsq[...] = mm(sin_ref[...], d_act, TN, HI) * (1.0 / E)

    def sixth_pass(g, _):
        w = wts[rows8(g), :][:, None, :]
        out = cube(du[0, rows256(g), :]) + sum_q[None] + w * (cube(du[1, rows256(g), :]) + sum_qs[None])
        out = out + dsq[rows8(g), :][:, None, :]
        demb[rows8(g)] = out.astype(BF)
        return 0

    lax.fori_loop(0, groups, sixth_pass, 0, unroll=8)

    def by_slot(s, _):
        dslot[s] = demb[place_ref[s]]
        return 0

    lax.fori_loop(0, FIELDS, by_slot, 0, unroll=16)

    for p in others:
        send(dslot.at[pair(p)], rd_ref.at[pair(t)], ds.at[p], dr.at[t], {"tab": p})
    rd_ref[pair(t)] = dslot[pair(t)]

    d_in = mm(d_act, squeeze, NT, HI)
    d_out = mm(act_one, d_pre_w, NT, HI)
    sr[0, c, 0:E] = jnp.concatenate([d_in, d_out], axis=1).astype(BF)
    sr[0, c, E : 2 * E] = jnp.zeros((E, LANES), BF)
    sr[0, c, E : 2 * E, 0:E] = d_bil.astype(BF)
    low = iota((16, LANES), 0)
    last = jnp.where(low == 0, d_last[:, :LANES], jnp.where(low == 1, d_last[:, LANES:], 0.0))
    sr[0, c, 2 * E : SMALL] = last.astype(BF)

    def peers(phase):
        if phase == 0:
            return c, [(1 - c, mate)]
        if phase == 1:
            return r, [(lax.rem(r + d, REP), {"rep": lax.rem(r + d, REP)}) for d in range(1, REP)]
        if phase == 2:
            return a, [(lax.rem(a + d, SIDE), {"tab": at(lax.rem(a + d, SIDE), b)}) for d in range(1, SIDE)]
        return b, [(lax.rem(b + d, SIDE), {"tab": at(a, lax.rem(b + d, SIDE))}) for d in range(1, SIDE)]

    def small_start(phase):
        me, rest = peers(phase)
        for d, (_, dev) in enumerate(rest):
            send(sr.at[phase, me], sr.at[phase, me], ss.at[phase, d], sq_r.at[phase, me], dev)

    def small_end(phase):
        me, rest = peers(phase)
        for d, (who, dev) in enumerate(rest):
            got(sr.at[phase, who], ss.at[phase, d], sq_r.at[phase, who], dev)
        size = 2 if phase == 0 else 4
        out = sr[phase, 0].astype(F32)
        for k in range(1, size):
            out = out + sr[phase, k].astype(F32)
        return out

    small_start(0)
    sr[1, r] = small_end(0).astype(BF)
    small_start(1)


    for d in range(1, SIDE):
        i = lax.rem(a + d, SIDE)
        got(r1.at[i], s1.at[d], q1.at[i], {"tab": at(i, b)})

    def first_sum(k, _):
        out = dfb[a, k].astype(F32)
        for d in range(1, SIDE):
            out = out + r1[lax.rem(a + d, SIDE), k].astype(F32)
        dfb[a, k] = out.astype(BF)
        return 0

    for d in range(1, SIDE):
        k = lax.rem(b + d, SIDE)
        first_sum(k, 0)
        send(dfb.at[a, k], r2.at[b], s2.at[d], q2.at[b], {"tab": at(a, k)})
    first_sum(b, 0)


    sr[2, a] = small_end(1).astype(BF)
    small_start(2)

    for d in range(1, SIDE):
        k = lax.rem(b + d, SIDE)
        got(r2.at[k], s2.at[d], q2.at[k], {"tab": at(a, k)})
    out = dfb[a, b].astype(F32)
    for d in range(1, SIDE):
        out = out + r2[lax.rem(b + d, SIDE)].astype(F32)
    rz[r] = out.astype(BF)
    for d in range(1, REP):
        o = lax.rem(r + d, REP)
        send(rz.at[r], rz.at[r], sz.at[d], qz.at[r], {"rep": o})

    for d in range(1, REP):
        got(rdz.at[peer(r, d)], szd.at[d], qzd.at[peer(r, d)], {"rep": peer(r, d)})
    out = rdz[0].astype(F32)
    for k in range(1, REP):
        out = out + rdz[k].astype(F32)
    mine = block_of(t)
    ag_ref[mine] = out.astype(BF)

    for p in others:
        send(ag_ref.at[mine], ag_ref.at[mine], gs.at[p], gr.at[t], {"tab": p})


    def d_wait(i, _):
        p = lax.rem(t + i, TAB)
        got(rd_ref.at[pair(p)], ds.at[p], dr.at[p], {"tab": p})
        return 0

    lax.fori_loop(1, TAB, d_wait, 0)

    sr[3, b] = small_end(2).astype(BF)
    small_start(3)

    def proj_pass(j, acc):
        left = jnp.concatenate([rd_ref[pair(2 * j)].reshape(2 * E, LANES), rd_ref[pair(2 * j + 1)].reshape(2 * E, LANES)], axis=1)
        right = jnp.concatenate([xs[0, rows256(j), :], xs[1, rows256(j), :]], axis=1)
        return acc + mm(left, right, NN)

    acc = lax.fori_loop(0, TAB // 2, proj_pass, jnp.zeros((2 * E, 2 * LANES), F32), unroll=8)
    dz[r] = jnp.concatenate([acc[:E, :LANES], acc[E:, LANES:]], axis=0).astype(BF)
    for d in range(1, REP):
        o = lax.rem(r + d, REP)
        send(dz.at[r], dz.at[r], sd.at[d], qd.at[r], {"rep": o})

    pt = pt_ref[...]
    nil = jnp.zeros((E, LANES), BF)
    wide = jnp.concatenate(
        [jnp.concatenate([pt[:E], nil], axis=1), jnp.concatenate([nil, pt[E:]], axis=1)], axis=0
    )
    writes = []
    for p in range(PARTS):
        for k in range(p * (TAB // PARTS), (p + 1) * (TAB // PARTS)):
            out = mm(rd_ref[2 * k : 2 * k + 2].reshape(2 * E, LANES), wide, TN).astype(BF)
            xs[0, k * LANES : (k + 1) * LANES] = out[:, :LANES]
            xs[1, k * LANES : (k + 1) * LANES] = out[:, LANES:]
        piece = pl.ds(p * part, part)
        writes.append(pltpu.make_async_copy(xs.at[:, piece], dx_hbm.at[:, piece], out_sem.at[p]))
        writes[p].start()


    for d in range(1, REP):
        o = lax.rem(r + d, REP)
        got(rz.at[o], sz.at[d], qz.at[o], {"rep": o})
    out = rz[0].astype(F32)
    for k in range(1, REP):
        out = out + rz[k].astype(F32)
    df_ref[...] = out

    for d in range(1, REP):
        o = lax.rem(r + d, REP)
        got(dz.at[o], sd.at[d], qd.at[o], {"rep": o})
    out = dz[0].astype(F32)
    for k in range(1, REP):
        out = out + dz[k].astype(F32)
    for i in range(2):
        dpt_ref[i] = jnp.where(keep[i], out[i * E : (i + 1) * E], 0.0)
    smf_ref[...] = small_end(3)

    def last_wait(i, _):
        p = lax.rem(t + i, TAB)
        dev = {"tab": p}
        got(lg_ref.at[p], ls.at[p], lr.at[p], dev)
        got(ag_ref.at[block_of(p)], gs.at[p], gr.at[p], dev)
        sent(e_ref.at[p], es.at[p], er.at[p], dev)
        sent(dslot.at[pair(p)], ds.at[p], dr.at[p], dev)
        sent(lg_ref.at[t], ls.at[p], lr.at[p], dev)
        sent(ag_ref.at[mine], gs.at[p], gr.at[p], dev)
        return 0

    lax.fori_loop(1, TAB, last_wait, 0)
    sent(js.at[half], ps.at[0], pr.at[0], mate)
    sent(dpb.at[0], ps.at[1], pr.at[1], mate)
    sent(d2.at[half], ps.at[2], pr.at[2], mate)
    for d in range(1, SIDE):
        i = lax.rem(a + d, SIDE)
        k = lax.rem(b + d, SIDE)
        o = lax.rem(r + d, REP)
        sent(dfb.at[i], s1.at[d], q1.at[i], {"tab": at(i, b)})
        sent(dfb.at[a, k], s2.at[d], q2.at[k], {"tab": at(a, k)})
        sent(rz.at[r], sz.at[d], qz.at[r], {"rep": o})
        sent(d2b.at[i], s1d.at[d], q1d.at[i], {"tab": at(i, b)})
        sent(d2b.at[a, k], s2d.at[d], q2d.at[k], {"tab": at(a, k)})
        sent(rdz.at[r], szd.at[d], qzd.at[r], {"rep": o})
        sent(dz.at[r], sd.at[d], qd.at[r], {"rep": o})
    for copy in writes:
        copy.wait()
    for phase in range(4):
        me, rest = peers(phase)
        for d, (_, dev) in enumerate(rest):
            sent(sr.at[phase, me], ss.at[phase, d], sq_r.at[phase, me], dev)


def exchange(placement, widths, labels, proj, sin, sout, bil, w1, w2, wl, pooled):
    vmem = pl.BlockSpec(memory_space=pltpu.VMEM)
    smem = pl.BlockSpec(memory_space=pltpu.SMEM)
    hbm = pl.BlockSpec(memory_space=pltpu.HBM)
    rows = FIELDS * E
    dma = pltpu.SemaphoreType.DMA
    arrays = (placement, labels, proj, sin, sout, bil, w1, w2, wl, pooled)
    return pl.pallas_call(
        main_kernel,
        in_specs=[smem] * 2 + [hbm] * len(arrays),
        out_specs=[hbm] + [vmem] * 5,
        out_shape=[
            jax.ShapeDtypeStruct(pooled.shape, BF),
            jax.ShapeDtypeStruct((TAB, 1, LANES), F32),
            jax.ShapeDtypeStruct((BLOCK, LANES), F32),
            jax.ShapeDtypeStruct((TAB, 16, LANES), BF),
            jax.ShapeDtypeStruct((SMALL, LANES), F32),
            jax.ShapeDtypeStruct((2, E, LANES), F32),
        ],
        scratch_shapes=[pltpu.VMEM((FIELDS, E, LANES), BF), pltpu.VMEM((2 * E, LANES), BF)]
        + [pltpu.VMEM(v.shape, v.dtype) for v in arrays]
        + [
            pltpu.VMEM((TAB, 2, E, LANES), BF),
            pltpu.VMEM((FIELDS, E, LANES), BF),
            pltpu.VMEM((rows, LANES), BF),
            pltpu.VMEM((2, rows, LANES), F32),
            pltpu.VMEM((2, rows, LANES), F32),
            pltpu.VMEM((FIELDS, LANES), F32),
            pltpu.VMEM((FIELDS, LANES), F32),
            pltpu.VMEM((FIELDS, LANES), F32),
            pltpu.VMEM((FIELDS, LANES), F32),
            pltpu.VMEM((TAB, LANES, LANES), BF),
            pltpu.VMEM((16, LANES, LANES), BF),
            pltpu.VMEM((2, LANES, HID), BF),
            pltpu.VMEM((TAB, 16, LANES), BF),
            pltpu.VMEM((16, 16, LANES), BF),
            pltpu.VMEM((FIELDS, E, LANES), BF),
            pltpu.VMEM((FIELDS, E, LANES), BF),
            pltpu.VMEM((SIDE, SIDE, BLOCK, LANES), BF),
            pltpu.VMEM((SIDE, SIDE, BLOCK, LANES), BF),
            pltpu.VMEM((SIDE, BLOCK, LANES), BF),
            pltpu.VMEM((REP, BLOCK, LANES), BF),
            pltpu.VMEM((4, 4, SMALL, LANES), BF),
            pltpu.VMEM((REP, 2 * E, LANES), BF),
            pltpu.VMEM((SIDE, SIDE, 16, LANES), BF),
            pltpu.VMEM((SIDE, SIDE, 16, LANES), BF),
            pltpu.VMEM((SIDE, 16, LANES), BF),
            pltpu.VMEM((REP, 16, LANES), BF),
            pltpu.VMEM((1, FIELDS), jnp.int32),
            pltpu.SMEM((1, FIELDS), jnp.int32),
            dma((10 + PARTS,)),
        ]
        + [dma((TAB,))] * 8
        + [dma((3,))] * 2
        + [dma((4,))] * 6
        + [dma((4, 4))] * 2
        + [dma((4,))] * 8
        + [dma((PARTS,))],
        compiler_params=pltpu.CompilerParams(
            collective_id=0, has_side_effects=True, vmem_limit_bytes=60 * 1024 * 1024
        ),
        name="exchange",
    )(placement, widths, *arrays)


def finish_kernel(
    tab_ref, ready_hbm, lg_hbm, df_hbm, ag_hbm, smf_hbm, dpt_hbm, route_hbm,
    scores_ref, dx_hbm, dproj_ref, din_ref, dout_ref, dbil_ref, dfirst_ref, dsecond_ref, dlast_ref,
    lg_ref, df_ref, ag_ref, smf_ref, route_ref, dx, load_sem, out_sem,
):
    pairs = (
        (lg_hbm, lg_ref), (route_hbm, route_ref), (smf_hbm, smf_ref), (df_hbm, df_ref), (ag_hbm, ag_ref),
        (dpt_hbm, dproj_ref),
    )
    part = dx.shape[1] // PARTS
    pieces = [pl.ds(p * part, part) for p in range(PARTS)]
    reads = [pltpu.make_async_copy(ready_hbm.at[:, v], dx.at[:, v], load_sem.at[6 + p]) for p, v in enumerate(pieces)]
    writes = [pltpu.make_async_copy(dx.at[:, v], dx_hbm.at[:, v], out_sem.at[p]) for p, v in enumerate(pieces)]
    loads = [pltpu.make_async_copy(src, dst, load_sem.at[i]) for i, (src, dst) in enumerate(pairs)]
    reads[0].start()
    for copy in loads + reads[1:]:
        copy.start()
    for p in range(PARTS):
        reads[p].wait()
        writes[p].start()
    for copy in loads:
        copy.wait()
    idx = route_ref[:, pl.ds(pl.multiple_of(tab_ref[0] * LANES, LANES), LANES)]
    table = lg_ref[...].reshape(TAB, LANES)
    low = jnp.broadcast_to(lax.rem(idx, LANES), (TAB, LANES))
    found = jnp.take_along_axis(table, low, axis=1)
    scores_ref[...] = jnp.sum(
        jnp.where(idx // LANES == iota((TAB, LANES), 0), found, 0.0), axis=0, keepdims=True
    )
    din_ref[...] = smf_ref[0:E, 0:FIELDS]
    dout_ref[...] = smf_ref[0:E, FIELDS:]
    dbil_ref[...] = smf_ref[E : 2 * E, 0:E]
    dlast_ref[:, 0:LANES] = smf_ref[2 * E : 2 * E + 1, :]
    dlast_ref[:, LANES:] = smf_ref[2 * E + 1 : 2 * E + 2, :]
    dfirst_ref[:, 0:LANES] = df_ref[0:LANES, :]
    dfirst_ref[:, LANES:] = df_ref[LANES : 2 * LANES, :]
    for i in range(16):
        dsecond_ref[16 * i : 16 * i + 16, 0:LANES] = ag_ref[2 * i].astype(F32)
        dsecond_ref[16 * i : 16 * i + 16, LANES:] = ag_ref[2 * i + 1].astype(F32)
    for w in writes:
        w.wait()


def finish(tab, ready, lg, df, ag, smf, dpt, route, pooled_shape):
    vmem = pl.BlockSpec(memory_space=pltpu.VMEM)
    smem = pl.BlockSpec(memory_space=pltpu.SMEM)
    hbm = pl.BlockSpec(memory_space=pltpu.HBM)
    arrays = (ready, lg, df, ag, smf, dpt, route)
    outs = [
        ((1, LANES), F32), (pooled_shape, BF), ((2, E, LANES), F32), ((E, FIELDS), F32), ((E, FIELDS), F32),
        ((E, E), F32), ((LANES, HID), F32), ((HID, HID), F32), ((1, HID), F32),
    ]
    return pl.pallas_call(
        finish_kernel,
        in_specs=[smem] + [hbm] * len(arrays),
        out_specs=[vmem, hbm] + [vmem] * 7,
        out_shape=[jax.ShapeDtypeStruct(s, d) for s, d in outs],
        scratch_shapes=[pltpu.VMEM(v.shape, v.dtype) for v in (lg, df, ag, smf, route)]
        + [
            pltpu.VMEM(pooled_shape, BF),
            pltpu.SemaphoreType.DMA((6 + PARTS,)),
            pltpu.SemaphoreType.DMA((PARTS,)),
        ],
        compiler_params=pltpu.CompilerParams(vmem_limit_bytes=60 * 1024 * 1024),
        name="finish",
    )(tab, *arrays)


def shards(pooled, widths, placement, route, labels, proj, senet_in, senet_out, bilinear, w_first, w_second, w_last):
    tab = lax.axis_index("tab").astype(jnp.int32).reshape(1)
    ready, lg, df, ag, smf, dpt = exchange(
        placement, widths, labels, jnp.swapaxes(proj, 1, 2), senet_in.T, senet_out, bilinear, w_first, w_second,
        w_last, pooled,
    )
    scores, dx, dproj, din, dout, dbil, dfirst, dsecond, dlast = finish(
        tab, ready, lg, df, ag, smf, dpt, route, pooled.shape
    )
    return scores, dx, jnp.swapaxes(dproj, 1, 2), din.T, dout, dbil, dfirst, dsecond, dlast[0]


def solution(mesh):
    whole = P()
    placed = (
        P("tab", "rep", None), whole, whole, P("rep", None), P("rep", None), whole, whole, whole, whole, whole,
        whole, whole,
    )
    return jax.shard_map(
        shards,
        mesh=mesh,
        in_specs=placed,
        out_specs=(
            P("rep", "tab"), P("tab", "rep", None), P("tab", None, None), whole, whole, whole, P("tab", None),
            whole, whole,
        ),
        check_vma=False,
    )
```

```python
import functools

import jax
import jax.numpy as jnp
from jax import lax
from jax.experimental import pallas as pl
from jax.experimental.pallas import tpu as pltpu
from jax.sharding import PartitionSpec as P

F32 = jnp.float32
BF = jnp.bfloat16
HI = lax.Precision.HIGHEST
NN = (((1,), (0,)), ((), ()))
NT = (((1,), (1,)), ((), ()))
TN = (((0,), (0,)), ((), ()))

FIELDS = 64
E = 32
TAB = 32
REP = 4
EARLY = 2
SIDE = 4
PARTS = 4
LANES = 128
HID = 256
BLOCK = 256
SMALL = 80
FACTOR = 0.125


def mm(a, b, dims, precision=None):
    return lax.dot_general(a, b, dims, precision=precision, preferred_element_type=F32)


def slope(u):
    s = jax.nn.sigmoid(u)
    return s * (1.0 + u * (1.0 - s))


def iota(shape, dim):
    return lax.broadcasted_iota(jnp.int32, shape, dim)


def send(src, dst, ssem, rsem, dev):
    pltpu.make_async_remote_copy(
        src_ref=src, dst_ref=dst, send_sem=ssem, recv_sem=rsem, device_id=dev,
        device_id_type=pl.DeviceIdType.MESH,
    ).start()


def got(dst, ssem, rsem, dev):
    pltpu.make_async_remote_copy(
        src_ref=dst, dst_ref=dst, send_sem=ssem, recv_sem=rsem, device_id=dev,
        device_id_type=pl.DeviceIdType.MESH,
    ).wait_recv()


def sent(src, ssem, rsem, dev):
    pltpu.make_async_remote_copy(
        src_ref=src, dst_ref=src, send_sem=ssem, recv_sem=rsem, device_id=dev,
        device_id_type=pl.DeviceIdType.MESH,
    ).wait_send()


def main_kernel(
    place_ref, width_ref, place_hbm, labels_hbm, proj_hbm, sin_hbm, sout_hbm, bil_hbm, w1_hbm, w2_hbm, wl_hbm, pooled_hbm,
    dx_hbm, lg_ref, df_ref, ag_ref, smf_ref, dpt_ref,
    rd_ref, pt_ref,
    place_vec, labels_ref, projs, sin_ref, sout_ref, bil_ref, w1, w2_ref, wl_ref, xs, e_ref, recv, emb, prod, du, sq, wts, dpw, dsq, js, jp, dpb, d2, d2p, demb, dslot, dfb, r1, r2, rz, sr, dz, d2b, rd1, rd2, rdz, inv_vec, inv_ref,
    load_sem, es, er, ds, dr, ls, lr, gs, gr, ps, pr, s1, q1, s2, q2, sz, qz, ss, sq_r, sd, qd, s1d, q1d, s2d, q2d, szd, qzd, out_sem,
):
    t = lax.axis_index("tab")
    r = lax.axis_index("rep")
    c = lax.rem(t, 2)
    n = t // 2
    x = n // SIDE
    y = lax.rem(n, SIDE)
    a = x + c * (y - x)
    b = y + c * (x - y)

    def at(a_, b_):
        return ((a_ + c * (b_ - a_)) * SIDE + (b_ + c * (a_ - b_))) * 2 + c

    def block_of(tab):
        c_ = lax.rem(tab, 2)
        n_ = tab // 2
        x_ = n_ // SIDE
        y_ = lax.rem(n_, SIDE)
        return 16 * c_ + SIDE * (x_ + c_ * (y_ - x_)) + y_ + c_ * (x_ - y_)

    mate = {"tab": t + 1 - 2 * c}
    barrier = pltpu.get_barrier_semaphore()

    def away(v):
        return min(v, SIDE - v)

    hops = sorted(
        ((dx, dy, dc) for dx in range(SIDE) for dy in range(SIDE) for dc in range(2) if dx or dy or dc),
        key=lambda h: -(away(h[0]) + away(h[1])),
    )
    others = [
        (lax.rem(x + dx, SIDE) * SIDE + lax.rem(y + dy, SIDE)) * 2 + lax.rem(c + dc, 2) for dx, dy, dc in hops
    ]

    for d in (2, 1, 3):
        pl.semaphore_signal(barrier, inc=1, device_id={"rep": lax.rem(r + d, REP)}, device_id_type=pl.DeviceIdType.MESH)
    for p in others:
        pl.semaphore_signal(barrier, inc=1, device_id={"tab": p}, device_id_type=pl.DeviceIdType.MESH)

    pairs = (
        (proj_hbm, projs), (labels_hbm, labels_ref), (bil_hbm, bil_ref), (sin_hbm, sin_ref), (sout_hbm, sout_ref),
        (w2_hbm, w2_ref), (wl_hbm, wl_ref), (w1_hbm, w1), (place_hbm, place_vec),
    )
    loads = [pltpu.make_async_copy(src, dst, load_sem.at[i]) for i, (src, dst) in enumerate(pairs)]
    part = xs.shape[1] // PARTS
    for k in range(PARTS):
        piece = pl.ds(k * part, part)
        loads.append(pltpu.make_async_copy(pooled_hbm.at[:, piece], xs.at[:, piece], load_sem.at[len(pairs) + k]))
    for k in [8, 0] + list(range(len(pairs), len(pairs) + PARTS)) + list(range(1, 8)):
        loads[k].start()

    loads[8].wait()
    line = place_vec[...].reshape(1, FIELDS)
    eye = iota((FIELDS, FIELDS), 0) == iota((FIELDS, FIELDS), 1)
    column = jnp.sum(jnp.where(eye, line, 0), axis=1, keepdims=True)
    spots = iota((FIELDS, FIELDS), 0)
    slot_of = jnp.sum(jnp.where(column == iota((FIELDS, FIELDS), 1), spots, 0), axis=0, keepdims=True)
    inv_vec[...] = jnp.minimum(slot_of, FIELDS - 1)
    invert = pltpu.make_async_copy(inv_vec, inv_ref, load_sem.at[9 + PARTS])
    invert.start()

    loads[0].wait()
    keep = []
    for i in range(2):
        field = place_ref[2 * t + i]
        keep.append(iota((E, LANES), 1) < width_ref[field])
        pt_ref[i * E : (i + 1) * E, :] = jnp.where(keep[i], projs[field].astype(F32), 0.0).astype(BF)
    for k in range(PARTS):
        loads[len(pairs) + k].wait()
        for i in range(2):
            out = mm(pt_ref[i * E : (i + 1) * E, :], xs[i, k * part : (k + 1) * part, :], NT).astype(BF)
            for d in range(part // LANES):
                e_ref[k * (part // LANES) + d, i] = out[:, d * LANES : (d + 1) * LANES]

    small_rows = (lax.rem(iota((HID, E), 0), E) == iota((HID, E), 1)).astype(BF)
    loads[1].wait()
    loads[2].wait()
    small_cols = (lax.rem(iota((E, HID), 1), E) == iota((E, HID), 0)).astype(BF)
    diag = (iota((HID, HID), 0) // E) == (iota((HID, HID), 1) // E)
    bil = bil_ref[...].astype(BF)
    tall = mm(small_rows, bil, NN).astype(BF)
    tall_t = mm(small_rows, bil, NT).astype(BF)
    kron = jnp.where(diag, mm(tall, small_cols, NN), 0.0).astype(BF)
    kron_t = jnp.where(diag, mm(tall_t, small_cols, NN), 0.0).astype(BF)
    square = iota((LANES, LANES), 0) == iota((LANES, LANES), 1)
    label_row = labels_ref[:, pl.ds(pl.multiple_of(t * LANES, LANES), LANES)].astype(F32)
    target = jnp.sum(jnp.where(square, label_row, 0.0), axis=1, keepdims=True)

    pl.semaphore_wait(barrier, TAB - 1 + REP - 1)

    def pair(p):
        return pl.ds(p * 2, 2)

    for p in others:
        send(e_ref.at[p], recv.at[pair(t)], es.at[p], er.at[t], {"tab": p})
    recv[pair(t)] = e_ref[t]

    def e_wait(i, _):
        p = lax.rem(t + i, TAB)
        got(recv.at[pair(p)], es.at[p], er.at[p], {"tab": p})
        return 0

    lax.fori_loop(1, TAB, e_wait, 0)

    def rows32(f):
        return pl.ds(pl.multiple_of(f * E, E), E)

    invert.wait()

    def by_field(f, _):
        emb[rows32(f), :] = recv[inv_ref[0, f]]
        return 0

    lax.fori_loop(0, FIELDS, by_field, 0, unroll=16)

    groups = FIELDS // 8

    def rows256(g):
        return pl.ds(pl.multiple_of(g * HID, HID), HID)

    def rows8(g):
        return pl.ds(pl.multiple_of(g * 8, 8), 8)

    def cube(v):
        return v.reshape(8, E, LANES)

    def flat(v):
        return v.reshape(HID, LANES)

    def first_pass(g, total):
        u = cube(emb[rows256(g), :].astype(F32))
        sq[rows8(g), :] = jnp.sum(u, axis=1) * (1.0 / E)
        return total + jnp.sum(u, axis=0)

    zero = jnp.zeros((E, LANES), F32)
    total = lax.fori_loop(0, groups, first_pass, zero, unroll=8)
    squeeze = sq[...]
    loads[3].wait()
    loads[4].wait()
    pre_one = mm(sin_ref[...], squeeze, NN, HI)
    act_one = pre_one * jax.nn.sigmoid(pre_one)
    weights = jax.nn.sigmoid(mm(sout_ref[...], act_one, TN, HI))
    wts[...] = weights

    def scaled_of(g):
        u = cube(emb[rows256(g), :].astype(F32))
        return u, u * wts[rows8(g), :][:, None, :]

    def second_pass(g, tot):
        return tot + jnp.sum(scaled_of(g)[1], axis=0)

    total_s = lax.fori_loop(0, groups, second_pass, zero, unroll=8)

    for k in range(5, 8):
        loads[k].wait()

    def third_pass(g, acc):
        u, sc = scaled_of(g)
        for k, (v, vb, tot) in enumerate(((u, emb[rows256(g), :], total), (sc, flat(sc).astype(BF), total_s))):
            p = mm(kron_t, vb, NN)
            prod[k, rows256(g), :] = p
            j = flat(cube(p) * (tot[None] - v) * FACTOR).astype(BF)
            chip = k * groups + g
            js[chip] = j[:LANES]
            js[16 + lax.rem(chip, SIDE) * SIDE + chip // SIDE] = j[LANES:]
            acc = acc + mm(j, w1[rows256(k * groups + g), :], TN)
        return acc

    pre_hidden = lax.fori_loop(0, groups, third_pass, jnp.zeros((LANES, HID), F32), unroll=8)
    half = pl.ds((1 - c) * 16, 16)
    send(js.at[half], jp, ps.at[0], pr.at[0], mate)

    h1 = (pre_hidden * jax.nn.sigmoid(pre_hidden)).astype(BF)
    pre_second = mm(h1, w2_ref[...], NN)
    h2 = (pre_second * jax.nn.sigmoid(pre_second)).astype(BF).astype(F32)
    wl = wl_ref[...].reshape(1, HID).astype(F32)
    logit = jnp.sum(h2 * wl, axis=1, keepdims=True)
    lg_ref[t] = jnp.sum(jnp.where(square, logit, 0.0), axis=0, keepdims=True)

    grad = jax.nn.sigmoid(logit) - target
    d_last = jnp.sum(grad * h2, axis=0, keepdims=True)
    dp2 = (grad * wl * slope(pre_second)).astype(BF)
    d_second = mm(h1, dp2, TN).astype(BF)
    for i in range(16):
        for h in range(2):
            d2[2 * i + h] = d_second[16 * i : 16 * i + 16, LANES * h : LANES * h + LANES]
    dp1 = (mm(dp2, w2_ref[...], NT) * slope(pre_hidden)).astype(BF)
    dpb[0] = dp1
    send(dpb.at[0], dpb.at[1], ps.at[1], pr.at[1], mate)
    send(d2.at[half], d2p, ps.at[2], pr.at[2], mate)

    def side(v):
        return jnp.concatenate([v[i * E : (i + 1) * E] for i in range(8)], axis=1)

    def fourth_pass(g, sums):
        u, sc = scaled_of(g)
        out = []
        bil_sum = sums[2]
        for k, (v, vb, tot) in enumerate(((u, emb[rows256(g), :], total), (sc, flat(sc).astype(BF), total_s))):
            up = cube(mm(w1[rows256(k * groups + g), :], dp1, NT)) * FACTOR
            dq = up * cube(prod[k, rows256(g), :])
            dp = flat(up * (tot[None] - v)).astype(BF)
            du[k, rows256(g), :] = mm(kron, dp, NN) - flat(dq)
            bil_sum = bil_sum + mm(side(vb), side(dp), NT)
            out.append(sums[k] + jnp.sum(dq, axis=0))
        return (*out, bil_sum)

    sums = lax.fori_loop(0, EARLY, fourth_pass, (zero, zero, jnp.zeros((E, E), F32)), unroll=2)

    def peer(me, d):
        return lax.rem(me + d, SIDE)

    got(jp, ps.at[0], pr.at[0], mate)
    got(dpb.at[1], ps.at[1], pr.at[1], mate)
    got(d2p, ps.at[2], pr.at[2], mate)
    d2b[...] = (d2[pl.ds(c * 16, 16)].astype(F32) + d2p[...].astype(F32)).astype(BF).reshape(d2b.shape)
    for d in range(1, SIDE):
        i = peer(a, d)
        send(d2b.at[i], rd1.at[a], s1d.at[d], q1d.at[a], {"tab": at(i, b)})

    both = dpb[...].reshape(2 * LANES, HID)

    def d_first_row(i):
        left = jnp.concatenate(
            [js[pl.ds(16 * c + i * SIDE, SIDE)].reshape(SIDE * LANES, LANES), jp[pl.ds(i * SIDE, SIDE)].reshape(SIDE * LANES, LANES)],
            axis=1,
        )
        out = mm(left, both, NN).astype(BF)
        for k in range(SIDE):
            for h in range(2):
                dfb[h, i, k] = out[k * LANES : (k + 1) * LANES, h * LANES : (h + 1) * LANES]

    for d in range(1, SIDE):
        i = peer(a, d)
        d_first_row(i)
        send(dfb.at[0, i], r1.at[0, a], s1.at[0, d], q1.at[0, a], {"tab": at(i, b)})
    for d in range(1, SIDE):
        i = peer(a, d)
        send(dfb.at[1, i], r1.at[1, a], s1.at[1, d], q1.at[1, a], {"tab": at(i, b)})
    d_first_row(a)

    for p in others:
        send(lg_ref.at[t], lg_ref.at[t], ls.at[p], lr.at[t], {"tab": p})
    for d in range(1, SIDE):
        i = peer(a, d)
        got(rd1.at[i], s1d.at[d], q1d.at[i], {"tab": at(i, b)})
    out = d2b[a].astype(F32)
    for d in range(1, SIDE):
        out = out + rd1[peer(a, d)].astype(F32)
    d2b[a] = out.astype(BF)
    for d in range(1, SIDE):
        k = peer(b, d)
        send(d2b.at[a, k], rd2.at[b], s2d.at[d], q2d.at[b], {"tab": at(a, k)})

    sum_q, sum_qs, d_bil = lax.fori_loop(EARLY, groups, fourth_pass, sums, unroll=6)

    for d in range(1, SIDE):
        k = peer(b, d)
        got(rd2.at[k], s2d.at[d], q2d.at[k], {"tab": at(a, k)})
    out = d2b[a, b].astype(F32)
    for d in range(1, SIDE):
        out = out + rd2[peer(b, d)].astype(F32)
    rdz[r] = out.astype(BF)
    for d in range(1, REP):
        send(rdz.at[r], rdz.at[r], szd.at[d], qzd.at[r], {"rep": peer(r, d)})

    def fifth_pass(g, _):
        u = cube(emb[rows256(g), :].astype(F32))
        w = wts[rows8(g), :]
        d_w = jnp.sum((cube(du[1, rows256(g), :]) + sum_qs[None]) * u, axis=1)
        dpw[rows8(g), :] = d_w * w * (1.0 - w)
        return 0

    lax.fori_loop(0, groups, fifth_pass, 0, unroll=8)
    d_pre_w = dpw[...]
    d_act = mm(sout_ref[...], d_pre_w, NN, HI) * slope(pre_one)
    dsq[...] = mm(sin_ref[...], d_act, TN, HI) * (1.0 / E)

    def sixth_pass(g, _):
        w = wts[rows8(g), :][:, None, :]
        out = cube(du[0, rows256(g), :]) + sum_q[None] + w * (cube(du[1, rows256(g), :]) + sum_qs[None])
        out = out + dsq[rows8(g), :][:, None, :]
        demb[rows8(g)] = out.astype(BF)
        return 0

    lax.fori_loop(0, groups, sixth_pass, 0, unroll=8)

    def by_slot(s, _):
        dslot[s] = demb[place_ref[s]]
        return 0

    lax.fori_loop(0, FIELDS, by_slot, 0, unroll=16)

    for p in others:
        send(dslot.at[pair(p)], rd_ref.at[pair(t)], ds.at[p], dr.at[t], {"tab": p})
    rd_ref[pair(t)] = dslot[pair(t)]

    d_in = mm(d_act, squeeze, NT, HI)
    d_out = mm(act_one, d_pre_w, NT, HI)
    sr[0, c, 0:E] = jnp.concatenate([d_in, d_out], axis=1).astype(BF)
    sr[0, c, E : 2 * E] = jnp.zeros((E, LANES), BF)
    sr[0, c, E : 2 * E, 0:E] = d_bil.astype(BF)
    low = iota((16, LANES), 0)
    last = jnp.where(low == 0, d_last[:, :LANES], jnp.where(low == 1, d_last[:, LANES:], 0.0))
    sr[0, c, 2 * E : SMALL] = last.astype(BF)

    def peers(phase):
        if phase == 0:
            return c, [(1 - c, mate)]
        if phase == 1:
            return r, [(lax.rem(r + d, REP), {"rep": lax.rem(r + d, REP)}) for d in range(1, REP)]
        if phase == 2:
            return a, [(lax.rem(a + d, SIDE), {"tab": at(lax.rem(a + d, SIDE), b)}) for d in range(1, SIDE)]
        return b, [(lax.rem(b + d, SIDE), {"tab": at(a, lax.rem(b + d, SIDE))}) for d in range(1, SIDE)]

    def small_start(phase):
        me, rest = peers(phase)
        for d, (_, dev) in enumerate(rest):
            send(sr.at[phase, me], sr.at[phase, me], ss.at[phase, d], sq_r.at[phase, me], dev)

    def small_end(phase):
        me, rest = peers(phase)
        for d, (who, dev) in enumerate(rest):
            got(sr.at[phase, who], ss.at[phase, d], sq_r.at[phase, who], dev)
        size = 2 if phase == 0 else 4
        out = sr[phase, 0].astype(F32)
        for k in range(1, size):
            out = out + sr[phase, k].astype(F32)
        return out

    small_start(0)
    sr[1, r] = small_end(0).astype(BF)
    small_start(1)


    def first_sum(h, k):
        out = dfb[h, a, k].astype(F32)
        for d in range(1, SIDE):
            out = out + r1[h, peer(a, d), k].astype(F32)
        dfb[h, a, k] = out.astype(BF)

    for h in range(2):
        for d in range(1, SIDE):
            i = peer(a, d)
            got(r1.at[h, i], s1.at[h, d], q1.at[h, i], {"tab": at(i, b)})
        for d in range(1, SIDE):
            k = peer(b, d)
            first_sum(h, k)
            send(dfb.at[h, a, k], r2.at[h, b], s2.at[h, d], q2.at[h, b], {"tab": at(a, k)})
        first_sum(h, b)

    sr[2, a] = small_end(1).astype(BF)
    small_start(2)

    for h in range(2):
        for d in range(1, SIDE):
            k = peer(b, d)
            got(r2.at[h, k], s2.at[h, d], q2.at[h, k], {"tab": at(a, k)})
        out = dfb[h, a, b].astype(F32)
        for d in range(1, SIDE):
            out = out + r2[h, peer(b, d)].astype(F32)
        rz[h, r] = out.astype(BF)
        for d in range(1, REP):
            send(rz.at[h, r], rz.at[h, r], sz.at[h, d], qz.at[h, r], {"rep": peer(r, d)})

    for d in range(1, REP):
        got(rdz.at[peer(r, d)], szd.at[d], qzd.at[peer(r, d)], {"rep": peer(r, d)})
    out = rdz[0].astype(F32)
    for k in range(1, REP):
        out = out + rdz[k].astype(F32)
    mine = block_of(t)
    ag_ref[mine] = out.astype(BF)

    for p in others:
        send(ag_ref.at[mine], ag_ref.at[mine], gs.at[p], gr.at[t], {"tab": p})


    def d_wait(i, _):
        p = lax.rem(t + i, TAB)
        got(rd_ref.at[pair(p)], ds.at[p], dr.at[p], {"tab": p})
        return 0

    lax.fori_loop(1, TAB, d_wait, 0)

    sr[3, b] = small_end(2).astype(BF)
    small_start(3)

    def proj_pass(j, acc):
        left = jnp.concatenate([rd_ref[pair(2 * j)].reshape(2 * E, LANES), rd_ref[pair(2 * j + 1)].reshape(2 * E, LANES)], axis=1)
        right = jnp.concatenate([xs[0, rows256(j), :], xs[1, rows256(j), :]], axis=1)
        return acc + mm(left, right, NN)

    acc = lax.fori_loop(0, TAB // 2, proj_pass, jnp.zeros((2 * E, 2 * LANES), F32), unroll=8)
    dz[r] = jnp.concatenate([acc[:E, :LANES], acc[E:, LANES:]], axis=0).astype(BF)
    for d in range(1, REP):
        o = lax.rem(r + d, REP)
        send(dz.at[r], dz.at[r], sd.at[d], qd.at[r], {"rep": o})

    pt = pt_ref[...]
    nil = jnp.zeros((E, LANES), BF)
    wide = jnp.concatenate(
        [jnp.concatenate([pt[:E], nil], axis=1), jnp.concatenate([nil, pt[E:]], axis=1)], axis=0
    )
    writes = []
    for p in range(PARTS):
        for k in range(p * (TAB // PARTS), (p + 1) * (TAB // PARTS)):
            out = mm(rd_ref[2 * k : 2 * k + 2].reshape(2 * E, LANES), wide, TN).astype(BF)
            xs[0, k * LANES : (k + 1) * LANES] = out[:, :LANES]
            xs[1, k * LANES : (k + 1) * LANES] = out[:, LANES:]
        piece = pl.ds(p * part, part)
        writes.append(pltpu.make_async_copy(xs.at[:, piece], dx_hbm.at[:, piece], out_sem.at[p]))
        writes[p].start()


    for h in range(2):
        for d in range(1, REP):
            o = peer(r, d)
            got(rz.at[h, o], sz.at[h, d], qz.at[h, o], {"rep": o})
        out = rz[h, 0].astype(F32)
        for k in range(1, REP):
            out = out + rz[h, k].astype(F32)
        df_ref[h * LANES : (h + 1) * LANES] = out

    for d in range(1, REP):
        o = lax.rem(r + d, REP)
        got(dz.at[o], sd.at[d], qd.at[o], {"rep": o})
    out = dz[0].astype(F32)
    for k in range(1, REP):
        out = out + dz[k].astype(F32)
    for i in range(2):
        dpt_ref[i] = jnp.where(keep[i], out[i * E : (i + 1) * E], 0.0)
    smf_ref[...] = small_end(3)

    def last_wait(i, _):
        p = lax.rem(t + i, TAB)
        dev = {"tab": p}
        got(lg_ref.at[p], ls.at[p], lr.at[p], dev)
        got(ag_ref.at[block_of(p)], gs.at[p], gr.at[p], dev)
        sent(e_ref.at[p], es.at[p], er.at[p], dev)
        sent(dslot.at[pair(p)], ds.at[p], dr.at[p], dev)
        sent(lg_ref.at[t], ls.at[p], lr.at[p], dev)
        sent(ag_ref.at[mine], gs.at[p], gr.at[p], dev)
        return 0

    lax.fori_loop(1, TAB, last_wait, 0)
    sent(js.at[half], ps.at[0], pr.at[0], mate)
    sent(dpb.at[0], ps.at[1], pr.at[1], mate)
    sent(d2.at[half], ps.at[2], pr.at[2], mate)
    for d in range(1, SIDE):
        i = lax.rem(a + d, SIDE)
        k = lax.rem(b + d, SIDE)
        o = lax.rem(r + d, REP)
        for h in range(2):
            sent(dfb.at[h, i], s1.at[h, d], q1.at[h, i], {"tab": at(i, b)})
            sent(dfb.at[h, a, k], s2.at[h, d], q2.at[h, k], {"tab": at(a, k)})
            sent(rz.at[h, r], sz.at[h, d], qz.at[h, r], {"rep": o})
        sent(d2b.at[i], s1d.at[d], q1d.at[i], {"tab": at(i, b)})
        sent(d2b.at[a, k], s2d.at[d], q2d.at[k], {"tab": at(a, k)})
        sent(rdz.at[r], szd.at[d], qzd.at[r], {"rep": o})
        sent(dz.at[r], sd.at[d], qd.at[r], {"rep": o})
    for copy in writes:
        copy.wait()
    for phase in range(4):
        me, rest = peers(phase)
        for d, (_, dev) in enumerate(rest):
            sent(sr.at[phase, me], ss.at[phase, d], sq_r.at[phase, me], dev)


def exchange(placement, widths, labels, proj, sin, sout, bil, w1, w2, wl, pooled):
    vmem = pl.BlockSpec(memory_space=pltpu.VMEM)
    smem = pl.BlockSpec(memory_space=pltpu.SMEM)
    hbm = pl.BlockSpec(memory_space=pltpu.HBM)
    rows = FIELDS * E
    dma = pltpu.SemaphoreType.DMA
    arrays = (placement, labels, proj, sin, sout, bil, w1, w2, wl, pooled)
    return pl.pallas_call(
        main_kernel,
        in_specs=[smem] * 2 + [hbm] * len(arrays),
        out_specs=[hbm] + [vmem] * 5,
        out_shape=[
            jax.ShapeDtypeStruct(pooled.shape, BF),
            jax.ShapeDtypeStruct((TAB, 1, LANES), F32),
            jax.ShapeDtypeStruct((BLOCK, LANES), F32),
            jax.ShapeDtypeStruct((TAB, 16, LANES), BF),
            jax.ShapeDtypeStruct((SMALL, LANES), F32),
            jax.ShapeDtypeStruct((2, E, LANES), F32),
        ],
        scratch_shapes=[pltpu.VMEM((FIELDS, E, LANES), BF), pltpu.VMEM((2 * E, LANES), BF)]
        + [pltpu.VMEM(v.shape, v.dtype) for v in arrays]
        + [
            pltpu.VMEM((TAB, 2, E, LANES), BF),
            pltpu.VMEM((FIELDS, E, LANES), BF),
            pltpu.VMEM((rows, LANES), BF),
            pltpu.VMEM((2, rows, LANES), F32),
            pltpu.VMEM((2, rows, LANES), F32),
            pltpu.VMEM((FIELDS, LANES), F32),
            pltpu.VMEM((FIELDS, LANES), F32),
            pltpu.VMEM((FIELDS, LANES), F32),
            pltpu.VMEM((FIELDS, LANES), F32),
            pltpu.VMEM((TAB, LANES, LANES), BF),
            pltpu.VMEM((16, LANES, LANES), BF),
            pltpu.VMEM((2, LANES, HID), BF),
            pltpu.VMEM((TAB, 16, LANES), BF),
            pltpu.VMEM((16, 16, LANES), BF),
            pltpu.VMEM((FIELDS, E, LANES), BF),
            pltpu.VMEM((FIELDS, E, LANES), BF),
            pltpu.VMEM((2, SIDE, SIDE, LANES, LANES), BF),
            pltpu.VMEM((2, SIDE, SIDE, LANES, LANES), BF),
            pltpu.VMEM((2, SIDE, LANES, LANES), BF),
            pltpu.VMEM((2, REP, LANES, LANES), BF),
            pltpu.VMEM((4, 4, SMALL, LANES), BF),
            pltpu.VMEM((REP, 2 * E, LANES), BF),
            pltpu.VMEM((SIDE, SIDE, 16, LANES), BF),
            pltpu.VMEM((SIDE, SIDE, 16, LANES), BF),
            pltpu.VMEM((SIDE, 16, LANES), BF),
            pltpu.VMEM((REP, 16, LANES), BF),
            pltpu.VMEM((1, FIELDS), jnp.int32),
            pltpu.SMEM((1, FIELDS), jnp.int32),
            dma((10 + PARTS,)),
        ]
        + [dma((TAB,))] * 8
        + [dma((3,))] * 2
        + [dma((2, 4))] * 6
        + [dma((4, 4))] * 2
        + [dma((4,))] * 8
        + [dma((PARTS,))],
        compiler_params=pltpu.CompilerParams(
            collective_id=0, has_side_effects=True, vmem_limit_bytes=60 * 1024 * 1024
        ),
        name="exchange",
    )(placement, widths, *arrays)


def finish_kernel(
    tab_ref, ready_hbm, lg_hbm, df_hbm, ag_hbm, smf_hbm, dpt_hbm, route_hbm,
    scores_ref, dx_hbm, dproj_ref, din_ref, dout_ref, dbil_ref, dfirst_ref, dsecond_ref, dlast_ref,
    lg_ref, df_ref, ag_ref, smf_ref, route_ref, dx, load_sem, out_sem,
):
    pairs = (
        (lg_hbm, lg_ref), (route_hbm, route_ref), (smf_hbm, smf_ref), (df_hbm, df_ref), (ag_hbm, ag_ref),
        (dpt_hbm, dproj_ref),
    )
    part = dx.shape[1] // PARTS
    pieces = [pl.ds(p * part, part) for p in range(PARTS)]
    reads = [pltpu.make_async_copy(ready_hbm.at[:, v], dx.at[:, v], load_sem.at[6 + p]) for p, v in enumerate(pieces)]
    writes = [pltpu.make_async_copy(dx.at[:, v], dx_hbm.at[:, v], out_sem.at[p]) for p, v in enumerate(pieces)]
    loads = [pltpu.make_async_copy(src, dst, load_sem.at[i]) for i, (src, dst) in enumerate(pairs)]
    reads[0].start()
    for copy in loads + reads[1:]:
        copy.start()
    for p in range(PARTS):
        reads[p].wait()
        writes[p].start()
    for copy in loads:
        copy.wait()
    idx = route_ref[:, pl.ds(pl.multiple_of(tab_ref[0] * LANES, LANES), LANES)]
    table = lg_ref[...].reshape(TAB, LANES)
    low = jnp.broadcast_to(lax.rem(idx, LANES), (TAB, LANES))
    found = jnp.take_along_axis(table, low, axis=1)
    scores_ref[...] = jnp.sum(
        jnp.where(idx // LANES == iota((TAB, LANES), 0), found, 0.0), axis=0, keepdims=True
    )
    din_ref[...] = smf_ref[0:E, 0:FIELDS]
    dout_ref[...] = smf_ref[0:E, FIELDS:]
    dbil_ref[...] = smf_ref[E : 2 * E, 0:E]
    dlast_ref[:, 0:LANES] = smf_ref[2 * E : 2 * E + 1, :]
    dlast_ref[:, LANES:] = smf_ref[2 * E + 1 : 2 * E + 2, :]
    dfirst_ref[:, 0:LANES] = df_ref[0:LANES, :]
    dfirst_ref[:, LANES:] = df_ref[LANES : 2 * LANES, :]
    for i in range(16):
        dsecond_ref[16 * i : 16 * i + 16, 0:LANES] = ag_ref[2 * i].astype(F32)
        dsecond_ref[16 * i : 16 * i + 16, LANES:] = ag_ref[2 * i + 1].astype(F32)
    for w in writes:
        w.wait()


def finish(tab, ready, lg, df, ag, smf, dpt, route, pooled_shape):
    vmem = pl.BlockSpec(memory_space=pltpu.VMEM)
    smem = pl.BlockSpec(memory_space=pltpu.SMEM)
    hbm = pl.BlockSpec(memory_space=pltpu.HBM)
    arrays = (ready, lg, df, ag, smf, dpt, route)
    outs = [
        ((1, LANES), F32), (pooled_shape, BF), ((2, E, LANES), F32), ((E, FIELDS), F32), ((E, FIELDS), F32),
        ((E, E), F32), ((LANES, HID), F32), ((HID, HID), F32), ((1, HID), F32),
    ]
    return pl.pallas_call(
        finish_kernel,
        in_specs=[smem] + [hbm] * len(arrays),
        out_specs=[vmem, hbm] + [vmem] * 7,
        out_shape=[jax.ShapeDtypeStruct(s, d) for s, d in outs],
        scratch_shapes=[pltpu.VMEM(v.shape, v.dtype) for v in (lg, df, ag, smf, route)]
        + [
            pltpu.VMEM(pooled_shape, BF),
            pltpu.SemaphoreType.DMA((6 + PARTS,)),
            pltpu.SemaphoreType.DMA((PARTS,)),
        ],
        compiler_params=pltpu.CompilerParams(vmem_limit_bytes=60 * 1024 * 1024),
        name="finish",
    )(tab, *arrays)


def shards(pooled, widths, placement, route, labels, proj, senet_in, senet_out, bilinear, w_first, w_second, w_last):
    tab = lax.axis_index("tab").astype(jnp.int32).reshape(1)
    ready, lg, df, ag, smf, dpt = exchange(
        placement, widths, labels, jnp.swapaxes(proj, 1, 2), senet_in.T, senet_out, bilinear, w_first, w_second,
        w_last, pooled,
    )
    scores, dx, dproj, din, dout, dbil, dfirst, dsecond, dlast = finish(
        tab, ready, lg, df, ag, smf, dpt, route, pooled.shape
    )
    return scores, dx, jnp.swapaxes(dproj, 1, 2), din.T, dout, dbil, dfirst, dsecond, dlast[0]


def solution(mesh):
    whole = P()
    placed = (
        P("tab", "rep", None), whole, whole, P("rep", None), P("rep", None), whole, whole, whole, whole, whole,
        whole, whole,
    )
    return jax.shard_map(
        shards,
        mesh=mesh,
        in_specs=placed,
        out_specs=(
            P("rep", "tab"), P("tab", "rep", None), P("tab", None, None), whole, whole, whole, P("tab", None),
            whole, whole,
        ),
        check_vma=False,
    )
```
